32 devices in a mesh: dp: 4 (over z), head: 8 (over y, x, core).
Axes of the slice: x: 2, y: 2, z: 4, core: 2. Of those that a mesh axis runs over, the one named last changes fastest.
Arguments:
- tokens: bfloat16 [2048, 4096], P('head', 'dp'), may hold values from -6 to 6
- lengths: int32 [32], P('dp'), may hold values from 0 to 1024, as said below
- attn_gain: bfloat16 [2048], P('head'), may hold values from 0.5 to 1.5
- w_query: bfloat16 [2048, 2048], P('head'), may hold values from -0.125 to 0.125
- w_key: bfloat16 [2048, 2048], P('head'), may hold values from -0.125 to 0.125
- w_value: bfloat16 [2048, 2048], P('head'), may hold values from -0.125 to 0.125
- w_gate: bfloat16 [2048, 2048], P('head'), may hold values from -0.125 to 0.125
- w_rate: bfloat16 [2048, 32], P(None, 'head'), may hold values from -0.0625 to 0.0625
- rate_bias: bfloat16 [32], P('head'), may hold values from -3.4 to 0.9
- inner_weight: bfloat16 [32, 64, 64], P('head'), may hold values from -0.75 to 0.75
- inner_bias: bfloat16 [32, 64], P('head'), may hold values from -3 to 3
- inner_gain: bfloat16 [32, 64], P('head'), may hold values from 0.5 to 1.5
- inner_shift: bfloat16 [32, 64], P('head'), may hold values from -2 to 2
- post_gain: bfloat16 [2048], P('head'), may hold values from 0.5 to 1.5
- post_shift: bfloat16 [2048], P('head'), may hold values from -2 to 2
- w_out: bfloat16 [2048, 2048], P('head'), may hold values from -0.1875 to 0.1875
- ffn_gain: bfloat16 [2048], P('head'), may hold values from 0.5 to 1.5
- w_hidden_gate: bfloat16 [5504, 2048], P('head'), may hold values from -0.125 to 0.125
- w_hidden_up: bfloat16 [5504, 2048], P('head'), may hold values from -0.125 to 0.125
- w_down: bfloat16 [5504, 2048], P('head'), may hold values from -0.15625 to 0.15625
- out_grad: bfloat16 [2048, 4096], P('head', 'dp'), may hold values from -6 to 6
Outputs:
- result: bfloat16 [2048, 4096], P('head', 'dp')
- grad_tokens: float32 [2048, 4096], P('head', 'dp')
- grad_attn_gain: float32 [2048], P('head')
- grad_w_query: float32 [2048, 2048], P('head')
- grad_w_key: float32 [2048, 2048], P('head')
- grad_w_value: float32 [2048, 2048], P('head')
- grad_w_gate: float32 [2048, 2048], P('head')
- grad_w_rate: float32 [2048, 32], P(None, 'head')
- grad_rate_bias: float32 [32], P('head')
- grad_inner_weight: float32 [32, 64, 64], P('head')
- grad_inner_bias: float32 [32, 64], P('head')
- grad_inner_gain: float32 [32, 64], P('head')
- grad_inner_shift: float32 [32, 64], P('head')
- grad_post_gain: float32 [2048], P('head')
- grad_post_shift: float32 [2048], P('head')
- grad_w_out: float32 [2048, 2048], P('head')
- grad_ffn_gain: float32 [2048], P('head')
- grad_w_hidden_gate: float32 [5504, 2048], P('head')
- grad_w_hidden_up: float32 [5504, 2048], P('head')
- grad_w_down: float32 [5504, 2048], P('head')
- mean_rate: float32 [], replicated
- max_rate: float32 [], replicated
The draws below stay inside these ranges and needn't reach their ends.
Inputs may be any that keep to these rules, and one draw needn't show every extreme that they name: For each index of dp, its 8 lengths rounded up to multiples of 16 sum to at most 1024; in every draw some index of dp holds one sequence of exactly 1024 tokens and zeros.
All inputs are finite; a program needn't handle non-finite values.
Results may differ from the reference program's by a relative error of at most 0.018.
Values may be sent and summed in bfloat16 or wider, within the bound.
No kernel may reach another device: no remote copies, remote signals or barrier semaphores. Data moves between devices by JAX's collectives and lax.ppermute only.
A program may use at most 192 MiB of HBM per device.

```python
import jax
import jax.numpy as jnp
from jax import lax

D = 2048
HEADS = 32
HD = 64
FF = 5504
MB = 16
TOK_DEV = 1024
SEQS_DEV = 8
TOKENS = 4096
SEQ_ALL = 32


def draw_lengths(key, part):
    segments = SEQ_ALL // SEQS_DEV
    blocks = TOK_DEV // MB
    key_full = jax.random.fold_in(key, 11)
    key_fill = jax.random.fold_in(key, 12)
    key_expo = jax.random.fold_in(key, 13)
    key_mult = jax.random.fold_in(key, 14)
    key_trim = jax.random.fold_in(key, 15)
    full_index = jax.random.randint(key_full, (), 0, segments)
    fill = jax.random.randint(key_fill, (segments,), blocks * 2 // 5, blocks + 1)
    expo = jax.random.randint(key_expo, (segments, SEQS_DEV), 0, 6)
    weights = jnp.left_shift(jnp.ones_like(expo), expo) * jax.random.randint(key_mult, (segments, SEQS_DEV), 1, 4)
    counts = fill[:, None] * weights // jnp.sum(weights, axis=1, keepdims=True)
    trim = jax.random.randint(key_trim, (segments, SEQS_DEV), 0, MB)
    seq_lens = jnp.where(counts > 0, counts * MB - trim, 0)
    single = jnp.zeros((SEQS_DEV,), jnp.int32).at[0].set(TOK_DEV)
    chosen = jnp.arange(segments, dtype=jnp.int32)[:, None] == full_index
    seq_lens = jnp.where(chosen, single[None, :], seq_lens)
    return seq_lens.reshape(-1).astype(jnp.int32)


def draw_rate_bias(key, part):
    order = jax.random.permutation(jax.random.fold_in(key, 23), HEADS).astype(jnp.float32)
    base = -3.0 + 3.5 * order / (HEADS - 1)
    noise = 0.1 * jnp.clip(jax.random.normal(jax.random.fold_in(key, 22), (HEADS,), jnp.float32), -3.0, 3.0)
    return (base + noise).astype(jnp.bfloat16)


def block_levels(key, dims, cuts, least, high):
    level, own = 1.0, jax.random.fold_in(key, 6)
    for dim, blocks in cuts:
        heights = jnp.exp(jax.random.uniform(jax.random.fold_in(own, dim), (blocks,), jnp.float32, least / len(cuts), high / len(cuts)))
        level = level * jnp.repeat(heights, dims[dim] // blocks).reshape([-1 if axis == dim else 1 for axis in range(len(dims))])
    return level


def bell_draw(rng, dims, deviation, most, cuts=(), held_as=jnp.bfloat16):
    loudness = block_levels(rng, dims, cuts, -0.22, 0.18) if cuts else 1.0
    entries = jax.random.normal(rng, dims, jnp.float32) * deviation * loudness
    return jnp.minimum(jnp.maximum(entries, -most), most).astype(held_as)


def setup_inputs(seed: int = 0) -> dict:
    key_of = jax.random.split(jax.random.key(seed), 22)
    return {
        "tokens": bell_draw(key_of[0], (D, TOKENS), 1.0, 6.0, ((0, 8), (1, 4))),
        "lengths": draw_lengths(jax.random.fold_in(key_of[21], 71), 0),
        "attn_gain": jnp.clip(1.0 + 0.1 * jax.random.normal(key_of[2], (D,), jnp.float32), 0.5, 1.5).astype(jnp.bfloat16),
        "w_query": bell_draw(key_of[3], (D, D), D ** -0.5, 0.125, ((0, 8),)),
        "w_key": bell_draw(key_of[4], (D, D), D ** -0.5, 0.125, ((0, 8),)),
        "w_value": bell_draw(key_of[5], (D, D), D ** -0.5, 0.125, ((0, 8),)),
        "w_gate": bell_draw(key_of[6], (D, D), D ** -0.5, 0.125, ((0, 8),)),
        "w_rate": bell_draw(key_of[7], (D, HEADS), (4 * D) ** -0.5, 0.0625, ((1, 8),)),
        "rate_bias": draw_rate_bias(jax.random.fold_in(key_of[21], 71), 0),
        "inner_weight": bell_draw(key_of[9], (HEADS, HD, HD), HD ** -0.5, 0.75, ((0, 8),)),
        "inner_bias": bell_draw(key_of[10], (HEADS, HD), 0.5, 3.0, ((0, 8),)),
        "inner_gain": jnp.clip(1.0 + 0.1 * jax.random.normal(key_of[11], (HEADS, HD), jnp.float32), 0.5, 1.5).astype(jnp.bfloat16),
        "inner_shift": bell_draw(key_of[12], (HEADS, HD), 0.3, 2.0, ((0, 8),)),
        "post_gain": jnp.clip(1.0 + 0.1 * jax.random.normal(key_of[13], (D,), jnp.float32), 0.5, 1.5).astype(jnp.bfloat16),
        "post_shift": bell_draw(key_of[14], (D,), 0.3, 2.0, ((0, 8),)),
        "w_out": bell_draw(key_of[15], (D, D), (D // 2) ** -0.5, 0.1875, ((0, 8),)),
        "ffn_gain": jnp.clip(1.0 + 0.1 * jax.random.normal(key_of[16], (D,), jnp.float32), 0.5, 1.5).astype(jnp.bfloat16),
        "w_hidden_gate": bell_draw(key_of[17], (FF, D), D ** -0.5, 0.125, ((0, 8),)),
        "w_hidden_up": bell_draw(key_of[18], (FF, D), D ** -0.5, 0.125, ((0, 8),)),
        "w_down": bell_draw(key_of[19], (FF, D), (FF // 4) ** -0.5, 0.15625, ((0, 8),)),
        "out_grad": bell_draw(key_of[20], (D, TOKENS), 1.0, 6.0, ((0, 8), (1, 4))),
    }


EPS = 1e-06
BASE_RATE = 1.0

@jax.custom_vjp
def low(v):
    return lax.optimization_barrier(v.astype(jnp.bfloat16)).astype(jnp.float32)

@jax.custom_vjp
def low_back(v):
    return v

def low_keep(v):
    return (low(v), None)

def low_pass(kept, grad):
    return (grad,)

def back_keep(v):
    return (v, None)

def back_low(kept, grad):
    return (low(grad),)
low.defvjp(low_keep, low_pass)
low_back.defvjp(back_keep, back_low)

def rms_scale(values):
    return lax.rsqrt(lax.optimization_barrier(jnp.mean(values * values, -1, keepdims=True)) + EPS)

def layer_norm(values, norm_gain, norm_shift):
    center = values - lax.optimization_barrier(jnp.mean(values, -1, keepdims=True))
    return center * lax.rsqrt(lax.optimization_barrier(jnp.mean(center * center, -1, keepdims=True)) + EPS) * norm_gain + norm_shift

def inner_grad(values, target, norm_gain, norm_shift):
    center = values - lax.optimization_barrier(jnp.mean(values, -1, keepdims=True))
    inv_std = lax.rsqrt(lax.optimization_barrier(jnp.mean(center * center, -1, keepdims=True)) + EPS)
    normed = center * inv_std
    upward = (normed * norm_gain + norm_shift - target) * norm_gain
    return inv_std * (upward - lax.optimization_barrier(jnp.mean(upward, -1, keepdims=True)) - normed * lax.optimization_barrier(jnp.mean(upward * normed, -1, keepdims=True)))

def post_mix(mixer_out, gate_in, norm_gain, norm_shift):
    return layer_norm(mixer_out, norm_gain, norm_shift) * jax.nn.gelu(gate_in, approximate=True)

def head_block(weight, offset_vec, query_rows, key_rows, value_rows, step_rates, valid_rows, norm_gain, norm_shift):
    highest = lax.Precision.HIGHEST
    positions = 1.0 / (jnp.arange(MB).astype(jnp.float32) + 1.0)
    lower = jnp.tril(jnp.ones((MB, MB), jnp.float32))
    weights = lower * positions[:, None] * step_rates[None, :]
    grad_z = inner_grad(jnp.dot(key_rows, weight, precision=highest) + offset_vec, value_rows - key_rows, norm_gain, norm_shift)
    scores = jnp.dot(query_rows, key_rows.T, precision=highest)
    zbar = jnp.dot(query_rows, weight, precision=highest) - jnp.dot(weights * scores, grad_z, precision=highest) + offset_vec - jnp.dot(weights, grad_z, precision=highest)
    output = (query_rows + layer_norm(zbar, norm_gain, norm_shift)) * valid_rows[:, None]
    last_rates = step_rates / MB
    new_weight = weight - jnp.dot((last_rates[:, None] * key_rows).T, grad_z, precision=highest)
    new_offset = offset_vec - jnp.dot(last_rates, grad_z, precision=highest)
    return (new_weight, new_offset, output)

def ttt_scan(queries, key_rows, value_rows, logits, valid_rows, reset_rows, init_weight, init_bias, norm_gain, norm_shift):
    row_count, head_count = logits.shape
    block_count = row_count // MB

    def blocks(array):
        return array.reshape(block_count, MB, head_count, HD).transpose(0, 2, 1, 3)
    step_rates = BASE_RATE / HD * jax.nn.sigmoid(logits) * valid_rows[:, None]
    rate_blocks = step_rates.reshape(block_count, MB, head_count).transpose(0, 2, 1)
    valid_blocks = valid_rows.reshape(block_count, MB)

    def advance(carry, pieces):
        weight, offset_vec = carry
        query_blk, key_blk, value_blk, rate_blk, valid_blk, reset_now = pieces
        weight = reset_now * init_weight + (1.0 - reset_now) * weight
        offset_vec = reset_now * init_bias + (1.0 - reset_now) * offset_vec
        new_weight, new_offset, output = jax.vmap(head_block, in_axes=(0, 0, 0, 0, 0, 0, None, 0, 0))(weight, offset_vec, query_blk, key_blk, value_blk, rate_blk, valid_blk, norm_gain, norm_shift)
        return ((new_weight, new_offset), output)
    carry_out, outputs = lax.scan(jax.checkpoint(advance), (init_weight, init_bias), (blocks(queries), blocks(key_rows), blocks(value_rows), rate_blocks, valid_blocks, reset_rows))
    return outputs.transpose(0, 2, 1, 3).reshape(row_count, head_count * HD)

def layout(seq_lens, row_count):
    padded = (seq_lens + MB - 1) // MB * MB
    starts = jnp.cumsum(padded, axis=1) - padded
    positions = jnp.arange(row_count, dtype=jnp.int32)
    inside = (positions[None, None, :] >= starts[:, :, None]) & (positions[None, None, :] < (starts + seq_lens)[:, :, None])
    valid_rows = jnp.any(inside, axis=1).astype(jnp.float32)
    block_first = jnp.arange(row_count // MB, dtype=jnp.int32) * MB
    begins = jnp.any((starts[:, :, None] == block_first[None, None, :]) & (seq_lens[:, :, None] > 0), axis=1)
    begins = begins | (block_first[None, :] == 0)
    return (valid_rows, begins.astype(jnp.float32))

def reference(tokens, lengths, attn_gain, w_query, w_key, w_value, w_gate, w_rate, rate_bias, inner_weight, inner_bias, inner_gain, inner_shift, post_gain, post_shift, w_out, ffn_gain, w_hidden_gate, w_hidden_up, w_down, out_grad):
    segments = SEQ_ALL // SEQS_DEV
    seq_lens = lengths.reshape(segments, SEQS_DEV)
    valid_seg, reset_seg = layout(seq_lens, TOK_DEV)
    valid_rows = valid_seg.reshape(-1)

    def product(left, right):
        return jnp.dot(left, right, precision=lax.Precision.HIGHEST)

    def split(array):
        return array.reshape(segments, TOK_DEV, array.shape[-1])
    segment_scan = jax.vmap(ttt_scan, in_axes=(0, 0, 0, 0, 0, 0, None, None, None, None))

    def forward(inputs, a_gain, query_w, key_w, value_w, gate_w, rate_w, bias_r, w_init, b_init, n_gain, n_shift, p_gain, p_shift, out_w, f_gain, hgate_w, hup_w, down_w):
        normed_in = low(inputs * rms_scale(inputs) * a_gain)
        queries = low_back(product(normed_in, query_w))
        key_rows = low_back(product(normed_in, key_w))
        value_rows = low_back(product(normed_in, value_w))
        gate_pre = low(low_back(product(normed_in, gate_w)))
        logits = low_back(product(normed_in, rate_w)) + bias_r
        mixer_out = segment_scan(split(queries), split(key_rows), split(value_rows), split(logits), valid_seg, reset_seg, w_init, b_init, n_gain, n_shift).reshape(TOKENS, HEADS * HD)
        mixed_gate = low(post_mix(low(mixer_out), gate_pre, p_gain, p_shift))
        hidden = inputs + low_back(product(mixed_gate, out_w))
        hidden_low = low(hidden)
        normed_mid = low(hidden_low * rms_scale(hidden_low) * f_gain)
        gate_val = low_back(product(normed_mid, hgate_w))
        up_val = low_back(product(normed_mid, hup_w))
        inner_act = low(jax.nn.silu(gate_val) * up_val)
        return (hidden + low_back(product(inner_act, down_w)), jax.nn.sigmoid(logits))
    flipped = (0, 2, 3, 4, 5, 14, 16, 17)
    stored = tuple((array.astype(jnp.float32) for array in (tokens, attn_gain, w_query, w_key, w_value, w_gate, w_rate, rate_bias, inner_weight, inner_bias, inner_gain, inner_shift, post_gain, post_shift, w_out, ffn_gain, w_hidden_gate, w_hidden_up, w_down)))
    floats = tuple((stored[index].T if index in flipped else stored[index] for index in range(len(stored))))
    result, pull_back, rates = jax.vjp(forward, *floats, has_aux=True)
    raw = pull_back(out_grad.astype(jnp.float32).T)
    grads = tuple((raw[index].T if index in flipped else raw[index] for index in range(len(raw))))
    masked = rates * valid_rows[:, None]
    mean_rate = jnp.sum(masked) / (TOKENS * HEADS)
    max_rate = jnp.max(masked)
    return (result.T.astype(jnp.bfloat16), grads[0], grads[1], grads[2], grads[3], grads[4], grads[5], grads[6], grads[7], grads[8], grads[9], grads[10], grads[11], grads[12], grads[13], grads[14], grads[15], grads[16], grads[17], grads[18], mean_rate, max_rate)
```

```python
import jax, jax.numpy as jnp
from jax import lax
from jax.experimental import pallas as pl
from jax.experimental.pallas import tpu as pltpu
import functools
HD=64; MB=16; EPS=1e-6
F32=jnp.float32; BF=jnp.bfloat16

def nn(a,b): return lax.dot_general(a,b,(((1,),(0,)),((),())),preferred_element_type=F32)
def nt(a,b): return lax.dot_general(a,b,(((1,),(1,)),((),())),preferred_element_type=F32)
def tn(a,b): return lax.dot_general(a,b,(((0,),(0,)),((),())),preferred_element_type=F32)

def avg(x): return jnp.sum(x,0,keepdims=True)*(1.0/HD)

def lane_heads(heads, rows):
    return lax.broadcasted_iota(jnp.int32,(rows,heads*MB),1)//MB

def spread(x, heads):
    ids=lane_heads(heads,HD)
    return jnp.concatenate([jnp.where(ids==h,x,jnp.zeros_like(x)) for h in range(heads)],0)

def gather_blocks(x, heads):
    ids=lane_heads(heads,HD)
    out=jnp.zeros((HD,heads*MB),F32)
    for h in range(heads):
        out=out+jnp.where(ids==h,x[h*HD:(h+1)*HD],0.0)
    return out

def split_heads(ref, group, heads):
    cols=[ref[h*HD:(h+1)*HD, pl.ds(pl.multiple_of(group*128,128),128)] for h in range(heads)]
    return [jnp.concatenate([c[:,p*MB:(p+1)*MB] for c in cols],1) for p in range(8)]

def merge_heads(ref, group, parts, heads):
    for h in range(heads):
        blk=jnp.concatenate([p[:,h*MB:(h+1)*MB] for p in parts],1)
        ref[h*HD:(h+1)*HD, pl.ds(pl.multiple_of(group*128,128),128)]=blk.astype(ref.dtype)

def padded(x):
    rows=lax.broadcasted_iota(jnp.int32,(MB,x.shape[1]),0)
    return jnp.concatenate([x,jnp.where(rows==0,1.0,0.0).astype(F32)],0)

def same_head(heads):
    L=heads*MB
    r=lax.broadcasted_iota(jnp.int32,(L,L),0); c=lax.broadcasted_iota(jnp.int32,(L,L),1)
    return r//MB==c//MB, r%MB, c%MB

def step_grad(zt, td, g, s):
    mu=avg(zt); cen=zt-mu
    r=lax.rsqrt(avg(cen*cen)+EPS)
    n=cen*r
    v=n*g+s-td
    u=v*g
    m1=avg(u); m2=avg(u*n)
    return r,n,v,u,m2,r*(u-m1-n*m2)

def fwd_kernel(heads, nb, reset, qT, kT, vT, er, vr, w0, c0, g_ref, s_ref, wi, ci,
               outT, zt_o, zb_o, td_o, qa_o, ka_o, wt_o, wo, co, mp, q32):
    L=heads*MB
    same,ri,ci_=same_head(heads)
    tri=jnp.where(same&(ri<=ci_), 16.0/(ci_.astype(F32)+1.0), 0.0)
    diag=jnp.where(same,1.0,0.0)
    def pre(gr,_):
        qs=split_heads(qT,gr,heads); ks=split_heads(kT,gr,heads); vs=split_heads(vT,gr,heads)
        for p in range(8):
            b=gr*8+p
            td_o[b]=vs[p]-ks[p]
            q32[b]=qs[p]
            qa_o[b]=padded(qs[p]).astype(BF)
            ka_o[b]=padded(ks[p]).astype(BF)
        return 0
    lax.fori_loop(0,nb//8,pre,0)
    def pre2(b,_):
        nxt=jnp.minimum(b+1,nb-1)
        ke=(ka_o[b].astype(F32)*(er[b]*(1.0/MB))).astype(BF)
        keep=jnp.where(reset[nxt]>0,0.0,1.0)
        m=tn(ke,ka_o[nxt])*(diag*keep)
        pt=tn(ke,qa_o[b])*tri
        mp[b]=jnp.concatenate([m,pt],1).astype(BF)
        return 0
    lax.fori_loop(0,nb,pre2,0,unroll=4)
    g=g_ref[...]; s=s_ref[...]
    ids=lane_heads(heads,L)
    rows=lax.broadcasted_iota(jnp.int32,(L,L),0)//MB
    def body(b,carry):
        zt,wt,ct=carry
        nxt=jnp.minimum(b+1,nb-1)
        rs=reset[nxt]>0
        wt_b=wt.astype(BF)
        wt_o[b]=wt_b; zt_o[b]=zt
        r,n,v,u,m2,gt=step_grad(zt,td_o[b],g,s)
        gb=gt.astype(BF)
        kn=spread(ka_o[nxt][:HD],heads)
        wsel=jnp.where(rs,w0[...],wt).astype(BF)
        csel=jnp.where(rs,c0[...],ct)
        yk=nn(wsel,kn)+csel
        yq=nn(wt_b,spread(qa_o[b][:HD],heads))+ct
        rr=nn(gb,mp[b])
        e16=er[b]*(1.0/MB)
        ke=(ka_o[b][:HD].astype(F32)*e16).astype(BF)
        rw=nt(gb,spread(ke,heads))
        ec=jnp.where(same,jnp.broadcast_to(e16,(L,L)),0.0).astype(BF)
        rc=nt(gb,ec)
        zb_o[b]=yq-rr[:,L:]
        z2=yk-rr[:,:L]
        wn=jnp.where(rs,w0[...],wt-rw)
        cn=jnp.where(rs,c0[...],ct-rc)
        @pl.when(b==nb-1)
        def _():
            wo[...]=wt-rw; co[...]=ct-rc
        return z2,wn,cn
    rs0=reset[0]>0
    wt=jnp.where(rs0,w0[...],wi[...]); ct=jnp.where(rs0,c0[...],ci[...])
    zt=nn(wt.astype(BF),spread(ka_o[0][:HD],heads))+ct
    lax.fori_loop(0,nb,body,(zt,wt,ct))
    def post(gr,_):
        outs=[]
        for p in range(8):
            b=gr*8+p
            zb=zb_o[b]; cen=zb-avg(zb)
            n=cen*lax.rsqrt(avg(cen*cen)+EPS)
            outs.append((q32[b]+n*g+s)*vr[b])
        merge_heads(outT,gr,outs,heads)
        return 0
    lax.fori_loop(0,nb//8,post,0)

VM=pl.BlockSpec(memory_space=pltpu.VMEM)
SM=pl.BlockSpec(memory_space=pltpu.SMEM)

def ttt_fwd(reset, qT,kT,vT, er, vr, w0,c0,g,s, wi,ci):
    T=qT.shape[1]; heads=qT.shape[0]//HD; nb=T//MB; L=heads*MB; S=jax.ShapeDtypeStruct
    outs=[S((heads*HD,T),BF),S((nb,HD,L),F32),S((nb,HD,L),F32),S((nb,HD,L),F32),S((nb,HD+MB,L),BF),S((nb,HD+MB,L),BF),
          S((nb,HD,heads*HD),BF),S((HD,heads*HD),F32),S((HD,L),F32)]
    return pl.pallas_call(functools.partial(fwd_kernel,heads,nb),out_shape=outs,
        in_specs=[SM]+[VM]*11,out_specs=[VM]*len(outs),
        scratch_shapes=[pltpu.VMEM((nb,L,2*L),BF),pltpu.VMEM((nb,HD,L),F32)],
        compiler_params=pltpu.CompilerParams(vmem_limit_bytes=56<<20), name="mix_forward")(reset,qT,kT,vT,er,vr,w0,c0,g,s,wi,ci)

def bwd_kernel(heads, nb, reset, dOT, zt_i, zb_i, td_i, qa_i, ka_i, wt_i, er, vr, g_ref, s_ref, li, lci,
               dqT, dkT, dvT, de_o, dg_o, ds_o, dw0_o, dc0_o, lo, lco,
               n_s, v_s, r_s, m2_s, gb_s, gh_s, nm_s, u_s, uc_s, dq_s, dk_s, du_s, dz_s, h_s, la_s):
    L=heads*MB
    g=g_ref[...]; s=s_ref[...]
    same,ri,cj=same_head(heads)
    tri=jnp.where(same&(cj<=ri),1.0/(ri.astype(F32)+1.0),0.0)
    diag=jnp.where(same,1.0,0.0)
    diag_b=diag.astype(BF)
    dg_o[...]=jnp.zeros((HD,L),F32); ds_o[...]=jnp.zeros((HD,L),F32)
    dw0_o[...]=jnp.zeros_like(dw0_o); dc0_o[...]=jnp.zeros_like(dc0_o)
    def pre(gr,_):
        dos=split_heads(dOT,gr,heads)
        dga=jnp.zeros((HD,L),F32); dsa=jnp.zeros((HD,L),F32)
        for p in range(8):
            b=gr*8+p
            dO=dos[p].astype(F32)*vr[b]
            zb=zb_i[b]; cen=zb-avg(zb); rb=lax.rsqrt(avg(cen*cen)+EPS); nbar=cen*rb
            dga=dga+dO*nbar; dsa=dsa+dO
            dn=dO*g
            dzb=rb*(dn-avg(dn)-nbar*avg(dn*nbar))
            dzb_b=dzb.astype(BF)
            r,n,v,u,m2,gt=step_grad(zt_i[b],td_i[b],g,s)
            gb=gt.astype(BF)
            n_s[b]=n; v_s[b]=v; r_s[b]=r; m2_s[b]=m2; gb_s[b]=gt
            e=er[b]
            ka=ka_i[b]; qa=qa_i[b]
            st=tn(qa,ka)*tri
            gh_s[b]=-nn(dzb_b,(st*e).astype(BF))
            dp=-tn(dzb_b,gb)
            de_o[b]=jnp.sum(dp*st,0,keepdims=True)
            dS=(dp*tri*e).astype(BF)
            dq_s[b]=dO+gather_blocks(tn(wt_i[b],dzb_b),heads)+nt(ka[:HD],dS)
            dk_s[b]=nn(qa[:HD],dS)
            prev=jnp.maximum(b-1,0)
            keep=jnp.where(reset[b]>0,0.0,1.0)
            nm_s[b]=(tn(ka,ka_i[prev])*(diag*keep)).astype(BF)
            u_s[b]=nt(dzb_b,spread(qa[:HD],heads))
            uc_s[b]=nn(dzb_b,diag_b)
        dg_o[...]+=dga; ds_o[...]+=dsa
        return 0
    lax.fori_loop(0,nb//8,pre,0)
    def body(k,carry):
        ht,la,lc=carry
        b=nb-1-k
        prev=jnp.maximum(b-1,0)
        rs=reset[b]>0
        n=n_s[b]; v=v_s[b]; r=r_s[b]; m2=m2_s[b]; gt=gb_s[b]
        h_s[b]=ht
        la_s[b]=la.astype(BF)
        dG=gh_s[b]-(er[b]*(1.0/MB))*ht
        da=r*dG
        m3=avg(da); m4=avg(da*n); m6a=avg(dG*gt)
        du=da-m3-n*m4
        dn=(du*g-v*m4)*g-da*m2
        m5=avg(dn); m6=m6a+avg(dn*n)
        dz=(r*(dn-m5-n*m6)).astype(BF)
        du_s[b]=du
        dz_s[b]=dz
        la2=la+u_s[b]; lc2=lc+uc_s[b]
        y=nn(la2.astype(BF),spread(ka_i[prev][:HD],heads))+lc2
        h2=jnp.where(rs,0.0,y)+nn(dz,nm_s[b])
        la3=la2+nt(dz,spread(ka_i[b][:HD],heads)); lc3=lc2+nn(dz,diag_b)
        @pl.when(rs)
        def _():
            dw0_o[...]+=la3; dc0_o[...]+=lc3
        return h2,jnp.where(rs,0.0,la3),jnp.where(rs,0.0,lc3)
    la=li[...]; lc=lci[...]
    ht=nn(la.astype(BF),spread(ka_i[nb-1][:HD],heads))+lc
    ht,la,lc=lax.fori_loop(0,nb,body,(ht,la,lc))
    lo[...]=la; lco[...]=lc
    def post(gr,_):
        dqs=[];dks=[];dvs=[]
        dga=jnp.zeros((HD,L),F32); dsa=jnp.zeros((HD,L),F32)
        for p in range(8):
            b=gr*8+p
            du=du_s[b]; dug=du*g; gt=gb_s[b]
            dga=dga+du*v_s[b]+dug*n_s[b]; dsa=dsa+dug
            dvs.append(-dug)
            dqs.append(dq_s[b])
            de_o[b]=de_o[b]-avg(gt*h_s[b])*(HD/MB)
            dks.append(dug+dk_s[b]-(er[b]*(1.0/MB))*gather_blocks(tn(la_s[b],gt.astype(BF)),heads)
                       +gather_blocks(tn(wt_i[b],dz_s[b]),heads))
        merge_heads(dqT,gr,dqs,heads); merge_heads(dkT,gr,dks,heads); merge_heads(dvT,gr,dvs,heads)
        dg_o[...]+=dga; ds_o[...]+=dsa
        return 0
    lax.fori_loop(0,nb//8,post,0)

def ttt_bwd(reset, dOT, zt,zb,td,qa,ka,wt,er,vr,g,s,li,lci):
    T=dOT.shape[1]; heads=dOT.shape[0]//HD; nb=T//MB; L=heads*MB; S=jax.ShapeDtypeStruct
    W=heads*HD
    outs=[S((W,T),BF)]*3+[S((nb,1,L),F32)]+[S((HD,L),F32)]*2+[S((HD,W),F32),S((HD,L),F32)]*2
    V=pltpu.VMEM
    scr=[V((nb,HD,L),F32),V((nb,HD,L),F32),V((nb,1,L),F32),V((nb,1,L),F32),V((nb,HD,L),F32),V((nb,HD,L),F32),
         V((nb,L,L),BF),V((nb,HD,W),F32),V((nb,HD,L),F32),V((nb,HD,L),F32),V((nb,HD,L),F32),V((nb,HD,L),F32),
         V((nb,HD,L),BF),V((nb,HD,L),F32),V((nb,HD,W),BF)]
    return pl.pallas_call(functools.partial(bwd_kernel,heads,nb),out_shape=outs,
        in_specs=[SM]+[VM]*13,out_specs=[VM]*len(outs),scratch_shapes=scr,
        compiler_params=pltpu.CompilerParams(vmem_limit_bytes=60<<20), name="mix_backward")(reset,dOT,zt,zb,td,qa,ka,wt,er,vr,g,s,li,lci)

def lane_rows(x, heads):
    T=x.shape[1]
    return x.reshape(heads,T//MB,MB).transpose(1,0,2).reshape(T//MB,1,heads*MB)
def lane_cols(x):
    return jnp.repeat(x.T,MB,axis=1)


from jax.sharding import PartitionSpec as P


def col_sum(x):
    return jnp.sum(x, 0, keepdims=True)


def gelu_tanh(values):
    return jax.nn.gelu(values, approximate=True)


def layout(seq_lens, row_count):
    padded = (seq_lens + MB - 1) // MB * MB
    starts = jnp.cumsum(padded) - padded
    positions = jnp.arange(row_count, dtype=jnp.int32)
    inside = (positions[None, :] >= starts[:, None]) & (positions[None, :] < (starts + seq_lens)[:, None])
    valid_rows = jnp.any(inside, axis=0).astype(F32)
    block_first = jnp.arange(row_count // MB, dtype=jnp.int32) * MB
    begins = jnp.any((starts[:, None] == block_first[None, :]) & (seq_lens[:, None] > 0), axis=0)
    return valid_rows, (begins | (block_first == 0)).astype(jnp.int32)


def on_device(
    tokens, lengths, attn_gain, w_query, w_key, w_value, w_gate, w_rate, rate_bias,
    inner_weight, inner_bias, inner_gain, inner_shift, post_gain, post_shift, w_out,
    ffn_gain, w_hidden_gate, w_hidden_up, w_down, out_grad,
):
    tok = tokens.shape[1]
    own = tokens.shape[0]
    heads = inner_weight.shape[0]
    devs = lax.axis_size("head")
    width = own * devs
    first = lax.axis_index("head") * own

    def gather(x):
        return lax.all_gather(x, "head", axis=0, tiled=True)

    def mine(x):
        return lax.dynamic_slice_in_dim(x, first, own, 0)

    valid, reset = layout(lengths, tok)
    vrow = valid[None, :]
    gains = lax.all_gather(jnp.stack([attn_gain, post_gain, post_shift, ffn_gain]), "head", axis=1, tiled=True)
    gains = gains.astype(F32)[:, :, None]
    x = gather(tokens).astype(F32)
    q1 = lax.rsqrt(col_sum(x * x) / width + EPS)
    nin = (x * q1 * gains[0]).astype(BF)
    q_t = nn(w_query, nin)
    k_t = nn(w_key, nin)
    v_t = nn(w_value, nin)
    gate = nn(w_gate, nin).astype(BF)
    logits = tn(w_rate, nin) + rate_bias.astype(F32)[:, None]
    sig = jax.nn.sigmoid(logits)
    masked = sig * vrow
    er = lane_rows(masked * (1.0 / HD), heads)
    vr = lane_rows(jnp.broadcast_to(vrow, (heads, tok)), heads)
    w0 = inner_weight.astype(F32).transpose(2, 0, 1).reshape(HD, own)
    c0 = lane_cols(inner_bias.astype(F32))
    ig = lane_cols(inner_gain.astype(F32))
    ish = lane_cols(inner_shift.astype(F32))
    zw = jnp.zeros_like(w0)
    zc = jnp.zeros_like(c0)
    mixer_own, zt, zb, td, qa, ka, wt, _, _ = ttt_fwd(reset, q_t, k_t, v_t, er, vr, w0, c0, ig, ish, zw, zc)
    rate_part = jnp.sum(masked)
    max_rate = lax.pmax(jnp.max(masked), ("dp", "head"))

    mix = gather(mixer_own).astype(F32)
    gates = gather(gate).astype(F32)
    cen = mix - col_sum(mix) / width
    r3 = lax.rsqrt(col_sum(cen * cen) / width + EPS)
    mixed = ((cen * r3 * gains[1] + gains[2]) * gelu_tanh(gates)).astype(BF)
    hidden = tokens.astype(F32) + nn(w_out, mixed)
    hid = gather(hidden.astype(BF)).astype(F32)
    q2 = lax.rsqrt(col_sum(hid * hid) / width + EPS)
    nmid = (hid * q2 * gains[3]).astype(BF)
    gate_val = nn(w_hidden_gate, nmid)
    up_val = nn(w_hidden_up, nmid)
    sg = jax.nn.sigmoid(gate_val)
    act = (gate_val * sg * up_val).astype(BF)
    ffn = lax.psum_scatter(tn(w_down, act).astype(BF), "head", scatter_dimension=0, tiled=True)
    result = (hidden + ffn.astype(F32)).astype(BF)

    g_full = gather(out_grad)
    g_down = nt(act, g_full)
    g_act = nn(w_down, g_full)
    g_up = (g_act * gate_val * sg).astype(BF)
    g_gate = (g_act * up_val * sg * (1.0 + gate_val * (1.0 - sg))).astype(BF)
    g_hgate = nt(g_gate, nmid)
    g_hup = nt(g_up, nmid)
    gn = lax.psum_scatter(
        tn(w_hidden_gate, g_gate) + tn(w_hidden_up, g_up), "head", scatter_dimension=0, tiled=True
    )
    hid_own = mine(hid)
    fg_own = ffn_gain.astype(F32)[:, None]
    mid_dot, rate_head = lax.psum((col_sum(hid_own * fg_own * gn), rate_part), "head")
    g_ffn_gain = jnp.sum(gn * hid_own * q2, 1)
    g_hidden = out_grad.astype(F32) + q2 * fg_own * gn - hid_own * q2**3 * mid_dot / width
    g_branch = g_hidden.astype(BF)
    g_w_out = nt(g_branch, mixed)
    gm = lax.psum_scatter(tn(w_out, g_branch), "head", scatter_dimension=0, tiled=True)
    n3 = mine(cen) * r3
    pg_own = post_gain.astype(F32)[:, None]
    ps_own = post_shift.astype(F32)[:, None]
    a_own, gelu_pull = jax.vjp(gelu_tanh, gate.astype(F32))
    g_post_gain = jnp.sum(gm * a_own * n3, 1)
    g_post_shift = jnp.sum(gm * a_own, 1)
    g_gate_pre = gelu_pull(gm * (n3 * pg_own + ps_own))[0].astype(BF)
    m = gm * a_own * pg_own
    s_plain, s_norm = lax.psum((col_sum(m), col_sum(m * n3)), "head")
    g_mixer = r3 * (m - s_plain / width - n3 * s_norm / width)
    dq, dk, dv, de, dgl, dsl, dw0, dc0, _, _ = ttt_bwd(
        reset, g_mixer, zt, zb, td, qa, ka, wt, er, vr, ig, ish, zw, zc
    )
    de_rows = de.reshape(tok // MB, heads, MB).transpose(1, 0, 2).reshape(heads, tok)
    g_logits = de_rows * vrow * (1.0 / HD) * sig * (1.0 - sig)
    gl = g_logits.astype(BF)
    g_inner_w = dw0.reshape(HD, heads, HD).transpose(1, 2, 0)
    g_inner_b = dc0.reshape(HD, heads, MB)[:, :, 0].T
    g_inner_g = dgl.reshape(HD, heads, MB).sum(-1).T
    g_inner_s = dsl.reshape(HD, heads, MB).sum(-1).T
    g_wq = nt(dq, nin)
    g_wk = nt(dk, nin)
    g_wv = nt(dv, nin)
    g_wg = nt(g_gate_pre, nin)
    g_wr = nt(nin, gl)
    part = tn(w_query, dq) + tn(w_key, dk) + tn(w_value, dv) + tn(w_gate, g_gate_pre) + nn(w_rate, gl)
    gi_full = lax.psum(part.astype(BF), "head").astype(F32)
    g_attn_gain = jnp.sum(mine(gi_full * x) * q1, 1)
    in_dot = col_sum(x * gains[0] * gi_full)
    x_own = tokens.astype(F32)
    g_tokens = (
        g_hidden + q1 * attn_gain.astype(F32)[:, None] * mine(gi_full) - x_own * q1**3 * in_dot / width
    )

    def over_dp(v):
        return lax.psum(v.astype(BF), "dp").astype(F32)

    mean_rate = over_dp(rate_head) / (tok * lax.axis_size("dp") * heads * devs)
    return (
        result, g_tokens, over_dp(g_attn_gain), over_dp(g_wq), over_dp(g_wk), over_dp(g_wv), over_dp(g_wg),
        over_dp(g_wr), over_dp(jnp.sum(g_logits, 1)), over_dp(g_inner_w), over_dp(g_inner_b),
        over_dp(g_inner_g), over_dp(g_inner_s), over_dp(g_post_gain), over_dp(g_post_shift), over_dp(g_w_out),
        over_dp(g_ffn_gain), over_dp(g_hgate), over_dp(g_hup), over_dp(g_down), mean_rate, max_rate,
    )


def solution(mesh):
    h = P("head")
    m = P("head", None)
    c = P("head", None, None)
    t = P("head", "dp")
    r = P(None, "head")
    ins = (t, P("dp"), h, m, m, m, m, r, h, c, m, m, m, h, h, m, h, m, m, m, t)
    outs = (t, t, h, m, m, m, m, r, h, c, m, m, m, h, h, m, h, m, m, m, P(), P())
    return jax.shard_map(on_device, mesh=mesh, in_specs=ins, out_specs=outs, check_vma=False)
```

```python
import jax, jax.numpy as jnp
from jax import lax
from jax.experimental import pallas as pl
from jax.experimental.pallas import tpu as pltpu
import functools
HD=64; MB=16; EPS=1e-6
F32=jnp.float32; BF=jnp.bfloat16

def nn(a,b): return lax.dot_general(a,b,(((1,),(0,)),((),())),preferred_element_type=F32)
def nt(a,b): return lax.dot_general(a,b,(((1,),(1,)),((),())),preferred_element_type=F32)
def tn(a,b): return lax.dot_general(a,b,(((0,),(0,)),((),())),preferred_element_type=F32)

def avg(x): return jnp.sum(x,0,keepdims=True)*(1.0/HD)

def lane_heads(heads, rows):
    return lax.broadcasted_iota(jnp.int32,(rows,heads*MB),1)//MB

def spread(x, heads):
    ids=lane_heads(heads,HD)
    return jnp.concatenate([jnp.where(ids==h,x,jnp.zeros_like(x)) for h in range(heads)],0)

def gather_blocks(x, heads):
    ids=lane_heads(heads,HD)
    out=jnp.zeros((HD,heads*MB),F32)
    for h in range(heads):
        out=out+jnp.where(ids==h,x[h*HD:(h+1)*HD],0.0)
    return out

def split_heads(ref, group, heads):
    cols=[ref[h*HD:(h+1)*HD, pl.ds(pl.multiple_of(group*128,128),128)] for h in range(heads)]
    return [jnp.concatenate([c[:,p*MB:(p+1)*MB] for c in cols],1) for p in range(8)]

def merge_heads(ref, group, parts, heads):
    for h in range(heads):
        blk=jnp.concatenate([p[:,h*MB:(h+1)*MB] for p in parts],1)
        ref[h*HD:(h+1)*HD, pl.ds(pl.multiple_of(group*128,128),128)]=blk.astype(ref.dtype)

def padded(x):
    rows=lax.broadcasted_iota(jnp.int32,(MB,x.shape[1]),0)
    return jnp.concatenate([x,jnp.where(rows==0,1.0,0.0).astype(F32)],0)

def same_head(heads):
    L=heads*MB
    r=lax.broadcasted_iota(jnp.int32,(L,L),0); c=lax.broadcasted_iota(jnp.int32,(L,L),1)
    return r//MB==c//MB, r%MB, c%MB

def step_grad(zt, td, g, s):
    mu=avg(zt); cen=zt-mu
    r=lax.rsqrt(avg(cen*cen)+EPS)
    n=cen*r
    v=n*g+s-td
    u=v*g
    m1=avg(u); m2=avg(u*n)
    return r,n,v,u,m2,r*(u-m1-n*m2)

def fwd_kernel(heads, nb, reset, qT, kT, vT, rows, consts,
               outT, zt_o, zb_o, td_o, qa_o, ka_o, wt_o, mp, q32):
    L=heads*MB
    same,ri,ci_=same_head(heads)
    tri=jnp.where(same&(ri<=ci_), 16.0/(ci_.astype(F32)+1.0), 0.0)
    diag=jnp.where(same,1.0,0.0)
    def pre(gr,_):
        qs=split_heads(qT,gr,heads); ks=split_heads(kT,gr,heads); vs=split_heads(vT,gr,heads)
        for p in range(8):
            b=gr*8+p
            td_o[b]=vs[p]-ks[p]
            q32[b]=qs[p]
            qa_o[b]=padded(qs[p]).astype(BF)
            ka_o[b]=padded(ks[p]).astype(BF)
        return 0
    lax.fori_loop(0,nb//8,pre,0)
    def pre2(b,_):
        nxt=jnp.minimum(b+1,nb-1)
        ke=(ka_o[b].astype(F32)*(rows[b,0:1]*(1.0/MB))).astype(BF)
        keep=jnp.where(reset[nxt]>0,0.0,1.0)
        m=tn(ke,ka_o[nxt])*(diag*keep)
        pt=tn(ke,qa_o[b])*tri
        mp[b]=jnp.concatenate([m,pt],1).astype(BF)
        return 0
    lax.fori_loop(0,nb,pre2,0,unroll=4)
    w0,c0,g,s=unpack_consts(consts,heads)
    def body(b,carry):
        zt,wt,ct=carry
        nxt=jnp.minimum(b+1,nb-1)
        rs=reset[nxt]>0
        wt_b=wt.astype(BF)
        wt_o[b]=wt_b; zt_o[b]=zt
        r,n,v,u,m2,gt=step_grad(zt,td_o[b],g,s)
        gb=gt.astype(BF)
        kn=spread(ka_o[nxt][:HD],heads)
        wsel=jnp.where(rs,w0,wt).astype(BF)
        csel=jnp.where(rs,c0,ct)
        yk=nn(wsel,kn)+csel
        yq=nn(wt_b,spread(qa_o[b][:HD],heads))+ct
        rr=nn(gb,mp[b])
        e16=rows[b,0:1]*(1.0/MB)
        ke=(ka_o[b][:HD].astype(F32)*e16).astype(BF)
        rw=nt(gb,spread(ke,heads))
        ec=jnp.where(same,jnp.broadcast_to(e16,(L,L)),0.0).astype(BF)
        rc=nt(gb,ec)
        zb_o[b]=yq-rr[:,L:]
        z2=yk-rr[:,:L]
        return z2,jnp.where(rs,w0,wt-rw),jnp.where(rs,c0,ct-rc)
    zt=nn(w0.astype(BF),spread(ka_o[0][:HD],heads))+c0
    lax.fori_loop(0,nb,body,(zt,w0,c0))
    def post(gr,_):
        outs=[]
        for p in range(8):
            b=gr*8+p
            zb=zb_o[b]; cen=zb-avg(zb)
            n=cen*lax.rsqrt(avg(cen*cen)+EPS)
            outs.append((q32[b]+n*g+s)*rows[b,1:2])
        merge_heads(outT,gr,outs,heads)
        return 0
    lax.fori_loop(0,nb//8,post,0)

VM=pl.BlockSpec(memory_space=pltpu.VMEM)
SM=pl.BlockSpec(memory_space=pltpu.SMEM)
AN=pl.BlockSpec(memory_space=pl.ANY)

def pack_consts(w0, c0, g, s):
    heads=w0.shape[0]
    cols=[w0.transpose(2,0,1).reshape(HD,heads*HD)]+[lane_cols(v) for v in (c0,g,s)]
    return jnp.concatenate([jnp.pad(v,((0,0),(0,-v.shape[1]%128))) for v in cols],1)

def unpack_consts(ref, heads):
    wide=(heads*HD+127)//128*128; step=(heads*MB+127)//128*128
    return [ref[:,:heads*HD]]+[ref[:,wide+i*step:wide+i*step+heads*MB] for i in range(3)]

def ttt_fwd(reset, qT,kT,vT, rows, consts):
    T=qT.shape[1]; heads=qT.shape[0]//HD; nb=T//MB; L=heads*MB; S=jax.ShapeDtypeStruct
    outs=[S((heads*HD,T),BF),S((nb,HD,L),F32),S((nb,HD,L),F32),S((nb,HD,L),F32),S((nb,HD+MB,L),BF),S((nb,HD+MB,L),BF),
          S((nb,HD,heads*HD),BF)]
    return pl.pallas_call(functools.partial(fwd_kernel,heads,nb),out_shape=outs,
        in_specs=[SM]+[VM]*5,out_specs=[VM]*len(outs),
        scratch_shapes=[pltpu.VMEM((nb,L,2*L),BF),pltpu.VMEM((nb,HD,L),F32)],
        compiler_params=pltpu.CompilerParams(vmem_limit_bytes=56<<20), name="mix_forward",
        cost_estimate=pl.CostEstimate(flops=T*heads*4000*64*50, bytes_accessed=T*heads*64*40, transcendentals=0))(
            reset,qT,kT,vT,rows,consts)

def bwd_kernel(heads, nb, base, last, reset, dOT, zt_i, zb_i, td_i, qa_i, ka_i, wt_i, rows, consts, *refs):
    if last:
        li=lci=None
    else:
        li,lci=refs[:2]; refs=refs[5:]
    (dqT, dkT, dvT, de_o, dg_o, ds_o, dw0_o, dc0_o, lo, lco,
               n_s, v_s, r_s, m2_s, gb_s, gh_s, nm_s, u_s, uc_s, dq_s, dk_s, du_s, dz_s, h_s, la_s)=refs
    L=heads*MB
    _,_,g,s=unpack_consts(consts,heads)
    same,ri,cj=same_head(heads)
    tri=jnp.where(same&(cj<=ri),1.0/(ri.astype(F32)+1.0),0.0)
    diag=jnp.where(same,1.0,0.0)
    diag_b=diag.astype(BF)
    dg_o[...]=jnp.zeros((HD,L),F32); ds_o[...]=jnp.zeros((HD,L),F32)
    dw0_o[...]=jnp.zeros_like(dw0_o); dc0_o[...]=jnp.zeros_like(dc0_o)
    def pre(gr,_):
        dos=split_heads(dOT,gr,heads)
        dga=jnp.zeros((HD,L),F32); dsa=jnp.zeros((HD,L),F32)
        for p in range(8):
            b=gr*8+p
            dO=dos[p].astype(F32)*rows[b,1:2]
            zb=zb_i[b]; cen=zb-avg(zb); rb=lax.rsqrt(avg(cen*cen)+EPS); nbar=cen*rb
            dga=dga+dO*nbar; dsa=dsa+dO
            dn=dO*g
            dzb=rb*(dn-avg(dn)-nbar*avg(dn*nbar))
            dzb_b=dzb.astype(BF)
            r,n,v,u,m2,gt=step_grad(zt_i[b],td_i[b],g,s)
            gb=gt.astype(BF)
            n_s[b]=n; v_s[b]=v; r_s[b]=r; m2_s[b]=m2; gb_s[b]=gt
            e=rows[b,0:1]
            ka=ka_i[b]; qa=qa_i[b]
            st=tn(qa,ka)*tri
            gh_s[b]=-nn(dzb_b,(st*e).astype(BF))
            dp=-tn(dzb_b,gb)
            de_o[b]=jnp.sum(dp*st,0,keepdims=True)
            dS=(dp*tri*e).astype(BF)
            dq_s[b]=dO+gather_blocks(tn(wt_i[b],dzb_b),heads)+nt(ka[:HD],dS)
            dk_s[b]=nn(qa[:HD],dS)
            prev=jnp.maximum(b-1,0)
            keep=jnp.where(reset[base+b]>0,0.0,1.0)
            nm_s[b]=(tn(ka,ka_i[prev])*(diag*keep)).astype(BF)
            u_s[b]=nt(dzb_b,spread(qa[:HD],heads))
            uc_s[b]=nn(dzb_b,diag_b)
        dg_o[...]+=dga; ds_o[...]+=dsa
        return 0
    lax.fori_loop(0,nb//8,pre,0)
    def body(k,carry):
        ht,la,lc=carry
        b=nb-1-k
        prev=jnp.maximum(b-1,0)
        rs=reset[base+b]>0
        n=n_s[b]; v=v_s[b]; r=r_s[b]; m2=m2_s[b]; gt=gb_s[b]
        h_s[b]=ht
        la_s[b]=la.astype(BF)
        dG=gh_s[b]-(rows[b,0:1]*(1.0/MB))*ht
        da=r*dG
        m3=avg(da); m4=avg(da*n); m6a=avg(dG*gt)
        du=da-m3-n*m4
        dn=(du*g-v*m4)*g-da*m2
        m5=avg(dn); m6=m6a+avg(dn*n)
        dz=(r*(dn-m5-n*m6)).astype(BF)
        du_s[b]=du
        dz_s[b]=dz
        la2=la+u_s[b]; lc2=lc+uc_s[b]
        y=nn(la2.astype(BF),spread(ka_i[prev][:HD],heads))+lc2
        h2=jnp.where(rs,0.0,y)+nn(dz,nm_s[b])
        la3=la2+nt(dz,spread(ka_i[b][:HD],heads)); lc3=lc2+nn(dz,diag_b)
        @pl.when(rs)
        def _():
            dw0_o[...]+=la3; dc0_o[...]+=lc3
        return h2,jnp.where(rs,0.0,la3),jnp.where(rs,0.0,lc3)
    la=jnp.zeros((HD,heads*HD),F32) if last else li[...]
    lc=jnp.zeros((HD,L),F32) if last else lci[...]
    ht=nn(la.astype(BF),spread(ka_i[nb-1][:HD],heads))+lc
    ht,la,lc=lax.fori_loop(0,nb,body,(ht,la,lc))
    lo[...]=la; lco[...]=lc
    def post(gr,_):
        dqs=[];dks=[];dvs=[]
        dga=jnp.zeros((HD,L),F32); dsa=jnp.zeros((HD,L),F32)
        for p in range(8):
            b=gr*8+p
            du=du_s[b]; dug=du*g; gt=gb_s[b]
            dga=dga+du*v_s[b]+dug*n_s[b]; dsa=dsa+dug
            dvs.append(-dug)
            dqs.append(dq_s[b])
            de_o[b]=de_o[b]-avg(gt*h_s[b])*(HD/MB)
            dks.append(dug+dk_s[b]-(rows[b,0:1]*(1.0/MB))*gather_blocks(tn(la_s[b],gt.astype(BF)),heads)
                       +gather_blocks(tn(wt_i[b],dz_s[b]),heads))
        merge_heads(dqT,gr,dqs,heads); merge_heads(dkT,gr,dks,heads); merge_heads(dvT,gr,dvs,heads)
        dg_o[...]+=dga; ds_o[...]+=dsa
        return 0
    lax.fori_loop(0,nb//8,post,0)

def ttt_bwd(part, parts, reset, dOT, zt,zb,td,qa,ka,wt,rows,consts, carry=None):
    T=dOT.shape[1]//parts; heads=dOT.shape[0]//HD; nb=T//MB; L=heads*MB; S=jax.ShapeDtypeStruct
    W=heads*HD; last=part==parts-1
    outs=[S((W,T*parts),BF)]*3+[S((nb,1,L),F32)]+[S((HD,L),F32)]*2+[S((HD,W),F32),S((HD,L),F32)]*2
    V=pltpu.VMEM
    scr=[V((nb,HD,L),F32),V((nb,HD,L),F32),V((nb,1,L),F32),V((nb,1,L),F32),V((nb,HD,L),F32),V((nb,HD,L),F32),
         V((nb,L,L),BF),V((nb,HD,W),F32),V((nb,HD,L),F32),V((nb,HD,L),F32),V((nb,HD,L),F32),V((nb,HD,L),F32),
         V((nb,HD,L),BF),V((nb,HD,L),F32),V((nb,HD,W),BF)]
    def whole(*dims): return pl.BlockSpec(dims,lambda i:(0,)*len(dims))
    def third(*dims): return pl.BlockSpec((nb,)+dims,lambda i:(part,)+(0,)*len(dims))
    nat=pl.BlockSpec((W,T),lambda i:(0,part))
    ins=[SM,nat]+[third(HD,L)]*3+[third(HD+MB,L)]*2+[third(HD,W),third(2,L),whole(*consts.shape)]
    args=[reset,dOT,zt,zb,td,qa,ka,wt,rows,consts]
    alias={}
    if not last:
        ins+=[whole(HD,W),whole(HD,L)]+[AN]*3
        alias={12:0,13:1,14:2}
        args+=list(carry)
    return pl.pallas_call(functools.partial(bwd_kernel,heads,nb,part*nb,last),out_shape=outs,grid=(1,),
        in_specs=ins,out_specs=[nat]*3+[whole(nb,1,L)]+[whole(HD,L)]*2+[whole(HD,W),whole(HD,L)]*2,
        scratch_shapes=scr,input_output_aliases=alias,
        compiler_params=pltpu.CompilerParams(vmem_limit_bytes=60<<20), name="mix_backward",
        cost_estimate=pl.CostEstimate(flops=T*heads*4000*64*60, bytes_accessed=T*heads*64*60, transcendentals=0))(*args)

def lane_rows(x, heads):
    T=x.shape[1]
    return x.reshape(heads,T//MB,MB).transpose(1,0,2).reshape(T//MB,1,heads*MB)
def lane_cols(x):
    return jnp.repeat(x.T,MB,axis=1)


ROWS = 64


def fetch(pieces, spots, buf, sems):
    copies = []
    for i, p in enumerate(pieces):
        at = pl.ds(pl.multiple_of(spots[i], 16), p.shape[0])
        copies.append(pltpu.make_async_copy(p, buf.at[at], sems.at[i]))
        copies[-1].start()
    for c in copies:
        c.wait()


def fold(buf, width, f):
    def add(i, acc):
        v = f(buf[pl.ds(pl.multiple_of(i * ROWS, ROWS), ROWS), :].astype(F32))
        return acc + jnp.sum(v.reshape(ROWS // 8, 8, v.shape[1]), 0)

    acc = lax.fori_loop(0, width // ROWS, add, jnp.zeros((8, buf.shape[1]), F32))
    return jnp.sum(acc, 0, keepdims=True)


def rms_kernel(n, lane, width, spots, gains, *refs):
    pieces, (out, scale_out, buf, sems) = refs[:n], refs[n:]
    fetch(pieces, spots, buf, sems)
    scale = lax.rsqrt(fold(buf, width, lambda v: v * v) * (1.0 / width) + EPS)
    scale_out[...] = scale

    def write(i, _):
        at = pl.ds(pl.multiple_of(i * ROWS, ROWS), ROWS)
        gain = gains[at, lane:lane + 1].astype(F32)
        out[at, :] = (buf[at, :].astype(F32) * scale * gain).astype(BF)
        return 0

    lax.fori_loop(0, width // ROWS, write, 0)


def mixed_kernel(n, width, spots, gains, gates, *refs):
    pieces, (out, mean_out, scale_out, buf, sems) = refs[:n], refs[n:]
    fetch(pieces, spots, buf, sems)
    mean = fold(buf, width, lambda v: v) * (1.0 / width)
    scale = lax.rsqrt(fold(buf, width, lambda v: (v - mean) * (v - mean)) * (1.0 / width) + EPS)
    mean_out[...] = mean
    scale_out[...] = scale

    def write(i, _):
        at = pl.ds(pl.multiple_of(i * ROWS, ROWS), ROWS)
        normed = (buf[at, :].astype(F32) - mean) * scale * gains[at, 1:2].astype(F32) + gains[at, 2:3].astype(F32)
        out[at, :] = (normed * jax.nn.gelu(gates[at, :].astype(F32), approximate=True)).astype(BF)
        return 0

    lax.fori_loop(0, width // ROWS, write, 0)


def rms_rows(pieces, spots, gains, lane, tok, width):
    n = len(pieces)
    return pl.pallas_call(
        functools.partial(rms_kernel, n, lane, width),
        out_shape=[jax.ShapeDtypeStruct((width, tok), BF), jax.ShapeDtypeStruct((1, tok), F32)],
        in_specs=[SM, VM] + [AN] * n, out_specs=[VM, VM],
        scratch_shapes=[pltpu.VMEM((width, tok), BF), pltpu.SemaphoreType.DMA((n,))],
        compiler_params=pltpu.CompilerParams(vmem_limit_bytes=40 << 20), name="rms_rows",
        cost_estimate=pl.CostEstimate(flops=8 * width * tok, bytes_accessed=4 * width * tok, transcendentals=0),
    )(spots, gains, *pieces)


def mixed_rows(pieces, spots, gates, gains, tok, width):
    n = len(pieces)
    return pl.pallas_call(
        functools.partial(mixed_kernel, n, width),
        out_shape=[jax.ShapeDtypeStruct((width, tok), BF)] + [jax.ShapeDtypeStruct((1, tok), F32)] * 2,
        in_specs=[SM, VM, VM] + [AN] * n, out_specs=[VM] * 3,
        scratch_shapes=[pltpu.VMEM((width, tok), BF), pltpu.SemaphoreType.DMA((n,))],
        compiler_params=pltpu.CompilerParams(vmem_limit_bytes=48 << 20), name="mixed_rows",
        cost_estimate=pl.CostEstimate(flops=20 * width * tok, bytes_accessed=6 * width * tok, transcendentals=0),
    )(spots, gains, gates, *pieces)


def hold(x, *deps):
    return lax.optimization_barrier((x,) + deps)[0]


def spread_pieces(x, devs, *deps):
    if devs != 8:
        return [lax.all_gather(x, "head", axis=0, tiled=True)]
    rows = x.shape[0]

    def swap(v, bit):
        return lax.ppermute(v, "head", [(i, i ^ bit) for i in range(8)])

    along_x = swap(x, 2)
    along_y = swap(x, 4)
    peer = swap(x, 1)
    if deps:
        along_x, along_y = hold(along_x, *deps), hold(along_y, *deps)
    diag_low = swap(along_x[:rows // 2], 4)
    diag_high = swap(along_y[rows // 2:], 2)
    return [x, peer, along_x, swap(along_x, 1), along_y, swap(along_y, 1),
            diag_low, diag_high, swap(diag_low, 1), swap(diag_high, 1)]


def piece_spots(own, devs):
    if devs != 8:
        return jnp.zeros((1,), jnp.int32)
    me = lax.axis_index("head")
    half = own // 2
    places = [(0, 0), (1, 0), (2, 0), (3, 0), (4, 0), (5, 0), (6, 0), (6, half), (7, 0), (7, half)]
    return jnp.stack([(me ^ bits) * own + off for bits, off in places]).astype(jnp.int32)


from jax.sharding import PartitionSpec as P


def col_sum(x):
    return jnp.sum(x, 0, keepdims=True)


def gelu_tanh(values):
    return jax.nn.gelu(values, approximate=True)


def layout(seq_lens, row_count):
    padded = (seq_lens + MB - 1) // MB * MB
    starts = jnp.cumsum(padded) - padded
    positions = jnp.arange(row_count, dtype=jnp.int32)
    inside = (positions[None, :] >= starts[:, None]) & (positions[None, :] < (starts + seq_lens)[:, None])
    valid_rows = jnp.any(inside, axis=0).astype(F32)
    block_first = jnp.arange(row_count // MB, dtype=jnp.int32) * MB
    begins = jnp.any((starts[:, None] == block_first[None, :]) & (seq_lens[:, None] > 0), axis=0)
    return valid_rows, (begins | (block_first == 0)).astype(jnp.int32)


class LineSum:
    def __init__(self, x):
        self.x = x
        self.near = lax.ppermute(x, "dp", [(0, 1), (3, 2)])

    def cross(self, *deps):
        near = hold(self.near, *deps) if deps else self.near
        self.half = (self.x.astype(F32) + near.astype(F32)).astype(BF)
        self.across = lax.ppermute(self.half, "dp", [(1, 2), (2, 1)])

    def back(self, *deps):
        across = hold(self.across, *deps) if deps else self.across
        self.total = (self.half.astype(F32) + across.astype(F32)).astype(BF)
        self.ends = lax.ppermute(self.total, "dp", [(1, 0), (2, 3)])

    def result(self, *deps):
        ends = hold(self.ends, *deps) if deps else self.ends
        at = lax.axis_index("dp")
        return jnp.where((at == 0) | (at == 3), ends, self.total).astype(F32)


class WholeSum:
    def __init__(self, x):
        self.x = self.half = self.total = x

    def cross(self, *deps):
        pass

    def back(self, *deps):
        pass

    def result(self, *deps):
        return lax.psum(self.x, "dp").astype(F32)


def on_device(
    tokens, lengths, attn_gain, w_query, w_key, w_value, w_gate, w_rate, rate_bias,
    inner_weight, inner_bias, inner_gain, inner_shift, post_gain, post_shift, w_out,
    ffn_gain, w_hidden_gate, w_hidden_up, w_down, out_grad,
):
    tok = tokens.shape[1]
    own = tokens.shape[0]
    heads = inner_weight.shape[0]
    devs = lax.axis_size("head")
    width = own * devs
    line = LineSum if lax.axis_size("dp") == 4 else WholeSum

    def gather(x):
        return lax.all_gather(x, "head", axis=0, tiled=True)

    valid, reset = layout(lengths, tok)
    vrow = valid[None, :]
    spots = piece_spots(own, devs)
    consts = pack_consts(*[v.astype(F32) for v in (inner_weight, inner_bias, inner_gain, inner_shift)])
    gains = lax.all_gather(jnp.stack([attn_gain, post_gain, post_shift, ffn_gain]), "head", axis=1, tiled=True)
    gains = jnp.pad(gains.T, ((0, 0), (0, 124)))
    tok_pieces = spread_pieces(tokens, devs, gains, consts)
    g_full = gather(hold(out_grad, *tok_pieces[-4:-2]))
    nin, q1 = rms_rows(tok_pieces, spots, gains, 0, tok, width)
    gate = nn(w_gate, nin).astype(BF)
    gates = gather(hold(gate, g_full) if devs != 8 else gate)
    nin_q = hold(nin, gate)
    q_t = nn(w_query, nin_q)
    k_t = nn(w_key, nin_q)
    v_t = nn(w_value, nin_q)
    logits = tn(w_rate, nin) + rate_bias.astype(F32)[:, None]
    sig = jax.nn.sigmoid(logits)
    masked = sig * vrow
    er = lane_rows(masked * (1.0 / HD), heads)
    vr = lane_rows(jnp.broadcast_to(vrow, (heads, tok)), heads)
    rows = jnp.concatenate([er, vr], 1)
    mixer_own, zt, zb, td, qa, ka, wt = ttt_fwd(reset, q_t, k_t, v_t, rows, consts)

    mixed, mean3, r3 = mixed_rows(spread_pieces(mixer_own, devs), spots, gates, gains, tok, width)
    hidden = tokens.astype(F32) + nn(w_out, mixed)
    hidden_low = hidden.astype(BF)
    nmid, q2 = rms_rows(spread_pieces(hidden_low, devs), spots, gains, 3, tok, width)
    gate_val = nn(w_hidden_gate, nmid)
    up_val = nn(w_hidden_up, nmid)
    sg = jax.nn.sigmoid(gate_val)
    act = (gate_val * sg * up_val).astype(BF)

    def halves(x):
        cut = x.shape[0] // 32 * 16
        return line(x[:cut]), line(x[cut:])

    d0, d1 = halves(nt(act, g_full).astype(BF))
    g_act = nn(w_down, hold(g_full, d0.x))
    g_up = (g_act * gate_val * sg).astype(BF)
    g_gate = (g_act * up_val * sg * (1.0 + gate_val * (1.0 - sg))).astype(BF)
    gn_part = (tn(w_hidden_gate, g_gate) + tn(w_hidden_up, g_up)).astype(BF)
    gn = lax.psum_scatter(gn_part, "head", scatter_dimension=0, tiled=True)
    h0, h1 = halves(nt(hold(g_gate, gn_part), nmid).astype(BF))
    u0, u1 = halves(nt(hold(g_up, gn_part), nmid).astype(BF))
    d0.cross(u1.x)
    gn = hold(gn, d0.half).astype(F32)
    hid_own = hidden_low.astype(F32)
    fg_own = ffn_gain.astype(F32)[:, None]
    here = lax.axis_index("head") + 1
    marks = lax.broadcasted_iota(jnp.int32, (1, 128), 1)
    rates = jnp.where(marks == 0, jnp.sum(masked), jnp.where(marks == here, jnp.max(masked), 0.0))
    mid_dot, rates = lax.psum((col_sum(hid_own * fg_own * gn), rates), "head")
    g_ffn_gain = jnp.sum(gn * hid_own * q2, 1)
    g_hidden = out_grad.astype(F32) + q2 * fg_own * gn - hid_own * q2**3 * mid_dot / width
    g_branch = g_hidden.astype(BF)
    gm_part = tn(w_out, g_branch).astype(BF)
    gm = lax.psum_scatter(gm_part, "head", scatter_dimension=0, tiled=True)
    d1.cross(gm_part)
    d0.back(gm_part, d1.half)
    so = line(nt(hold(g_branch, d0.total), mixed).astype(BF))
    ffn_part = tn(w_down, hold(act, so.x)).astype(BF)
    h0.cross(so.x, ffn_part)
    d1.back(h0.half)
    gm = hold(gm, d1.total).astype(F32)
    h1.cross(gm)
    h0.back(h1.half)
    n3 = (mixer_own.astype(F32) - mean3) * r3
    pg_own = post_gain.astype(F32)[:, None]
    ps_own = post_shift.astype(F32)[:, None]
    a_own, gelu_pull = jax.vjp(gelu_tanh, gate.astype(F32))
    g_post_gain = jnp.sum(gm * a_own * n3, 1)
    g_post_shift = jnp.sum(gm * a_own, 1)
    g_gate_pre = gelu_pull(gm * (n3 * pg_own + ps_own))[0].astype(BF)
    m = gm * a_own * pg_own
    s_plain, s_norm = lax.psum((col_sum(m), col_sum(m * n3)), "head")
    g_mixer = r3 * (m - s_plain / width - n3 * s_norm / width)
    ffn = lax.psum_scatter(hold(ffn_part, gm), "head", scatter_dimension=0, tiled=True)
    result = (hidden + ffn.astype(F32)).astype(BF)
    sg_w = line(nt(hold(g_gate_pre, s_plain), nin).astype(BF))
    g_mixer = hold(g_mixer, sg_w.x, h0.total)
    saved = (zt, zb, td, qa, ka, wt, rows, consts)
    b1 = ttt_bwd(1, 2, reset, g_mixer, *saved)
    u0.cross(b1[8])
    h1.back(b1[8], u0.half)
    lam, lam_c = hold(b1[8], h1.total), b1[9]
    b0 = ttt_bwd(0, 2, reset, g_mixer, *saved, carry=(lam, lam_c) + tuple(b1[:3]))
    dq, dk, dv = b0[:3]
    de = jnp.concatenate([b0[3], b1[3]], 0)
    dgl, dsl, dw0, dc0 = [b0[i] + b1[i] for i in range(4, 8)]
    u1.cross(dq)
    de_rows = de.reshape(tok // MB, heads, MB).transpose(1, 0, 2).reshape(heads, tok)
    g_logits = de_rows * vrow * (1.0 / HD) * sig * (1.0 - sig)
    gl = g_logits.astype(BF)
    g_inner_w = dw0.reshape(HD, heads, HD).transpose(1, 2, 0)
    g_inner_b = dc0.reshape(HD, heads, MB)[:, :, 0].T
    g_inner_g = dgl.reshape(HD, heads, MB).sum(-1).T
    g_inner_s = dsl.reshape(HD, heads, MB).sum(-1).T
    nin_l = hold(nin, u1.half)
    q = line(nt(dq, nin_l).astype(BF))
    k = line(nt(dk, nin_l).astype(BF))
    v0, v1 = halves(nt(dv, nin_l).astype(BF))
    u0.back(v1.x)
    gi_part = hold((tn(w_query, dq) + tn(w_key, dk) + tn(w_value, dv) + tn(w_gate, g_gate_pre) + nn(w_rate, gl)).astype(BF), u0.total)
    gi = lax.psum_scatter(gi_part, "head", scatter_dimension=0, tiled=True)
    so.cross(gi_part)
    g_wr = nt(gl, hold(nin_l, so.half))
    u1.back(g_wr)
    sg_w.cross(u1.total)
    so.back(sg_w.half)
    q.cross(so.total)
    gi = hold(gi, q.half).astype(F32)
    x_own = tokens.astype(F32)
    ag_own = attn_gain.astype(F32)[:, None]
    in_dot = lax.psum(col_sum(x_own * ag_own * gi), "head")
    sg_w.back(in_dot)
    k.cross(sg_w.total)
    g_attn_gain = jnp.sum(gi * x_own * q1, 1)
    g_tokens = g_hidden + q1 * ag_own * gi - x_own * q1**3 * in_dot / width
    there = lax.axis_index("dp") + 1
    top = jnp.max(jnp.where((marks > 0), rates, 0.0))
    rates = jnp.where(marks == 0, rates[0, 0], jnp.where(marks == there, top, 0.0))
    small = [g_attn_gain, g_wr, jnp.sum(g_logits, 1), g_inner_w, g_inner_b, g_inner_g, g_inner_s,
             g_post_gain, g_post_shift, g_ffn_gain]
    small = lax.psum([hold(x.astype(BF), k.half) for x in small] + [rates], "dp")
    rates = small.pop()
    s_attn, s_wr, s_rb, s_iw, s_ib, s_ig, s_is, s_pg, s_ps, s_fg = [x.astype(F32) for x in small]
    mean_rate = rates[0, 0] / (tok * lax.axis_size("dp") * heads * devs)
    max_rate = jnp.max(jnp.where(marks > 0, rates, 0.0))
    q.back(s_attn)
    v0.cross(q.total)
    v1.cross(v0.half)
    k.back(v1.half)
    v0.back(k.total)
    v1.back(v0.total)

    def joined(*parts):
        return jnp.concatenate([s.result() for s in parts], 0)

    return (
        result, g_tokens, s_attn, q.result(), k.result(), joined(v0, v1), sg_w.result(),
        s_wr.T, s_rb, s_iw, s_ib, s_ig, s_is, s_pg, s_ps, so.result(),
        s_fg, joined(h0, h1), joined(u0, u1), joined(d0, d1), mean_rate, max_rate,
    )


def solution(mesh):
    h = P("head")
    m = P("head", None)
    c = P("head", None, None)
    t = P("head", "dp")
    r = P(None, "head")
    ins = (t, P("dp"), h, m, m, m, m, r, h, c, m, m, m, h, h, m, h, m, m, m, t)
    outs = (t, t, h, m, m, m, m, r, h, c, m, m, m, h, h, m, h, m, m, m, P(), P())
    return jax.shard_map(on_device, mesh=mesh, in_specs=ins, out_specs=outs, check_vma=False)
```

```python
import jax, jax.numpy as jnp
from jax import lax
from jax.experimental import pallas as pl
from jax.experimental.pallas import tpu as pltpu
import functools
HD=64; MB=16; EPS=1e-6
F32=jnp.float32; BF=jnp.bfloat16

def nn(a,b): return lax.dot_general(a,b,(((1,),(0,)),((),())),preferred_element_type=F32)
def nt(a,b): return lax.dot_general(a,b,(((1,),(1,)),((),())),preferred_element_type=F32)
def tn(a,b): return lax.dot_general(a,b,(((0,),(0,)),((),())),preferred_element_type=F32)

def avg(x): return jnp.sum(x,0,keepdims=True)*(1.0/HD)

def lane_heads(heads, rows):
    return lax.broadcasted_iota(jnp.int32,(rows,heads*MB),1)//MB

def spread(x, heads):
    ids=lane_heads(heads,HD)
    return jnp.concatenate([jnp.where(ids==h,x,jnp.zeros_like(x)) for h in range(heads)],0)

def gather_blocks(x, heads):
    ids=lane_heads(heads,HD)
    out=jnp.zeros((HD,heads*MB),F32)
    for h in range(heads):
        out=out+jnp.where(ids==h,x[h*HD:(h+1)*HD],0.0)
    return out

def split_heads(ref, group, heads):
    cols=[ref[h*HD:(h+1)*HD, pl.ds(pl.multiple_of(group*128,128),128)] for h in range(heads)]
    return [jnp.concatenate([c[:,p*MB:(p+1)*MB] for c in cols],1) for p in range(8)]

def merge_heads(ref, group, parts, heads):
    for h in range(heads):
        blk=jnp.concatenate([p[:,h*MB:(h+1)*MB] for p in parts],1)
        ref[h*HD:(h+1)*HD, pl.ds(pl.multiple_of(group*128,128),128)]=blk.astype(ref.dtype)

def padded(x):
    rows=lax.broadcasted_iota(jnp.int32,(MB,x.shape[1]),0)
    return jnp.concatenate([x,jnp.where(rows==0,1.0,0.0).astype(F32)],0)

def same_head(heads):
    L=heads*MB
    r=lax.broadcasted_iota(jnp.int32,(L,L),0); c=lax.broadcasted_iota(jnp.int32,(L,L),1)
    return r//MB==c//MB, r%MB, c%MB

def step_grad(zt, td, g, s):
    mu=avg(zt); cen=zt-mu
    r=lax.rsqrt(avg(cen*cen)+EPS)
    n=cen*r
    v=n*g+s-td
    u=v*g
    m1=avg(u); m2=avg(u*n)
    return r,n,v,u,m2,r*(u-m1-n*m2)

def fwd_kernel(heads, nb, reset, qT, kT, vT, rate, valid, consts,
               outT, zt_o, zb_o, td_o, qa_o, ka_o, wt_o, rows, mp, q32):
    L=heads*MB
    same,ri,ci_=same_head(heads)
    tri=jnp.where(same&(ri<=ci_), 16.0/(ci_.astype(F32)+1.0), 0.0)
    diag=jnp.where(same,1.0,0.0)
    def pre(gr,_):
        qs=split_heads(qT,gr,heads); ks=split_heads(kT,gr,heads); vs=split_heads(vT,gr,heads)
        at=pl.ds(pl.multiple_of(gr*128,128),128)
        rt=rate[:,at]; vl=valid[:,at]
        for p in range(8):
            b=gr*8+p
            cut=slice(p*MB,(p+1)*MB)
            rows[b]=jnp.concatenate([jnp.concatenate([rt[h:h+1,cut] for h in range(heads)],1),
                                     jnp.concatenate([vl[:,cut]]*heads,1)],0)
            td_o[b]=vs[p]-ks[p]
            q32[b]=qs[p]
            qa_o[b]=padded(qs[p]).astype(BF)
            ka_o[b]=padded(ks[p]).astype(BF)
        return 0
    lax.fori_loop(0,nb//8,pre,0)
    def pre2(b,_):
        nxt=jnp.minimum(b+1,nb-1)
        ke=(ka_o[b].astype(F32)*(rows[b,0:1]*(1.0/MB))).astype(BF)
        keep=jnp.where(reset[nxt]>0,0.0,1.0)
        m=tn(ke,ka_o[nxt])*(diag*keep)
        pt=tn(ke,qa_o[b])*tri
        mp[b]=jnp.concatenate([m,pt],1).astype(BF)
        return 0
    lax.fori_loop(0,nb,pre2,0,unroll=4)
    w0,c0,g,s=unpack_consts(consts,heads)
    def body(b,carry):
        zt,wt,ct=carry
        nxt=jnp.minimum(b+1,nb-1)
        rs=reset[nxt]>0
        wt_b=wt.astype(BF)
        wt_o[b]=wt_b; zt_o[b]=zt
        r,n,v,u,m2,gt=step_grad(zt,td_o[b],g,s)
        gb=gt.astype(BF)
        kn=spread(ka_o[nxt][:HD],heads)
        wsel=jnp.where(rs,w0,wt).astype(BF)
        csel=jnp.where(rs,c0,ct)
        yk=nn(wsel,kn)+csel
        yq=nn(wt_b,spread(qa_o[b][:HD],heads))+ct
        rr=nn(gb,mp[b])
        e16=rows[b,0:1]*(1.0/MB)
        ke=(ka_o[b][:HD].astype(F32)*e16).astype(BF)
        rw=nt(gb,spread(ke,heads))
        ec=jnp.where(same,jnp.broadcast_to(e16,(L,L)),0.0).astype(BF)
        rc=nt(gb,ec)
        zb_o[b]=yq-rr[:,L:]
        z2=yk-rr[:,:L]
        return z2,jnp.where(rs,w0,wt-rw),jnp.where(rs,c0,ct-rc)
    zt=nn(w0.astype(BF),spread(ka_o[0][:HD],heads))+c0
    lax.fori_loop(0,nb,body,(zt,w0,c0))
    def post(gr,_):
        outs=[]
        for p in range(8):
            b=gr*8+p
            zb=zb_o[b]; cen=zb-avg(zb)
            n=cen*lax.rsqrt(avg(cen*cen)+EPS)
            outs.append((q32[b]+n*g+s)*rows[b,1:2])
        merge_heads(outT,gr,outs,heads)
        return 0
    lax.fori_loop(0,nb//8,post,0)

VM=pl.BlockSpec(memory_space=pltpu.VMEM)
SM=pl.BlockSpec(memory_space=pltpu.SMEM)
AN=pl.BlockSpec(memory_space=pl.ANY)

def pack_consts(w0, c0, g, s):
    heads=w0.shape[0]
    cols=[w0.transpose(2,0,1).reshape(HD,heads*HD)]+[lane_cols(v) for v in (c0,g,s)]
    return jnp.concatenate([jnp.pad(v,((0,0),(0,-v.shape[1]%128))) for v in cols],1)

def unpack_consts(ref, heads):
    wide=(heads*HD+127)//128*128; step=(heads*MB+127)//128*128
    return [ref[:,:heads*HD]]+[ref[:,wide+i*step:wide+i*step+heads*MB] for i in range(3)]

def ttt_fwd(reset, qT,kT,vT, rate, valid, consts):
    T=qT.shape[1]; heads=qT.shape[0]//HD; nb=T//MB; L=heads*MB; S=jax.ShapeDtypeStruct
    outs=[S((heads*HD,T),BF),S((nb,HD,L),F32),S((nb,HD,L),F32),S((nb,HD,L),F32),S((nb,HD+MB,L),BF),S((nb,HD+MB,L),BF),
          S((nb,HD,heads*HD),BF),S((nb,2,L),F32)]
    def whole(v): return pl.BlockSpec(v.shape,lambda i:(0,)*len(v.shape))
    args=[qT,kT,vT,rate,valid,consts]
    return pl.pallas_call(functools.partial(fwd_kernel,heads,nb),out_shape=outs,grid=(1,),
        in_specs=[SM]+[whole(v) for v in args],out_specs=[whole(v) for v in outs],
        scratch_shapes=[pltpu.VMEM((nb,L,2*L),BF),pltpu.VMEM((nb,HD,L),F32)],
        compiler_params=pltpu.CompilerParams(vmem_limit_bytes=44<<20), name="mix_forward",
        cost_estimate=pl.CostEstimate(flops=T*heads*4000*64*50, bytes_accessed=T*heads*64*40, transcendentals=0))(
            reset,*args)

def bwd_kernel(heads, nb, base, last, reset, dOT, zt_i, zb_i, td_i, qa_i, ka_i, wt_i, rows, consts, *refs):
    if last:
        li=lci=None
    else:
        li,lci=refs[:2]; refs=refs[5:]
    (dqT, dkT, dvT, de_o, dg_o, ds_o, dw0_o, dc0_o, lo, lco,
               n_s, v_s, r_s, m2_s, gb_s, gh_s, nm_s, u_s, uc_s, dq_s, dk_s, du_s, dz_s, h_s, la_s, de_s)=refs
    L=heads*MB
    _,_,g,s=unpack_consts(consts,heads)
    same,ri,cj=same_head(heads)
    tri=jnp.where(same&(cj<=ri),1.0/(ri.astype(F32)+1.0),0.0)
    diag=jnp.where(same,1.0,0.0)
    diag_b=diag.astype(BF)
    dg_o[...]=jnp.zeros((HD,L),F32); ds_o[...]=jnp.zeros((HD,L),F32)
    dw0_o[...]=jnp.zeros_like(dw0_o); dc0_o[...]=jnp.zeros_like(dc0_o)
    def pre(gr,_):
        dos=split_heads(dOT,gr,heads)
        dga=jnp.zeros((HD,L),F32); dsa=jnp.zeros((HD,L),F32)
        for p in range(8):
            b=gr*8+p
            dO=dos[p].astype(F32)*rows[b,1:2]
            zb=zb_i[b]; cen=zb-avg(zb); rb=lax.rsqrt(avg(cen*cen)+EPS); nbar=cen*rb
            dga=dga+dO*nbar; dsa=dsa+dO
            dn=dO*g
            dzb=rb*(dn-avg(dn)-nbar*avg(dn*nbar))
            dzb_b=dzb.astype(BF)
            r,n,v,u,m2,gt=step_grad(zt_i[b],td_i[b],g,s)
            gb=gt.astype(BF)
            n_s[b]=n; v_s[b]=v; r_s[b]=r; m2_s[b]=m2; gb_s[b]=gt
            e=rows[b,0:1]
            ka=ka_i[b]; qa=qa_i[b]
            st=tn(qa,ka)*tri
            gh_s[b]=-nn(dzb_b,(st*e).astype(BF))
            dp=-tn(dzb_b,gb)
            de_s[b]=jnp.sum(dp*st,0,keepdims=True)
            dS=(dp*tri*e).astype(BF)
            dq_s[b]=dO+gather_blocks(tn(wt_i[b],dzb_b),heads)+nt(ka[:HD],dS)
            dk_s[b]=nn(qa[:HD],dS)
            prev=jnp.maximum(b-1,0)
            keep=jnp.where(reset[base+b]>0,0.0,1.0)
            nm_s[b]=(tn(ka,ka_i[prev])*(diag*keep)).astype(BF)
            u_s[b]=nt(dzb_b,spread(qa[:HD],heads))
            uc_s[b]=nn(dzb_b,diag_b)
        dg_o[...]+=dga; ds_o[...]+=dsa
        return 0
    lax.fori_loop(0,nb//8,pre,0)
    def body(k,carry):
        ht,la,lc=carry
        b=nb-1-k
        prev=jnp.maximum(b-1,0)
        rs=reset[base+b]>0
        n=n_s[b]; v=v_s[b]; r=r_s[b]; m2=m2_s[b]; gt=gb_s[b]
        h_s[b]=ht
        la_s[b]=la.astype(BF)
        dG=gh_s[b]-(rows[b,0:1]*(1.0/MB))*ht
        da=r*dG
        m3=avg(da); m4=avg(da*n); m6a=avg(dG*gt)
        du=da-m3-n*m4
        dn=(du*g-v*m4)*g-da*m2
        m5=avg(dn); m6=m6a+avg(dn*n)
        dz=(r*(dn-m5-n*m6)).astype(BF)
        du_s[b]=du
        dz_s[b]=dz
        la2=la+u_s[b]; lc2=lc+uc_s[b]
        y=nn(la2.astype(BF),spread(ka_i[prev][:HD],heads))+lc2
        h2=jnp.where(rs,0.0,y)+nn(dz,nm_s[b])
        la3=la2+nt(dz,spread(ka_i[b][:HD],heads)); lc3=lc2+nn(dz,diag_b)
        @pl.when(rs)
        def _():
            dw0_o[...]+=la3; dc0_o[...]+=lc3
        return h2,jnp.where(rs,0.0,la3),jnp.where(rs,0.0,lc3)
    la=jnp.zeros((HD,heads*HD),F32) if last else li[...]
    lc=jnp.zeros((HD,L),F32) if last else lci[...]
    ht=nn(la.astype(BF),spread(ka_i[nb-1][:HD],heads))+lc
    ht,la,lc=lax.fori_loop(0,nb,body,(ht,la,lc))
    lo[...]=la; lco[...]=lc
    def post(gr,_):
        dqs=[];dks=[];dvs=[];des=[]
        dga=jnp.zeros((HD,L),F32); dsa=jnp.zeros((HD,L),F32)
        for p in range(8):
            b=gr*8+p
            du=du_s[b]; dug=du*g; gt=gb_s[b]
            dga=dga+du*v_s[b]+dug*n_s[b]; dsa=dsa+dug
            dvs.append(-dug)
            dqs.append(dq_s[b])
            des.append(de_s[b]-avg(gt*h_s[b])*(HD/MB))
            dks.append(dug+dk_s[b]-(rows[b,0:1]*(1.0/MB))*gather_blocks(tn(la_s[b],gt.astype(BF)),heads)
                       +gather_blocks(tn(wt_i[b],dz_s[b]),heads))
        de_o[:,pl.ds(pl.multiple_of(gr*128,128),128)]=jnp.concatenate(
            [jnp.concatenate([d[:,h*MB:(h+1)*MB] for d in des],1) for h in range(heads)],0)
        merge_heads(dqT,gr,dqs,heads); merge_heads(dkT,gr,dks,heads); merge_heads(dvT,gr,dvs,heads)
        dg_o[...]+=dga; ds_o[...]+=dsa
        return 0
    lax.fori_loop(0,nb//8,post,0)

def ttt_bwd(part, parts, reset, dOT, zt,zb,td,qa,ka,wt,rows,consts, carry=None):
    T=dOT.shape[1]//parts; heads=dOT.shape[0]//HD; nb=T//MB; L=heads*MB; S=jax.ShapeDtypeStruct
    W=heads*HD; last=part==parts-1
    outs=[S((W,T*parts),BF)]*3+[S((heads,T),F32)]+[S((HD,L),F32)]*2+[S((HD,W),F32),S((HD,L),F32)]*2
    V=pltpu.VMEM
    scr=[V((nb,HD,L),F32),V((nb,HD,L),F32),V((nb,1,L),F32),V((nb,1,L),F32),V((nb,HD,L),F32),V((nb,HD,L),F32),
         V((nb,L,L),BF),V((nb,HD,W),F32),V((nb,HD,L),F32),V((nb,HD,L),F32),V((nb,HD,L),F32),V((nb,HD,L),F32),
         V((nb,HD,L),BF),V((nb,HD,L),F32),V((nb,HD,W),BF),V((nb,1,L),F32)]
    def whole(*dims): return pl.BlockSpec(dims,lambda i:(0,)*len(dims))
    def third(*dims): return pl.BlockSpec((nb,)+dims,lambda i:(part,)+(0,)*len(dims))
    nat=pl.BlockSpec((W,T),lambda i:(0,part))
    ins=[SM,nat]+[third(HD,L)]*3+[third(HD+MB,L)]*2+[third(HD,W),third(2,L),whole(*consts.shape)]
    args=[reset,dOT,zt,zb,td,qa,ka,wt,rows,consts]
    alias={}
    if not last:
        ins+=[whole(HD,W),whole(HD,L)]+[AN]*3
        alias={12:0,13:1,14:2}
        args+=list(carry)
    return pl.pallas_call(functools.partial(bwd_kernel,heads,nb,part*nb,last),out_shape=outs,grid=(1,),
        in_specs=ins,out_specs=[nat]*3+[whole(heads,T)]+[whole(HD,L)]*2+[whole(HD,W),whole(HD,L)]*2,
        scratch_shapes=scr,input_output_aliases=alias,
        compiler_params=pltpu.CompilerParams(vmem_limit_bytes=36<<20), name="mix_backward",
        cost_estimate=pl.CostEstimate(flops=T*heads*64, bytes_accessed=T*heads, transcendentals=0))(*args)

def lane_cols(x):
    return jnp.repeat(x.T,MB,axis=1)


ROWS = 64


def fetch(pieces, spots, buf, sems):
    copies = []
    for i, p in enumerate(pieces):
        at = pl.ds(pl.multiple_of(spots[i], 16), p.shape[0])
        copies.append(pltpu.make_async_copy(p, buf.at[at], sems.at[i]))
        copies[-1].start()
    for c in copies:
        c.wait()


def fold(buf, width, f):
    def add(i, acc):
        v = f(buf[pl.ds(pl.multiple_of(i * ROWS, ROWS), ROWS), :].astype(F32))
        return acc + jnp.sum(v.reshape(ROWS // 8, 8, v.shape[1]), 0)

    acc = lax.fori_loop(0, width // ROWS, add, jnp.zeros((8, buf.shape[1]), F32))
    return jnp.sum(acc, 0, keepdims=True)


def rms_kernel(n, lane, width, fresh, spots, blocks, *refs):
    pieces, (out, scale_out, gains, buf, sems, gain_sems) = refs[:n], refs[n:]
    if fresh:
        copies = []
        for i in range(blocks.shape[0]):
            at = pl.ds(pl.multiple_of(spots[i if i < 7 else 8], 16), blocks.shape[1])
            copies.append(pltpu.make_async_copy(blocks.at[i], gains.at[at], gain_sems.at[i]))
            copies[-1].start()
        fetch(pieces, spots, buf, sems)
        for c in copies:
            c.wait()
    else:
        fetch(pieces, spots, buf, sems)
    scale = lax.rsqrt(fold(buf, width, lambda v: v * v) * (1.0 / width) + EPS)
    scale_out[...] = scale
    source = gains if fresh else blocks

    def write(i, _):
        at = pl.ds(pl.multiple_of(i * ROWS, ROWS), ROWS)
        gain = source[at, lane:lane + 1].astype(F32)
        out[at, :] = (buf[at, :].astype(F32) * scale * gain).astype(BF)
        return 0

    lax.fori_loop(0, width // ROWS, write, 0)
    if not fresh:
        gains[...] = jnp.zeros_like(gains)


def moments_kernel(n, width, spots, *refs):
    pieces, (out, mean_out, scale_out, sems) = refs[:n], refs[n:]
    fetch(pieces, spots, out, sems)
    mean = fold(out, width, lambda v: v) * (1.0 / width)
    mean_out[...] = mean
    scale_out[...] = lax.rsqrt(fold(out, width, lambda v: (v - mean) * (v - mean)) * (1.0 / width) + EPS)


def rms_rows(pieces, spots, gains, lane, tok, width):
    n = len(pieces)
    fresh = gains.ndim == 3
    count = gains.shape[0] if fresh else 1
    S = jax.ShapeDtypeStruct
    return pl.pallas_call(
        functools.partial(rms_kernel, n, lane, width, fresh),
        out_shape=[S((width, tok), BF), S((1, tok), F32), S((width, 128) if fresh else (16, 128), BF)],
        in_specs=[SM, AN if fresh else VM] + [AN] * n, out_specs=[VM, VM, VM],
        scratch_shapes=[pltpu.VMEM((width, tok), BF), pltpu.SemaphoreType.DMA((n,)), pltpu.SemaphoreType.DMA((count,))],
        compiler_params=pltpu.CompilerParams(vmem_limit_bytes=16 << 20), name="rms_rows",
        cost_estimate=pl.CostEstimate(flops=8 * width * tok, bytes_accessed=4 * width * tok, transcendentals=0),
    )(spots, gains, *pieces)


def moments_rows(pieces, spots, tok, width):
    n = len(pieces)
    return pl.pallas_call(
        functools.partial(moments_kernel, n, width),
        out_shape=[jax.ShapeDtypeStruct((width, tok), BF)] + [jax.ShapeDtypeStruct((1, tok), F32)] * 2,
        in_specs=[SM] + [AN] * n, out_specs=[VM] * 3,
        scratch_shapes=[pltpu.SemaphoreType.DMA((n,))],
        compiler_params=pltpu.CompilerParams(vmem_limit_bytes=16 << 20), name="moments_rows",
        cost_estimate=pl.CostEstimate(flops=8 * width * tok, bytes_accessed=4 * width * tok, transcendentals=0),
    )(spots, *pieces)


def hold(x, *deps):
    return lax.optimization_barrier((x,) + deps)[0]


class Pieces:
    def __init__(self, x, devs):
        if devs != 8:
            self.direct = self.diag = (x,)
            self.all = [lax.all_gather(x, "head", axis=0, tiled=True)]
            return
        rows = x.shape[0]

        def swap(v, bit):
            return lax.ppermute(v, "head", [(i, i ^ bit) for i in range(8)])

        along_x = swap(x, 2)
        along_y = swap(x, 4)
        peer = swap(x, 1)
        low = swap(along_x[:rows // 2], 4)
        high = swap(along_y[rows // 2:], 2)
        self.direct = (along_x, along_y)
        self.diag = (low, high)
        self.all = [x, peer, along_x, swap(along_x, 1), along_y, swap(along_y, 1), low, high, swap(low, 1), swap(high, 1)]


class Scatter:
    def __init__(self, left, right, rows, own, devs):
        self.own, self.devs = own, devs
        self.terms = None
        if devs != 8:
            total = sum(tn(a, b) for a, b in zip(left, right)).astype(BF)
            self.pair = (total, total[:16])
            self.dot = jnp.sum(total.astype(F32) * rows.astype(F32), 0, keepdims=True)
            return
        me = lax.axis_index("head")
        self.chip = me // 2
        keep, give, self.dot = parts((me % 2).reshape(1), left, right, rows, own)
        self.pair = (keep, give)

    def swap(self, v, bit):
        return lax.ppermute(v, "head", [(i, i ^ bit) for i in range(8)])

    def add(self, a, b):
        return (a.astype(F32) + b.astype(F32)).astype(BF)

    def spread(self):
        if self.devs != 8:
            return
        half = self.own // 2
        self.acc = self.add(self.pair[0], self.swap(self.pair[1], 1))
        far, to_x, to_y, home = [lax.dynamic_index_in_dim(self.acc, self.chip ^ k, 0, keepdims=False) for k in (3, 1, 2, 0)]
        low, high = self.swap(far[:half], 2), self.swap(far[half:], 4)
        x_low, y_high = self.swap(to_x[:half], 2), self.swap(to_y[half:], 4)
        x_high, y_low = self.swap(self.add(to_x[half:], high), 2), self.swap(self.add(to_y[:half], low), 4)
        self.terms = (home, (x_low, x_high), (y_low, y_high))

    def result(self):
        if self.devs != 8:
            return lax.psum_scatter(self.pair[0], "head", scatter_dimension=0, tiled=True).astype(F32)
        if self.terms is None:
            self.spread()
        home, *pairs = self.terms
        total = home.astype(F32)
        for pair in pairs:
            total = total + jnp.concatenate([v.astype(F32) for v in pair], 0)
        return total


def spread_gains(cols, devs):
    cols = jnp.pad(cols, ((0, 0), (0, 128 - cols.shape[1])))[None]
    if devs != 8:
        return lax.all_gather(cols, "head", axis=1, tiled=True)
    for bit in (1, 2, 4):
        cols = jnp.concatenate([cols, lax.ppermute(cols, "head", [(i, i ^ bit) for i in range(8)])], 0)
    return cols


def piece_spots(own, devs):
    if devs != 8:
        return jnp.zeros((1,), jnp.int32)
    me = lax.axis_index("head")
    half = own // 2
    places = [(0, 0), (1, 0), (2, 0), (3, 0), (4, 0), (5, 0), (6, 0), (6, half), (7, 0), (7, half)]
    return jnp.stack([(me ^ bits) * own + off for bits, off in places]).astype(jnp.int32)


FREE = pl.CostEstimate(flops=0, bytes_accessed=0, transcendentals=0)
COLS = 512


def wide_params(mib):
    return pltpu.CompilerParams(vmem_limit_bytes=mib << 20)


def wgrad_kernel(a, b, out):
    out[...] = nt(a[...], b[...]).astype(BF)


def wgrad(a, b):
    rows, tok = a.shape
    n = b.shape[0]
    return pl.pallas_call(
        wgrad_kernel, grid=(n // COLS,), out_shape=jax.ShapeDtypeStruct((rows, n), BF),
        in_specs=[pl.BlockSpec((rows, tok), lambda i: (0, 0)), pl.BlockSpec((COLS, tok), lambda i: (i, 0))],
        out_specs=pl.BlockSpec((rows, COLS), lambda i: (0, i)),
        compiler_params=wide_params(24), cost_estimate=FREE, name="weight_gradient")(a, b)


def column_blocks(v):
    return pl.BlockSpec((v.shape[0], COLS), lambda i: (0, i))


def half_kernel(x, air, out):
    out[...] = (x[...].astype(F32) + air[:x.shape[0], :].astype(F32)).astype(BF)


def half_sum(x, air):
    return pl.pallas_call(
        half_kernel, grid=(x.shape[1] // COLS,), out_shape=jax.ShapeDtypeStruct(x.shape, BF),
        in_specs=[column_blocks(x), column_blocks(air)], out_specs=column_blocks(x),
        compiler_params=wide_params(16), cost_estimate=FREE, name="half_sum")(x, air)


def outgoing_kernel(end, x, half, air, out):
    def put(v):
        out[:v.shape[0], :] = v
        if v.shape[0] < out.shape[0]:
            out[v.shape[0]:, :] = jnp.zeros((out.shape[0] - v.shape[0], out.shape[1]), BF)

    @pl.when(end[0] > 0)
    def _():
        put(x[...])

    @pl.when(end[0] == 0)
    def _():
        put((half[...].astype(F32) + air[...].astype(F32)).astype(BF))


def outgoing(end, x, half, air):
    out = jax.ShapeDtypeStruct((max(x.shape[0], half.shape[0]), x.shape[1]), BF)
    return pl.pallas_call(
        outgoing_kernel, grid=(x.shape[1] // COLS,), out_shape=out,
        in_specs=[SM] + [column_blocks(v) for v in (x, half, air)], out_specs=column_blocks(out),
        compiler_params=wide_params(16), cost_estimate=FREE, name="outgoing")(end, x, half, air)


def finish_kernel(sizes, end, *refs):
    n = len(sizes)
    airs, sents, out = refs[:n], refs[n:2 * n], refs[2 * n]
    for chosen, kind in ((airs, 1), (sents, 0)):
        @pl.when(end[0] == kind)
        def _():
            at = 0
            for v, rows in zip(chosen, sizes):
                out[at:at + rows, :] = v[:rows, :].astype(F32)
                at += rows


def finish(end, jobs):
    sizes = [job.x.shape[0] for job in jobs]
    vals = [job.landed for job in jobs] + [job.sent for job in jobs]
    out = jax.ShapeDtypeStruct((sum(sizes), vals[0].shape[1]), F32)
    return pl.pallas_call(
        functools.partial(finish_kernel, sizes), grid=(out.shape[1] // COLS,), out_shape=out,
        in_specs=[SM] + [column_blocks(v) for v in vals], out_specs=column_blocks(out),
        compiler_params=wide_params(24), cost_estimate=FREE, name="finish")(end, *vals)


def parts_kernel(n, core, *refs):
    left, right, (rows, keep, give, dot) = refs[:n], refs[n:2 * n], refs[2 * n:]
    which = pl.program_id(1)
    total = tn(left[0][...], right[0][...])
    for a, b in zip(left[1:], right[1:]):
        total = total + tn(a[...], b[...])
    low = total.astype(BF)

    @pl.when((pl.program_id(0) == 0) & (which == 0))
    def _():
        dot[...] = jnp.zeros_like(dot)

    dot[...] += jnp.sum(low.astype(F32) * rows[...].astype(F32), 0, keepdims=True)

    @pl.when(which == 0)
    def _():
        keep[0] = low

    @pl.when(which == 1)
    def _():
        give[0] = low


def parts(core, left, right, rows, own):
    tok = right[0].shape[1]
    n = len(left)
    chips = left[0].shape[1] // (2 * own)
    block = lambda c, w, core: c * 2 + (core[0] ^ w)
    S = jax.ShapeDtypeStruct
    spec = pltpu.PrefetchScalarGridSpec(
        num_scalar_prefetch=1, grid=(chips, 2),
        in_specs=[pl.BlockSpec((v.shape[0], own), lambda c, w, core: (0, block(c, w, core))) for v in left]
        + [pl.BlockSpec(v.shape, lambda c, w, core: (0, 0)) for v in right]
        + [pl.BlockSpec((own, tok), lambda c, w, core: (block(c, w, core), 0))],
        out_specs=[pl.BlockSpec((1, own, tok), lambda c, w, core: (c, 0, 0))] * 2
        + [pl.BlockSpec((1, tok), lambda c, w, core: (0, 0))])
    return pl.pallas_call(
        functools.partial(parts_kernel, n), grid_spec=spec,
        out_shape=[S((chips, own, tok), BF)] * 2 + [S((1, tok), F32)],
        compiler_params=wide_params(32), name="parts",
        cost_estimate=pl.CostEstimate(flops=10**10, bytes_accessed=10**7, transcendentals=0))(core, *left, *right, rows)


from jax.sharding import PartitionSpec as P


def col_sum(x):
    return jnp.sum(x, 0, keepdims=True)


def gelu_tanh(values):
    return jax.nn.gelu(values, approximate=True)


def layout(seq_lens, row_count):
    padded = (seq_lens + MB - 1) // MB * MB
    starts = jnp.cumsum(padded) - padded
    positions = jnp.arange(row_count, dtype=jnp.int32)
    inside = (positions[None, :] >= starts[:, None]) & (positions[None, :] < (starts + seq_lens)[:, None])
    valid_rows = jnp.any(inside, axis=0).astype(F32)
    block_first = jnp.arange(row_count // MB, dtype=jnp.int32) * MB
    begins = jnp.any((starts[:, None] == block_first[None, :]) & (seq_lens[:, None] > 0), axis=0)
    return valid_rows, (begins | (block_first == 0)).astype(jnp.int32)


def tie(*values):
    return lax.optimization_barrier(values)


class Sum:
    def __init__(self, x):
        self.x = x
        self.half = self.air = self.sent = self.landed = None


class Belt:
    def __init__(self):
        self.line = lax.axis_size("dp") == 4
        at = lax.axis_index("dp")
        self.end = ((at == 0) | (at == 3)).astype(jnp.int32).reshape(1)
        self.outer = self.inner = None

    def load(self, job, back):
        if back is None:
            return job.x
        if job is None:
            return half_sum(back.half, back.air)
        return outgoing(self.end, job.x, back.half, back.air)

    def tick(self, x, *values):
        job = Sum(x) if x is not None else None
        if not self.line:
            return (job,) + tuple(tie(*values)) if values else (job,)
        airs = ([self.outer[2]] if self.outer else []) + ([self.inner.air] if self.inner else [])
        held = tie(*airs, *([x] if job else []), *values)
        if job:
            job.x = held[len(airs)]
        values = held[len(airs) + (1 if job else 0):]
        back, self.inner = self.inner, None
        if back:
            back.air = held[len(airs) - 1]
        if self.outer:
            sent, gone, _ = self.outer
            if gone:
                gone.landed = held[0]
            if sent:
                sent.half = half_sum(sent.x, held[0])
                sent.air = lax.ppermute(sent.half, "dp", [(1, 2), (2, 1)])
                self.inner = sent
        self.outer = None
        if job or back:
            load = self.load(job, back)
            self.outer = (job, back, lax.ppermute(load, "dp", [(0, 1), (1, 0), (2, 3), (3, 2)]))
            if back:
                back.sent = load
        return (job,) + tuple(values)

    def drain(self):
        while self.outer or self.inner:
            self.tick(None)

    def result(self, *jobs):
        if not self.line:
            return lax.psum(jnp.concatenate([job.x for job in jobs], 0), "dp").astype(F32)
        return finish(self.end, jobs)


def on_device(
    tokens, lengths, attn_gain, w_query, w_key, w_value, w_gate, w_rate, rate_bias,
    inner_weight, inner_bias, inner_gain, inner_shift, post_gain, post_shift, w_out,
    ffn_gain, w_hidden_gate, w_hidden_up, w_down, out_grad,
):
    tok = tokens.shape[1]
    own = tokens.shape[0]
    heads = inner_weight.shape[0]
    devs = lax.axis_size("head")
    width = own * devs
    belt = Belt()

    def gather(x):
        return lax.all_gather(x, "head", axis=0, tiled=True)

    def head_sum(v):
        if devs != 8:
            return lax.psum(v, "head")
        for bit in (1, 2, 4):
            v = v + lax.ppermute(v, "head", [(i, i ^ bit) for i in range(8)])
        return v

    valid, reset = layout(lengths, tok)
    vrow = valid[None, :]
    spots = piece_spots(own, devs)
    stacked = jnp.concatenate([w_query, w_key, w_value, w_gate, jnp.pad(w_rate.T, ((0, 16 - heads), (0, 0)))], 0)
    tok_pieces = Pieces(tokens, devs)
    gain_blocks = spread_gains(jnp.stack([attn_gain, post_gain, post_shift, ffn_gain], 1), devs)
    consts = [hold(v, *tok_pieces.direct).astype(F32) for v in (inner_weight, inner_bias, inner_gain, inner_shift)]
    consts = pack_consts(*consts)
    nin, q1, gains = rms_rows(tok_pieces.all, spots, gain_blocks, 0, tok, width)
    g_full = gather(hold(out_grad, q1))
    gate = nn(w_gate, nin).astype(BF)
    gates = gather(gate)
    nin_q = hold(nin, gate)
    q_t = nn(w_query, nin_q)
    k_t = nn(w_key, nin_q)
    v_t = nn(w_value, nin_q)
    logits = tn(w_rate, nin) + rate_bias.astype(F32)[:, None]
    sig = jax.nn.sigmoid(logits)
    masked = sig * vrow
    mixer_own, zt, zb, td, qa, ka, wt, rows = ttt_fwd(
        reset, q_t, k_t, v_t, masked * (1.0 / HD), vrow, consts)

    mixer_own, g_full = tie(mixer_own, g_full)
    mix_pieces = Pieces(mixer_own, devs)
    mix, mean3, r3 = moments_rows(mix_pieces.all, spots, tok, width)
    gain_cols = gains.astype(F32)
    mixed = (((mix.astype(F32) - mean3) * r3 * gain_cols[:, 1:2] + gain_cols[:, 2:3])
             * gelu_tanh(gates.astype(F32))).astype(BF)
    hidden = tokens.astype(F32) + nn(w_out, mixed)
    hidden_low = hidden.astype(BF)
    nmid, q2, _ = rms_rows(Pieces(hidden_low, devs).all, spots, gains, 3, tok, width)
    gate_val = nn(w_hidden_gate, nmid)
    up_val = nn(w_hidden_up, nmid)
    sg = jax.nn.sigmoid(gate_val)
    act = (gate_val * sg * up_val).astype(BF)

    def halves(x, other):
        cut = (x.shape[0] // 2 + 7) // 8 * 8
        return wgrad(x[:cut], other), wgrad(x[cut:], other)

    down = halves(act, g_full)
    here = lax.axis_index("head") + 1
    marks = lax.broadcasted_iota(jnp.int32, (1, tok), 1)
    rates = jnp.where(marks == 0, jnp.sum(masked), jnp.where(marks == here, jnp.max(masked), 0.0))
    d0, g_full, rates = belt.tick(down[0], g_full, rates)
    g_act = nn(w_down, g_full)
    g_up = (g_act * gate_val * sg).astype(BF)
    g_gate = (g_act * up_val * sg * (1.0 + gate_val * (1.0 - sg))).astype(BF)
    gn = Scatter([w_hidden_gate, w_hidden_up], [g_gate, g_up], nmid, own, devs)
    d1, *gn.pair, gn.dot, rates, g_up, g_gate = belt.tick(down[1], *gn.pair, gn.dot, rates, g_up, g_gate)
    gn.spread()
    hgate = halves(g_gate, nmid)
    sums = head_sum(jnp.concatenate([gn.dot, rates], 0))
    mid_dot, rates = sums[:1], sums[1:]
    gn = gn.result()
    h0, gn, mid_dot, rates, g_up, h1_x = belt.tick(hgate[0], gn, mid_dot, rates, g_up, hgate[1])
    hid_own = hidden_low.astype(F32)
    fg_own = ffn_gain.astype(F32)[:, None]
    g_ffn_gain = jnp.sum(gn * hid_own * q2, 1)
    g_hidden = out_grad.astype(F32) + q2 * fg_own * gn - hid_own * q2**2 * mid_dot / width
    g_branch = g_hidden.astype(BF)
    gm = Scatter([w_out], [g_branch], mixed, own, devs)
    hup = halves(g_up, nmid)
    h1, *gm.pair, g_branch, u0_x = belt.tick(h1_x, *gm.pair, g_branch, hup[0])
    gm.spread()
    out_w = wgrad(g_branch, mixed)
    gm = gm.result()
    u0, gm, out_w, u1_x = belt.tick(u0_x, gm, out_w, hup[1])
    n3 = (mixer_own.astype(F32) - mean3) * r3
    pg_own = post_gain.astype(F32)[:, None]
    ps_own = post_shift.astype(F32)[:, None]
    a_own, gelu_pull = jax.vjp(gelu_tanh, gate.astype(F32))
    g_post_gain = jnp.sum(gm * a_own * n3, 1)
    g_post_shift = jnp.sum(gm * a_own, 1)
    g_gate_pre = gelu_pull(gm * (n3 * pg_own + ps_own))[0].astype(BF)
    m = gm * a_own * pg_own
    sums = head_sum(jnp.concatenate([col_sum(m), col_sum(m * n3)], 0))
    s_plain, s_norm = sums[:1], sums[1:]
    g_mixer = r3 * (m - s_plain / width - n3 * s_norm / width)
    u1, g_mixer, g_gate_pre, out_w = belt.tick(u1_x, g_mixer, g_gate_pre, out_w)
    gate_w = wgrad(g_gate_pre, nin)
    saved = (zt, zb, td, qa, ka, wt, rows, consts)
    b1 = ttt_bwd(1, 2, reset, g_mixer, *saved)
    so, lam, lam_c, gate_w = belt.tick(out_w, b1[8], b1[9], gate_w)
    b0 = ttt_bwd(0, 2, reset, g_mixer, *saved, carry=(lam, lam_c) + tuple(b1[:3]))
    dq, dk, dv = b0[:3]
    de_rows = jnp.concatenate([b0[3], b1[3]], 1)
    dgl, dsl, dw0, dc0 = [b0[i] + b1[i] for i in range(4, 8)]
    g_logits = de_rows * vrow * (1.0 / HD) * sig * (1.0 - sig)
    gl = g_logits.astype(BF)
    g_inner_w = dw0.reshape(HD, heads, HD).transpose(1, 2, 0)
    g_inner_b = dc0.reshape(HD, heads, MB)[:, :, 0].T
    g_inner_g = dgl.reshape(HD, heads, MB).sum(-1).T
    g_inner_s = dsl.reshape(HD, heads, MB).sum(-1).T
    wide_q, wide_k, wide_v = [wgrad(v, nin) for v in (dq, dk, dv)]
    wg, dq, dk, dv, gl, wide_q, wide_k, wide_v = belt.tick(gate_w, dq, dk, dv, gl, wide_q, wide_k, wide_v)
    tall = jnp.concatenate([dq, dk, dv, g_gate_pre, jnp.pad(gl, ((0, 16 - heads), (0, 0)))], 0)
    gi = Scatter([stacked], [tall], nin, own, devs)
    q, *gi.pair, gi.dot, act, wide_k = belt.tick(wide_q, *gi.pair, gi.dot, act, wide_k)
    gi.spread()
    in_dot = head_sum(gi.dot)
    gi = gi.result()
    g_wr = nt(gl, nin)
    ffn_part = tn(w_down, act).astype(BF)
    ffn = lax.psum_scatter(ffn_part, "head", scatter_dimension=0, tiled=True)
    result = (hidden + ffn.astype(F32)).astype(BF)
    k, gi, in_dot, g_wr = belt.tick(wide_k, gi, in_dot, g_wr)
    x_own = tokens.astype(F32)
    ag_own = attn_gain.astype(F32)[:, None]
    g_attn_gain = jnp.sum(gi * x_own * q1, 1)
    g_tokens = g_hidden + q1 * ag_own * gi - x_own * q1**2 * in_dot / width
    top = jnp.max(jnp.where(marks > 0, rates, 0.0))
    both = jnp.stack([rates[0, 0], top])
    cut = []
    for _ in range(3):
        cut.append(lax.reduce_precision(both, 8, 7))
        both = both - cut[-1]
    dps = lax.axis_size("dp")
    slot = (jnp.arange(dps) == lax.axis_index("dp")).astype(F32)
    slots = (slot[:, None, None] * jnp.stack(cut)[None]).reshape(-1)
    vectors = [g_attn_gain, g_post_gain, g_post_shift, g_ffn_gain, g_inner_b, g_inner_g, g_inner_s,
               jnp.sum(g_logits, 1), slots]
    vectors = [jnp.pad(u.reshape(-1), (0, own - u.size)) for u in vectors]
    small = jnp.concatenate([u.astype(BF).reshape(-1) for u in vectors + [g_inner_w, g_wr]])
    count = small.shape[0]
    small = jnp.pad(small, (0, -count % (16 * width))).reshape(-1, width)
    v, = belt.tick(jnp.concatenate([wide_v, small], 0))
    belt.drain()
    s_wv = belt.result(v)
    s_wv, small = s_wv[:own], s_wv[own:].reshape(-1)
    s_attn, s_pg, s_ps, s_fg, s_ib, s_ig, s_is, s_rb, slots = [small[i * own:(i + 1) * own] for i in range(9)]
    s_ib, s_ig, s_is = [v.reshape(heads, HD) for v in (s_ib, s_ig, s_is)]
    s_rb = s_rb[:heads]
    wide = 9 * own + heads * HD * HD
    s_iw = small[9 * own:wide].reshape(heads, HD, HD)
    s_wr = small[wide:count].reshape(heads, width)
    slots = jnp.sum(slots[:dps * 6].reshape(dps, 3, 2), 1)
    mean_rate = jnp.sum(slots[:, 0]) / (tok * dps * heads * devs)
    max_rate = jnp.max(slots[:, 1])

    return (
        result, g_tokens, s_attn, belt.result(q), belt.result(k), s_wv, belt.result(wg),
        s_wr.T, s_rb, s_iw, s_ib, s_ig, s_is, s_pg, s_ps, belt.result(so),
        s_fg, belt.result(h0, h1), belt.result(u0, u1), belt.result(d0, d1), mean_rate, max_rate,
    )


def solution(mesh):
    h = P("head")
    m = P("head", None)
    c = P("head", None, None)
    t = P("head", "dp")
    r = P(None, "head")
    ins = (t, P("dp"), h, m, m, m, m, r, h, c, m, m, m, h, h, m, h, m, m, m, t)
    outs = (t, t, h, m, m, m, m, r, h, c, m, m, m, h, h, m, h, m, m, m, P(), P())
    return jax.shard_map(on_device, mesh=mesh, in_specs=ins, out_specs=outs, check_vma=False)
```

```python
import jax, jax.numpy as jnp
from jax import lax
from jax.experimental import pallas as pl
from jax.experimental.pallas import tpu as pltpu
import functools
HD=64; MB=16; EPS=1e-6
F32=jnp.float32; BF=jnp.bfloat16

def nn(a,b): return lax.dot_general(a,b,(((1,),(0,)),((),())),preferred_element_type=F32)
def nt(a,b): return lax.dot_general(a,b,(((1,),(1,)),((),())),preferred_element_type=F32)
def tn(a,b): return lax.dot_general(a,b,(((0,),(0,)),((),())),preferred_element_type=F32)

def avg(x): return jnp.sum(x,0,keepdims=True)*(1.0/HD)

def lane_heads(heads, rows):
    return lax.broadcasted_iota(jnp.int32,(rows,heads*MB),1)//MB

def spread(x, heads):
    ids=lane_heads(heads,HD)
    return jnp.concatenate([jnp.where(ids==h,x,jnp.zeros_like(x)) for h in range(heads)],0)

def gather_blocks(x, heads):
    ids=lane_heads(heads,HD)
    out=jnp.zeros((HD,heads*MB),F32)
    for h in range(heads):
        out=out+jnp.where(ids==h,x[h*HD:(h+1)*HD],0.0)
    return out

def split_heads(ref, group, heads):
    cols=[ref[h*HD:(h+1)*HD, pl.ds(pl.multiple_of(group*128,128),128)] for h in range(heads)]
    return [jnp.concatenate([c[:,p*MB:(p+1)*MB] for c in cols],1) for p in range(8)]

def merge_heads(ref, group, parts, heads):
    for h in range(heads):
        blk=jnp.concatenate([p[:,h*MB:(h+1)*MB] for p in parts],1)
        ref[h*HD:(h+1)*HD, pl.ds(pl.multiple_of(group*128,128),128)]=blk.astype(ref.dtype)

def padded(x):
    rows=lax.broadcasted_iota(jnp.int32,(MB,x.shape[1]),0)
    return jnp.concatenate([x,jnp.where(rows==0,1.0,0.0).astype(F32)],0)

def same_head(heads):
    L=heads*MB
    r=lax.broadcasted_iota(jnp.int32,(L,L),0); c=lax.broadcasted_iota(jnp.int32,(L,L),1)
    return r//MB==c//MB, r%MB, c%MB

def step_grad(zt, td, g, s):
    mu=avg(zt); cen=zt-mu
    r=lax.rsqrt(avg(cen*cen)+EPS)
    n=cen*r
    v=n*g+s-td
    u=v*g
    m1=avg(u); m2=avg(u*n)
    return r,n,v,u,m2,r*(u-m1-n*m2)

def fwd_kernel(heads, nb, reset, qT, kT, vT, rate, valid, consts,
               outT, zt_o, zb_o, td_o, qa_o, ka_o, wt_o, rows, mp, q32):
    L=heads*MB
    same,ri,ci_=same_head(heads)
    tri=jnp.where(same&(ri<=ci_), 16.0/(ci_.astype(F32)+1.0), 0.0)
    diag=jnp.where(same,1.0,0.0)
    def pre(gr,_):
        qs=split_heads(qT,gr,heads); ks=split_heads(kT,gr,heads); vs=split_heads(vT,gr,heads)
        at=pl.ds(pl.multiple_of(gr*128,128),128)
        rt=rate[:,at]; vl=valid[:,at]
        for p in range(8):
            b=gr*8+p
            cut=slice(p*MB,(p+1)*MB)
            rows[b]=jnp.concatenate([jnp.concatenate([rt[h:h+1,cut] for h in range(heads)],1),
                                     jnp.concatenate([vl[:,cut]]*heads,1)],0)
            td_o[b]=vs[p]-ks[p]
            q32[b]=qs[p]
            qa_o[b]=padded(qs[p]).astype(BF)
            ka_o[b]=padded(ks[p]).astype(BF)
        return 0
    lax.fori_loop(0,nb//8,pre,0)
    def pre2(b,_):
        nxt=jnp.minimum(b+1,nb-1)
        ke=(ka_o[b].astype(F32)*(rows[b,0:1]*(1.0/MB))).astype(BF)
        keep=jnp.where(reset[nxt]>0,0.0,1.0)
        m=tn(ke,ka_o[nxt])*(diag*keep)
        pt=tn(ke,qa_o[b])*tri
        mp[b]=jnp.concatenate([m,pt],1).astype(BF)
        return 0
    lax.fori_loop(0,nb,pre2,0,unroll=4)
    w0,c0,g,s=unpack_consts(consts,heads)
    def body(b,carry):
        zt,wt,ct=carry
        nxt=jnp.minimum(b+1,nb-1)
        rs=reset[nxt]>0
        wt_b=wt.astype(BF)
        wt_o[b]=wt_b; zt_o[b]=zt
        r,n,v,u,m2,gt=step_grad(zt,td_o[b],g,s)
        gb=gt.astype(BF)
        kn=spread(ka_o[nxt][:HD],heads)
        wsel=jnp.where(rs,w0,wt).astype(BF)
        csel=jnp.where(rs,c0,ct)
        yk=nn(wsel,kn)+csel
        yq=nn(wt_b,spread(qa_o[b][:HD],heads))+ct
        rr=nn(gb,mp[b])
        e16=rows[b,0:1]*(1.0/MB)
        ke=(ka_o[b][:HD].astype(F32)*e16).astype(BF)
        rw=nt(gb,spread(ke,heads))
        ec=jnp.where(same,jnp.broadcast_to(e16,(L,L)),0.0).astype(BF)
        rc=nt(gb,ec)
        zb_o[b]=yq-rr[:,L:]
        z2=yk-rr[:,:L]
        return z2,jnp.where(rs,w0,wt-rw),jnp.where(rs,c0,ct-rc)
    zt=nn(w0.astype(BF),spread(ka_o[0][:HD],heads))+c0
    lax.fori_loop(0,nb,body,(zt,w0,c0))
    def post(gr,_):
        outs=[]
        for p in range(8):
            b=gr*8+p
            zb=zb_o[b]; cen=zb-avg(zb)
            n=cen*lax.rsqrt(avg(cen*cen)+EPS)
            outs.append((q32[b]+n*g+s)*rows[b,1:2])
        merge_heads(outT,gr,outs,heads)
        return 0
    lax.fori_loop(0,nb//8,post,0)

VM=pl.BlockSpec(memory_space=pltpu.VMEM)
SM=pl.BlockSpec(memory_space=pltpu.SMEM)
AN=pl.BlockSpec(memory_space=pl.ANY)

def pack_consts(w0, c0, g, s):
    heads=w0.shape[0]
    cols=[w0.transpose(2,0,1).reshape(HD,heads*HD)]+[lane_cols(v) for v in (c0,g,s)]
    return jnp.concatenate([jnp.pad(v,((0,0),(0,-v.shape[1]%128))) for v in cols],1)

def unpack_consts(ref, heads):
    wide=(heads*HD+127)//128*128; step=(heads*MB+127)//128*128
    return [ref[:,:heads*HD]]+[ref[:,wide+i*step:wide+i*step+heads*MB] for i in range(3)]

def ttt_fwd(reset, qT,kT,vT, rate, valid, consts):
    T=qT.shape[1]; heads=qT.shape[0]//HD; nb=T//MB; L=heads*MB; S=jax.ShapeDtypeStruct
    outs=[S((heads*HD,T),BF),S((nb,HD,L),F32),S((nb,HD,L),F32),S((nb,HD,L),F32),S((nb,HD+MB,L),BF),S((nb,HD+MB,L),BF),
          S((nb,HD,heads*HD),BF),S((nb,2,L),F32)]
    def whole(v): return pl.BlockSpec(v.shape,lambda i:(0,)*len(v.shape))
    args=[qT,kT,vT,rate,valid,consts]
    return pl.pallas_call(functools.partial(fwd_kernel,heads,nb),out_shape=outs,grid=(1,),
        in_specs=[SM]+[whole(v) for v in args],out_specs=[whole(v) for v in outs],
        scratch_shapes=[pltpu.VMEM((nb,L,2*L),BF),pltpu.VMEM((nb,HD,L),F32)],
        compiler_params=pltpu.CompilerParams(vmem_limit_bytes=44<<20), name="mix_forward",
        cost_estimate=pl.CostEstimate(flops=T*heads*64, bytes_accessed=T*heads, transcendentals=0))(
            reset,*args)

def bwd_kernel(heads, nb, base, last, reset, dOT, zt_i, zb_i, td_i, qa_i, ka_i, wt_i, rows, consts, *refs):
    if last:
        li=lci=None
    else:
        li,lci=refs[:2]; refs=refs[5:]
    (dqT, dkT, dvT, de_o, dg_o, ds_o, dw0_o, dc0_o, lo, lco,
               n_s, v_s, r_s, m2_s, gb_s, gh_s, nm_s, u_s, uc_s, dq_s, dk_s, du_s, dz_s, h_s, la_s, de_s)=refs
    L=heads*MB
    _,_,g,s=unpack_consts(consts,heads)
    same,ri,cj=same_head(heads)
    tri=jnp.where(same&(cj<=ri),1.0/(ri.astype(F32)+1.0),0.0)
    diag=jnp.where(same,1.0,0.0)
    diag_b=diag.astype(BF)
    dg_o[...]=jnp.zeros((HD,L),F32); ds_o[...]=jnp.zeros((HD,L),F32)
    dw0_o[...]=jnp.zeros_like(dw0_o); dc0_o[...]=jnp.zeros_like(dc0_o)
    def pre(gr,_):
        dos=split_heads(dOT,gr,heads)
        dga=jnp.zeros((HD,L),F32); dsa=jnp.zeros((HD,L),F32)
        for p in range(8):
            b=gr*8+p
            dO=dos[p].astype(F32)*rows[b,1:2]
            zb=zb_i[b]; cen=zb-avg(zb); rb=lax.rsqrt(avg(cen*cen)+EPS); nbar=cen*rb
            dga=dga+dO*nbar; dsa=dsa+dO
            dn=dO*g
            dzb=rb*(dn-avg(dn)-nbar*avg(dn*nbar))
            dzb_b=dzb.astype(BF)
            r,n,v,u,m2,gt=step_grad(zt_i[b],td_i[b],g,s)
            gb=gt.astype(BF)
            n_s[b]=n; v_s[b]=v; r_s[b]=r; m2_s[b]=m2; gb_s[b]=gt
            e=rows[b,0:1]
            ka=ka_i[b]; qa=qa_i[b]
            st=tn(qa,ka)*tri
            gh_s[b]=-nn(dzb_b,(st*e).astype(BF))
            dp=-tn(dzb_b,gb)
            de_s[b]=jnp.sum(dp*st,0,keepdims=True)
            dS=(dp*tri*e).astype(BF)
            dq_s[b]=dO+gather_blocks(tn(wt_i[b],dzb_b),heads)+nt(ka[:HD],dS)
            dk_s[b]=nn(qa[:HD],dS)
            prev=jnp.maximum(b-1,0)
            keep=jnp.where(reset[base+b]>0,0.0,1.0)
            nm_s[b]=(tn(ka,ka_i[prev])*(diag*keep)).astype(BF)
            u_s[b]=nt(dzb_b,spread(qa[:HD],heads))
            uc_s[b]=nn(dzb_b,diag_b)
        dg_o[...]+=dga; ds_o[...]+=dsa
        return 0
    lax.fori_loop(0,nb//8,pre,0)
    def body(k,carry):
        ht,la,lc=carry
        b=nb-1-k
        prev=jnp.maximum(b-1,0)
        rs=reset[base+b]>0
        n=n_s[b]; v=v_s[b]; r=r_s[b]; m2=m2_s[b]; gt=gb_s[b]
        h_s[b]=ht
        la_s[b]=la.astype(BF)
        dG=gh_s[b]-(rows[b,0:1]*(1.0/MB))*ht
        da=r*dG
        m3=avg(da); m4=avg(da*n); m6a=avg(dG*gt)
        du=da-m3-n*m4
        dn=(du*g-v*m4)*g-da*m2
        m5=avg(dn); m6=m6a+avg(dn*n)
        dz=(r*(dn-m5-n*m6)).astype(BF)
        du_s[b]=du
        dz_s[b]=dz
        la2=la+u_s[b]; lc2=lc+uc_s[b]
        y=nn(la2.astype(BF),spread(ka_i[prev][:HD],heads))+lc2
        h2=jnp.where(rs,0.0,y)+nn(dz,nm_s[b])
        la3=la2+nt(dz,spread(ka_i[b][:HD],heads)); lc3=lc2+nn(dz,diag_b)
        @pl.when(rs)
        def _():
            dw0_o[...]+=la3; dc0_o[...]+=lc3
        return h2,jnp.where(rs,0.0,la3),jnp.where(rs,0.0,lc3)
    la=jnp.zeros((HD,heads*HD),F32) if last else li[...]
    lc=jnp.zeros((HD,L),F32) if last else lci[...]
    ht=nn(la.astype(BF),spread(ka_i[nb-1][:HD],heads))+lc
    ht,la,lc=lax.fori_loop(0,nb,body,(ht,la,lc))
    lo[...]=la; lco[...]=lc
    def post(gr,_):
        dqs=[];dks=[];dvs=[];des=[]
        dga=jnp.zeros((HD,L),F32); dsa=jnp.zeros((HD,L),F32)
        for p in range(8):
            b=gr*8+p
            du=du_s[b]; dug=du*g; gt=gb_s[b]
            dga=dga+du*v_s[b]+dug*n_s[b]; dsa=dsa+dug
            dvs.append(-dug)
            dqs.append(dq_s[b])
            des.append(de_s[b]-avg(gt*h_s[b])*(HD/MB))
            dks.append(dug+dk_s[b]-(rows[b,0:1]*(1.0/MB))*gather_blocks(tn(la_s[b],gt.astype(BF)),heads)
                       +gather_blocks(tn(wt_i[b],dz_s[b]),heads))
        de_o[:,pl.ds(pl.multiple_of(gr*128,128),128)]=jnp.concatenate(
            [jnp.concatenate([d[:,h*MB:(h+1)*MB] for d in des],1) for h in range(heads)],0)
        merge_heads(dqT,gr,dqs,heads); merge_heads(dkT,gr,dks,heads); merge_heads(dvT,gr,dvs,heads)
        dg_o[...]+=dga; ds_o[...]+=dsa
        return 0
    lax.fori_loop(0,nb//8,post,0)

def ttt_bwd(part, parts, reset, dOT, zt,zb,td,qa,ka,wt,rows,consts, carry=None):
    T=dOT.shape[1]//parts; heads=dOT.shape[0]//HD; nb=T//MB; L=heads*MB; S=jax.ShapeDtypeStruct
    W=heads*HD; last=part==parts-1
    outs=[S((W,T*parts),BF)]*3+[S((heads,T),F32)]+[S((HD,L),F32)]*2+[S((HD,W),F32),S((HD,L),F32)]*2
    V=pltpu.VMEM
    scr=[V((nb,HD,L),F32),V((nb,HD,L),F32),V((nb,1,L),F32),V((nb,1,L),F32),V((nb,HD,L),F32),V((nb,HD,L),F32),
         V((nb,L,L),BF),V((nb,HD,W),F32),V((nb,HD,L),F32),V((nb,HD,L),F32),V((nb,HD,L),F32),V((nb,HD,L),F32),
         V((nb,HD,L),BF),V((nb,HD,L),F32),V((nb,HD,W),BF),V((nb,1,L),F32)]
    def whole(*dims): return pl.BlockSpec(dims,lambda i:(0,)*len(dims))
    def third(*dims): return pl.BlockSpec((nb,)+dims,lambda i:(part,)+(0,)*len(dims))
    nat=pl.BlockSpec((W,T),lambda i:(0,part))
    ins=[SM,nat]+[third(HD,L)]*3+[third(HD+MB,L)]*2+[third(HD,W),third(2,L),whole(*consts.shape)]
    args=[reset,dOT,zt,zb,td,qa,ka,wt,rows,consts]
    alias={}
    if not last:
        ins+=[whole(HD,W),whole(HD,L)]+[AN]*3
        alias={12:0,13:1,14:2}
        args+=list(carry)
    return pl.pallas_call(functools.partial(bwd_kernel,heads,nb,part*nb,last),out_shape=outs,grid=(1,),
        in_specs=ins,out_specs=[nat]*3+[whole(heads,T)]+[whole(HD,L)]*2+[whole(HD,W),whole(HD,L)]*2,
        scratch_shapes=scr,input_output_aliases=alias,
        compiler_params=pltpu.CompilerParams(vmem_limit_bytes=36<<20), name="mix_backward",
        cost_estimate=pl.CostEstimate(flops=T*heads*64, bytes_accessed=T*heads, transcendentals=0))(*args)

def lane_cols(x):
    return jnp.repeat(x.T,MB,axis=1)


ROWS = 64


def fetch(pieces, spots, buf, sems, f):
    copies = []
    for i, p in enumerate(pieces):
        at = pl.ds(pl.multiple_of(spots[i], 16), p.shape[0])
        copies.append(pltpu.make_async_copy(p, buf.at[at], sems.at[i]))
        copies[-1].start()
    acc = jnp.zeros((8, buf.shape[1]), F32)
    for i, c in enumerate(copies):
        c.wait()
        acc = fold(buf, spots[i], pieces[i].shape[0], f, acc)
    return jnp.sum(acc, 0, keepdims=True)


def fold(buf, first, rows, f, acc):
    def add(i, acc):
        v = f(buf[pl.ds(pl.multiple_of(first + i * ROWS, ROWS), ROWS), :].astype(F32))
        return acc + jnp.sum(v.reshape(ROWS // 8, 8, v.shape[1]), 0)

    return lax.fori_loop(0, rows // ROWS, add, acc)


def rms_kernel(n, lane, width, fresh, spots, blocks, *refs):
    pieces, (out, scale_out, gains, buf, sems, gain_sems) = refs[:n], refs[n:]
    if fresh:
        copies = []
        for i in range(blocks.shape[0]):
            at = pl.ds(pl.multiple_of(spots[i if i < 7 else 8], 16), blocks.shape[1])
            copies.append(pltpu.make_async_copy(blocks.at[i], gains.at[at], gain_sems.at[i]))
            copies[-1].start()
    scale = lax.rsqrt(fetch(pieces, spots, buf, sems, lambda v: v * v) * (1.0 / width) + EPS)
    if fresh:
        for c in copies:
            c.wait()
    scale_out[...] = scale
    source = gains if fresh else blocks

    def write(i, _):
        at = pl.ds(pl.multiple_of(i * ROWS, ROWS), ROWS)
        gain = source[at, lane:lane + 1].astype(F32)
        out[at, :] = (buf[at, :].astype(F32) * scale * gain).astype(BF)
        return 0

    lax.fori_loop(0, width // ROWS, write, 0)
    if not fresh:
        gains[...] = jnp.zeros_like(gains)


def moments_kernel(n, width, spots, *refs):
    pieces, (out, mean_out, scale_out, sems) = refs[:n], refs[n:]
    mean = fetch(pieces, spots, out, sems, lambda v: v) * (1.0 / width)
    mean_out[...] = mean
    acc = fold(out, 0, width, lambda v: (v - mean) * (v - mean), jnp.zeros((8, out.shape[1]), F32))
    scale_out[...] = lax.rsqrt(jnp.sum(acc, 0, keepdims=True) * (1.0 / width) + EPS)


def rms_rows(pieces, spots, gains, lane, tok, width):
    n = len(pieces)
    fresh = gains.ndim == 3
    count = gains.shape[0] if fresh else 1
    S = jax.ShapeDtypeStruct
    return pl.pallas_call(
        functools.partial(rms_kernel, n, lane, width, fresh),
        out_shape=[S((width, tok), BF), S((1, tok), F32), S((width, 128) if fresh else (16, 128), BF)],
        in_specs=[SM, AN if fresh else VM] + [AN] * n, out_specs=[VM, VM, VM],
        scratch_shapes=[pltpu.VMEM((width, tok), BF), pltpu.SemaphoreType.DMA((n,)), pltpu.SemaphoreType.DMA((count,))],
        compiler_params=pltpu.CompilerParams(vmem_limit_bytes=16 << 20), name="rms_rows",
        cost_estimate=pl.CostEstimate(flops=8 * width * tok, bytes_accessed=4 * width * tok, transcendentals=0),
    )(spots, gains, *pieces)


def moments_rows(pieces, spots, tok, width):
    n = len(pieces)
    return pl.pallas_call(
        functools.partial(moments_kernel, n, width),
        out_shape=[jax.ShapeDtypeStruct((width, tok), BF)] + [jax.ShapeDtypeStruct((1, tok), F32)] * 2,
        in_specs=[SM] + [AN] * n, out_specs=[VM] * 3,
        scratch_shapes=[pltpu.SemaphoreType.DMA((n,))],
        compiler_params=pltpu.CompilerParams(vmem_limit_bytes=16 << 20), name="moments_rows",
        cost_estimate=pl.CostEstimate(flops=8 * width * tok, bytes_accessed=4 * width * tok, transcendentals=0),
    )(spots, *pieces)


def hold(x, *deps):
    return lax.optimization_barrier((x,) + deps)[0]


class Pieces:
    def __init__(self, x, devs):
        if devs != 8:
            self.direct = self.diag = (x,)
            self.all = [lax.all_gather(x, "head", axis=0, tiled=True)]
            return
        rows = x.shape[0]

        def swap(v, bit):
            return lax.ppermute(v, "head", [(i, i ^ bit) for i in range(8)])

        along_x = swap(x, 2)
        along_y = swap(x, 4)
        peer = swap(x, 1)
        low = swap(along_x[:rows // 2], 4)
        high = swap(along_y[rows // 2:], 2)
        self.direct = (along_x, along_y)
        self.diag = (low, high)
        self.all = [x, peer, along_x, swap(along_x, 1), along_y, swap(along_y, 1), low, high, swap(low, 1), swap(high, 1)]


class Scatter:
    def __init__(self, left, right, rows, own, devs):
        self.own, self.devs = own, devs
        self.terms = None
        if devs != 8:
            total = sum(tn(a, b) for a, b in zip(left, right)).astype(BF)
            self.pair = (total, total[:16])
            self.dot = jnp.sum(total.astype(F32) * rows.astype(F32), 0, keepdims=True)
            return
        me = lax.axis_index("head")
        self.chip = me // 2
        keep, give, self.dot = parts((me % 2).reshape(1), left, right, rows, own)
        self.pair = (keep, give)

    def swap(self, v, bit):
        return lax.ppermute(v, "head", [(i, i ^ bit) for i in range(8)])

    def add(self, a, b):
        return (a.astype(F32) + b.astype(F32)).astype(BF)

    def spread(self):
        if self.devs != 8:
            return
        half = self.own // 2
        self.acc = self.add(self.pair[0], self.swap(self.pair[1], 1))
        far, to_x, to_y, home = [lax.dynamic_index_in_dim(self.acc, self.chip ^ k, 0, keepdims=False) for k in (3, 1, 2, 0)]
        low, high = self.swap(far[:half], 2), self.swap(far[half:], 4)
        x_low, y_high = self.swap(to_x[:half], 2), self.swap(to_y[half:], 4)
        x_high, y_low = self.swap(self.add(to_x[half:], high), 2), self.swap(self.add(to_y[:half], low), 4)
        self.terms = (home, (x_low, x_high), (y_low, y_high))

    def result(self):
        if self.devs != 8:
            return lax.psum_scatter(self.pair[0], "head", scatter_dimension=0, tiled=True).astype(F32)
        if self.terms is None:
            self.spread()
        home, *pairs = self.terms
        total = home.astype(F32)
        for pair in pairs:
            total = total + jnp.concatenate([v.astype(F32) for v in pair], 0)
        return total


def spread_gains(cols, devs):
    cols = jnp.pad(cols, ((0, 0), (0, 128 - cols.shape[1])))[None]
    if devs != 8:
        return lax.all_gather(cols, "head", axis=1, tiled=True)
    for bit in (1, 2, 4):
        cols = jnp.concatenate([cols, lax.ppermute(cols, "head", [(i, i ^ bit) for i in range(8)])], 0)
    return cols


def piece_spots(own, devs):
    if devs != 8:
        return jnp.zeros((1,), jnp.int32)
    me = lax.axis_index("head")
    half = own // 2
    places = [(0, 0), (1, 0), (2, 0), (3, 0), (4, 0), (5, 0), (6, 0), (6, half), (7, 0), (7, half)]
    return jnp.stack([(me ^ bits) * own + off for bits, off in places]).astype(jnp.int32)


FREE = pl.CostEstimate(flops=0, bytes_accessed=0, transcendentals=0)
COLS = 512


def wide_params(mib):
    return pltpu.CompilerParams(vmem_limit_bytes=mib << 20)


def wgrad_kernel(a, b, out):
    out[...] = nt(a[...], b[...]).astype(BF)


def wgrad(a, b):
    rows, tok = a.shape
    n = b.shape[0]
    return pl.pallas_call(
        wgrad_kernel, grid=(n // COLS,), out_shape=jax.ShapeDtypeStruct((rows, n), BF),
        in_specs=[pl.BlockSpec((rows, tok), lambda i: (0, 0)), pl.BlockSpec((COLS, tok), lambda i: (i, 0))],
        out_specs=pl.BlockSpec((rows, COLS), lambda i: (0, i)),
        compiler_params=wide_params(24), cost_estimate=FREE, name="weight_gradient")(a, b)


def column_blocks(v):
    return pl.BlockSpec((v.shape[0], COLS), lambda i: (0, i))


def turn_kernel(landed, job, back, end, *refs):
    refs = list(refs)
    ins = [refs.pop(0) for _ in range(2 * landed + job * back + 2 * back)]
    if landed:
        x, air = ins.pop(0), ins.pop(0)
        half = refs.pop(0)
        half[...] = (x[...].astype(F32) + air[:x.shape[0], :].astype(F32)).astype(BF)
    if back:
        out = refs.pop(0)

        def put(v):
            out[:v.shape[0], :] = v
            if v.shape[0] < out.shape[0]:
                out[v.shape[0]:, :] = jnp.zeros((out.shape[0] - v.shape[0], out.shape[1]), BF)

        half, air = ins[-2:]

        def total():
            put((half[...].astype(F32) + air[...].astype(F32)).astype(BF))

        if job:
            pl.when(end[0] > 0)(lambda: put(ins[0][...]))
            pl.when(end[0] == 0)(total)
        else:
            total()


def turn(end, sent, came, job, back):
    ins = ([sent.x, came] if sent else []) + ([job.x] if job and back else []) + ([back.half, back.air] if back else [])
    outs = []
    if sent:
        outs.append(jax.ShapeDtypeStruct(sent.x.shape, BF))
    if back:
        rows = max(job.x.shape[0] if job else 0, back.half.shape[0])
        outs.append(jax.ShapeDtypeStruct((rows, back.half.shape[1]), BF))
    res = []
    if outs:
        res = list(pl.pallas_call(
            functools.partial(turn_kernel, bool(sent), bool(job), bool(back)), grid=(outs[0].shape[1] // COLS,),
            out_shape=outs, in_specs=[SM] + [column_blocks(v) for v in ins], out_specs=[column_blocks(v) for v in outs],
            compiler_params=wide_params(24), cost_estimate=FREE, name="turn")(end, *ins))
    half = res.pop(0) if sent else None
    load = res.pop(0) if back else (job.x if job else None)
    return half, load


def finish_kernel(sizes, end, *refs):
    n = len(sizes)
    airs, sents, out = refs[:n], refs[n:2 * n], refs[2 * n]
    for chosen, kind in ((airs, 1), (sents, 0)):
        @pl.when(end[0] == kind)
        def _():
            at = 0
            for v, rows in zip(chosen, sizes):
                out[at:at + rows, :] = v[:rows, :].astype(F32)
                at += rows


def finish(end, jobs):
    sizes = [job.x.shape[0] for job in jobs]
    vals = [job.landed for job in jobs] + [job.sent for job in jobs]
    out = jax.ShapeDtypeStruct((sum(sizes), vals[0].shape[1]), F32)
    return pl.pallas_call(
        functools.partial(finish_kernel, sizes), grid=(out.shape[1] // COLS,), out_shape=out,
        in_specs=[SM] + [column_blocks(v) for v in vals], out_specs=column_blocks(out),
        compiler_params=wide_params(24), cost_estimate=FREE, name="finish")(end, *vals)


def parts_kernel(n, core, *refs):
    left, right, (rows, keep, give, dot) = refs[:n], refs[n:2 * n], refs[2 * n:]
    which = pl.program_id(1)
    total = tn(left[0][...], right[0][...])
    for a, b in zip(left[1:], right[1:]):
        total = total + tn(a[...], b[...])
    low = total.astype(BF)

    @pl.when((pl.program_id(0) == 0) & (which == 0))
    def _():
        dot[...] = jnp.zeros_like(dot)

    dot[...] += jnp.sum(low.astype(F32) * rows[...].astype(F32), 0, keepdims=True)

    @pl.when(which == 0)
    def _():
        keep[0] = low

    @pl.when(which == 1)
    def _():
        give[0] = low


def parts(core, left, right, rows, own):
    tok = right[0].shape[1]
    n = len(left)
    chips = left[0].shape[1] // (2 * own)
    block = lambda c, w, core: c * 2 + (core[0] ^ w)
    S = jax.ShapeDtypeStruct
    spec = pltpu.PrefetchScalarGridSpec(
        num_scalar_prefetch=1, grid=(chips, 2),
        in_specs=[pl.BlockSpec((v.shape[0], own), lambda c, w, core: (0, block(c, w, core))) for v in left]
        + [pl.BlockSpec(v.shape, lambda c, w, core: (0, 0)) for v in right]
        + [pl.BlockSpec((own, tok), lambda c, w, core: (block(c, w, core), 0))],
        out_specs=[pl.BlockSpec((1, own, tok), lambda c, w, core: (c, 0, 0))] * 2
        + [pl.BlockSpec((1, tok), lambda c, w, core: (0, 0))])
    return pl.pallas_call(
        functools.partial(parts_kernel, n), grid_spec=spec,
        out_shape=[S((chips, own, tok), BF)] * 2 + [S((1, tok), F32)],
        compiler_params=wide_params(32), name="parts",
        cost_estimate=pl.CostEstimate(flops=10**10, bytes_accessed=10**7, transcendentals=0))(core, *left, *right, rows)


from jax.sharding import PartitionSpec as P


def col_sum(x):
    return jnp.sum(x, 0, keepdims=True)


def gelu_tanh(values):
    return jax.nn.gelu(values, approximate=True)


def layout(seq_lens, row_count):
    padded = (seq_lens + MB - 1) // MB * MB
    starts = jnp.cumsum(padded) - padded
    positions = jnp.arange(row_count, dtype=jnp.int32)
    inside = (positions[None, :] >= starts[:, None]) & (positions[None, :] < (starts + seq_lens)[:, None])
    valid_rows = jnp.any(inside, axis=0).astype(F32)
    block_first = jnp.arange(row_count // MB, dtype=jnp.int32) * MB
    begins = jnp.any((starts[:, None] == block_first[None, :]) & (seq_lens[:, None] > 0), axis=0)
    return valid_rows, (begins | (block_first == 0)).astype(jnp.int32)


def tie(*values):
    return lax.optimization_barrier(values)


class Sum:
    def __init__(self, x):
        self.x = x
        self.half = self.air = self.sent = self.landed = None


class Belt:
    def __init__(self):
        self.line = lax.axis_size("dp") == 4
        at = lax.axis_index("dp")
        self.end = ((at == 0) | (at == 3)).astype(jnp.int32).reshape(1)
        self.outer = self.inner = None
        self.groups = []
        self.idle = False

    def tick(self, x, *values):
        job = Sum(x) if x is not None else None
        if not self.line:
            return (job,) + tuple(tie(*values)) if values else (job,)
        airs = ([self.outer[2]] if self.outer else []) + ([self.inner.air] if self.inner else [])
        done = []
        if self.idle:
            done = [g for g in self.groups if g.out is None and all(s.landed is not None for s in g.jobs)]
            for g in done:
                g.out = finish(self.end, g.jobs)
        held = tie(*airs, *([x] if job else []), *values, *[g.out for g in done])
        for g, out in zip(reversed(done), reversed(held)):
            g.out = out
        if job:
            job.x = held[len(airs)]
        values = held[len(airs) + (1 if job else 0):len(held) - len(done)]
        back, self.inner = self.inner, None
        if back:
            back.air = held[len(airs) - 1]
        sent, gone = self.outer[:2] if self.outer else (None, None)
        if gone:
            gone.landed = held[0]
        half, load = turn(self.end, sent, held[0], job, back)
        if sent:
            sent.half = half
            sent.air = lax.ppermute(half, "dp", [(1, 2), (2, 1)])
            self.inner = sent
        self.outer = None
        if load is not None:
            self.outer = (job, back, lax.ppermute(load, "dp", [(0, 1), (1, 0), (2, 3), (3, 2)]))
            if back:
                back.sent = load
        loads = [v for v in (half, load) if v is not None]
        if values and loads:
            values = tie(*values, *loads)[:len(values)]
        return (job,) + tuple(values)

    def drain(self):
        self.idle = True
        while self.outer or self.inner:
            self.tick(None)

    def group(self, *jobs):
        self.groups.append(Group(jobs))
        return self.groups[-1]

    def result(self, group):
        if not self.line:
            return lax.psum(jnp.concatenate([s.x for s in group.jobs], 0), "dp").astype(F32)
        return finish(self.end, group.jobs) if group.out is None else group.out


class Group:
    def __init__(self, jobs):
        self.jobs = jobs
        self.out = None


def on_device(
    tokens, lengths, attn_gain, w_query, w_key, w_value, w_gate, w_rate, rate_bias,
    inner_weight, inner_bias, inner_gain, inner_shift, post_gain, post_shift, w_out,
    ffn_gain, w_hidden_gate, w_hidden_up, w_down, out_grad,
):
    tok = tokens.shape[1]
    own = tokens.shape[0]
    heads = inner_weight.shape[0]
    devs = lax.axis_size("head")
    width = own * devs
    belt = Belt()

    def gather(x):
        return lax.all_gather(x, "head", axis=0, tiled=True)

    def head_sum(v):
        if devs != 8:
            return lax.psum(v, "head")
        for bit in (1, 2, 4):
            v = v + lax.ppermute(v, "head", [(i, i ^ bit) for i in range(8)])
        return v

    valid, reset = layout(lengths, tok)
    vrow = valid[None, :]
    spots = piece_spots(own, devs)
    stacked = jnp.concatenate([w_query, w_key, w_value, w_gate, jnp.pad(w_rate.T, ((0, 16 - heads), (0, 0)))], 0)
    tok_pieces = Pieces(tokens, devs)
    gain_blocks = spread_gains(jnp.stack([attn_gain, post_gain, post_shift, ffn_gain], 1), devs)
    consts = [hold(v, *tok_pieces.direct).astype(F32) for v in (inner_weight, inner_bias, inner_gain, inner_shift)]
    consts = pack_consts(*consts)
    g_full = gather(hold(out_grad, gain_blocks, *tok_pieces.diag))
    nin, q1, gains = rms_rows(tok_pieces.all, spots, gain_blocks, 0, tok, width)
    gate = nn(w_gate, nin).astype(BF)
    gelu_own = gelu_tanh(gate.astype(F32))
    gates = gather(gelu_own.astype(BF))
    nin_q = hold(nin, gate)
    q_t = nn(w_query, nin_q)
    k_t = nn(w_key, nin_q)
    v_t = nn(w_value, nin_q)
    logits = tn(w_rate, nin) + rate_bias.astype(F32)[:, None]
    sig = jax.nn.sigmoid(logits)
    masked = sig * vrow
    mixer_own, zt, zb, td, qa, ka, wt, rows = ttt_fwd(
        reset, q_t, k_t, v_t, masked * (1.0 / HD), vrow, consts)

    mixer_own, g_full = tie(mixer_own, g_full)
    mix_pieces = Pieces(mixer_own, devs)
    mix, mean3, r3 = moments_rows(mix_pieces.all, spots, tok, width)
    gain_cols = gains.astype(F32)
    mixed = (((mix.astype(F32) - mean3) * r3 * gain_cols[:, 1:2] + gain_cols[:, 2:3])
             * gates.astype(F32)).astype(BF)
    hidden = tokens.astype(F32) + nn(w_out, mixed)
    hidden_low = hidden.astype(BF)
    nmid, q2, _ = rms_rows(Pieces(hidden_low, devs).all, spots, gains, 3, tok, width)
    gate_val = nn(w_hidden_gate, nmid)
    up_val = nn(w_hidden_up, nmid)
    sg = jax.nn.sigmoid(gate_val)
    act = (gate_val * sg * up_val).astype(BF)

    def halves(x, other):
        cut = (x.shape[0] // 2 + 7) // 8 * 8
        return wgrad(x[:cut], other), wgrad(x[cut:], other)

    down = halves(act, g_full)
    here = lax.axis_index("head") + 1
    marks = lax.broadcasted_iota(jnp.int32, (1, tok), 1)
    rates = jnp.where(marks == 0, jnp.sum(masked), jnp.where(marks == here, jnp.max(masked), 0.0))
    d0, g_full, rates = belt.tick(down[0], g_full, rates)
    g_act = nn(w_down, g_full)
    g_up = (g_act * gate_val * sg).astype(BF)
    g_gate = (g_act * up_val * sg * (1.0 + gate_val * (1.0 - sg))).astype(BF)
    gn = Scatter([w_hidden_gate, w_hidden_up], [g_gate, g_up], nmid, own, devs)
    d1, *gn.pair, gn.dot, rates, g_up, g_gate = belt.tick(down[1], *gn.pair, gn.dot, rates, g_up, g_gate)
    gn.spread()
    hgate = halves(g_gate, nmid)
    sums = head_sum(jnp.concatenate([gn.dot, rates], 0))
    mid_dot, rates = sums[:1], sums[1:]
    gn = gn.result()
    h0, gn, mid_dot, rates, g_up, h1_x = belt.tick(hgate[0], gn, mid_dot, rates, g_up, hgate[1])
    hid_own = hidden_low.astype(F32)
    fg_own = ffn_gain.astype(F32)[:, None]
    g_ffn_gain = jnp.sum(gn * hid_own * q2, 1)
    g_hidden = out_grad.astype(F32) + q2 * fg_own * gn - hid_own * q2**2 * mid_dot / width
    g_branch = g_hidden.astype(BF)
    gm = Scatter([w_out], [g_branch], mixed, own, devs)
    hup = halves(g_up, nmid)
    h1, *gm.pair, g_branch, u0_x = belt.tick(h1_x, *gm.pair, g_branch, hup[0])
    gm.spread()
    out_w = wgrad(g_branch, mixed)
    gm = gm.result()
    u0, gm, out_w, u1_x, act = belt.tick(u0_x, gm, out_w, hup[1], act)
    ffn_part = tn(w_down, act).astype(BF)
    n3 = (mixer_own.astype(F32) - mean3) * r3
    pg_own = post_gain.astype(F32)[:, None]
    ps_own = post_shift.astype(F32)[:, None]
    a_own, gelu_pull = jax.vjp(gelu_tanh, gate.astype(F32))
    g_post_gain = jnp.sum(gm * a_own * n3, 1)
    g_post_shift = jnp.sum(gm * a_own, 1)
    g_gate_pre = gelu_pull(gm * (n3 * pg_own + ps_own))[0].astype(BF)
    m = gm * a_own * pg_own
    sums = head_sum(jnp.concatenate([col_sum(m), col_sum(m * n3)], 0))
    s_plain, s_norm = sums[:1], sums[1:]
    g_mixer = r3 * (m - s_plain / width - n3 * s_norm / width)
    u1, g_mixer, g_gate_pre, out_w, ffn_part = belt.tick(u1_x, g_mixer, g_gate_pre, out_w, ffn_part)
    ffn = lax.psum_scatter(ffn_part, "head", scatter_dimension=0, tiled=True)
    gate_w = wgrad(g_gate_pre, nin)
    saved = (zt, zb, td, qa, ka, wt, rows, consts)
    b1 = ttt_bwd(1, 2, reset, g_mixer, *saved)
    so, lam, lam_c, gate_w = belt.tick(out_w, b1[8], b1[9], gate_w)
    b0 = ttt_bwd(0, 2, reset, g_mixer, *saved, carry=(lam, lam_c) + tuple(b1[:3]))
    dq, dk, dv = b0[:3]
    de_rows = jnp.concatenate([b0[3], b1[3]], 1)
    dgl, dsl, dw0, dc0 = [b0[i] + b1[i] for i in range(4, 8)]
    g_logits = de_rows * vrow * (1.0 / HD) * sig * (1.0 - sig)
    gl = g_logits.astype(BF)
    g_inner_w = dw0.reshape(HD, heads, HD).transpose(1, 2, 0)
    g_inner_b = dc0.reshape(HD, heads, MB)[:, :, 0].T
    g_inner_g = dgl.reshape(HD, heads, MB).sum(-1).T
    g_inner_s = dsl.reshape(HD, heads, MB).sum(-1).T
    wide_q, wide_k, wide_v = [wgrad(v, nin) for v in (dq, dk, dv)]
    wg, dq, dk, dv, gl, wide_q, wide_k, wide_v, ffn = belt.tick(
        gate_w, dq, dk, dv, gl, wide_q, wide_k, wide_v, ffn)
    result = (hidden + ffn.astype(F32)).astype(BF)
    tall = jnp.concatenate([dq, dk, dv, g_gate_pre, jnp.pad(gl, ((0, 16 - heads), (0, 0)))], 0)
    gi = Scatter([stacked], [tall], nin, own, devs)
    q, *gi.pair, gi.dot, wide_k = belt.tick(wide_q, *gi.pair, gi.dot, wide_k)
    gi.spread()
    in_dot = head_sum(gi.dot)
    gi = gi.result()
    g_wr = nt(gl, nin)
    k, gi, in_dot, g_wr = belt.tick(wide_k, gi, in_dot, g_wr)
    x_own = tokens.astype(F32)
    ag_own = attn_gain.astype(F32)[:, None]
    g_attn_gain = jnp.sum(gi * x_own * q1, 1)
    g_tokens = g_hidden + q1 * ag_own * gi - x_own * q1**2 * in_dot / width
    top = jnp.max(jnp.where(marks > 0, rates, 0.0))
    both = jnp.stack([rates[0, 0], top])
    cut = []
    for _ in range(3):
        cut.append(lax.reduce_precision(both, 8, 7))
        both = both - cut[-1]
    dps = lax.axis_size("dp")
    slot = (jnp.arange(dps) == lax.axis_index("dp")).astype(F32)
    slots = (slot[:, None, None] * jnp.stack(cut)[None]).reshape(-1)
    vectors = [g_attn_gain, g_post_gain, g_post_shift, g_ffn_gain, g_inner_b, g_inner_g, g_inner_s,
               jnp.sum(g_logits, 1), slots]
    vectors = [jnp.pad(u.reshape(-1), (0, own - u.size)) for u in vectors]
    small = jnp.concatenate([u.astype(BF).reshape(-1) for u in vectors + [g_inner_w, g_wr]])
    count = small.shape[0]
    small = jnp.pad(small, (0, -count % (16 * width))).reshape(-1, width)
    v, = belt.tick(jnp.concatenate([wide_v, small], 0))
    sums = [belt.group(*jobs) for jobs in ((d0, d1), (h0, h1), (u0, u1), (so,), (wg,), (q,), (k,), (v,))]
    belt.drain()
    s_down, s_hgate, s_hup, s_out, s_wg, s_wq, s_wk, s_wv = [belt.result(g) for g in sums]
    s_wv, small = s_wv[:own], s_wv[own:].reshape(-1)
    s_attn, s_pg, s_ps, s_fg, s_ib, s_ig, s_is, s_rb, slots = [small[i * own:(i + 1) * own] for i in range(9)]
    s_ib, s_ig, s_is = [v.reshape(heads, HD) for v in (s_ib, s_ig, s_is)]
    s_rb = s_rb[:heads]
    wide = 9 * own + heads * HD * HD
    s_iw = small[9 * own:wide].reshape(heads, HD, HD)
    s_wr = small[wide:count].reshape(heads, width)
    slots = jnp.sum(slots[:dps * 6].reshape(dps, 3, 2), 1)
    mean_rate = jnp.sum(slots[:, 0]) / (tok * dps * heads * devs)
    max_rate = jnp.max(slots[:, 1])

    return (
        result, g_tokens, s_attn, s_wq, s_wk, s_wv, s_wg,
        s_wr.T, s_rb, s_iw, s_ib, s_ig, s_is, s_pg, s_ps, s_out,
        s_fg, s_hgate, s_hup, s_down, mean_rate, max_rate,
    )


def solution(mesh):
    h = P("head")
    m = P("head", None)
    c = P("head", None, None)
    t = P("head", "dp")
    r = P(None, "head")
    ins = (t, P("dp"), h, m, m, m, m, r, h, c, m, m, m, h, h, m, h, m, m, m, t)
    outs = (t, t, h, m, m, m, m, r, h, c, m, m, m, h, h, m, h, m, m, m, P(), P())
    return jax.shard_map(on_device, mesh=mesh, in_specs=ins, out_specs=outs, check_vma=False)
```

```python
import jax, jax.numpy as jnp
from jax import lax
from jax.experimental import pallas as pl
from jax.experimental.pallas import tpu as pltpu
import functools
HD=64; MB=16; EPS=1e-6
F32=jnp.float32; BF=jnp.bfloat16

def nn(a,b): return lax.dot_general(a,b,(((1,),(0,)),((),())),preferred_element_type=F32)
def nt(a,b): return lax.dot_general(a,b,(((1,),(1,)),((),())),preferred_element_type=F32)
def tn(a,b): return lax.dot_general(a,b,(((0,),(0,)),((),())),preferred_element_type=F32)

def avg(x): return jnp.sum(x,0,keepdims=True)*(1.0/HD)

def lane_heads(heads, rows):
    return lax.broadcasted_iota(jnp.int32,(rows,heads*MB),1)//MB

def spread(x, heads):
    ids=lane_heads(heads,HD)
    return jnp.concatenate([jnp.where(ids==h,x,jnp.zeros_like(x)) for h in range(heads)],0)

def gather_blocks(x, heads):
    ids=lane_heads(heads,HD)
    out=jnp.zeros((HD,heads*MB),F32)
    for h in range(heads):
        out=out+jnp.where(ids==h,x[h*HD:(h+1)*HD],0.0)
    return out

def split_heads(ref, group, heads):
    cols=[ref[h*HD:(h+1)*HD, pl.ds(pl.multiple_of(group*128,128),128)] for h in range(heads)]
    return [jnp.concatenate([c[:,p*MB:(p+1)*MB] for c in cols],1) for p in range(8)]

def merge_heads(ref, group, parts, heads):
    for h in range(heads):
        blk=jnp.concatenate([p[:,h*MB:(h+1)*MB] for p in parts],1)
        ref[h*HD:(h+1)*HD, pl.ds(pl.multiple_of(group*128,128),128)]=blk.astype(ref.dtype)

def padded(x):
    rows=lax.broadcasted_iota(jnp.int32,(MB,x.shape[1]),0)
    return jnp.concatenate([x,jnp.where(rows==0,1.0,0.0).astype(F32)],0)

def same_head(heads):
    L=heads*MB
    r=lax.broadcasted_iota(jnp.int32,(L,L),0); c=lax.broadcasted_iota(jnp.int32,(L,L),1)
    return r//MB==c//MB, r%MB, c%MB

def step_grad(zt, td, g, s):
    mu=avg(zt); cen=zt-mu
    r=lax.rsqrt(avg(cen*cen)+EPS)
    n=cen*r
    v=n*g+s-td
    u=v*g
    m1=avg(u); m2=avg(u*n)
    return r,n,v,u,m2,r*(u-m1-n*m2)

def fwd_kernel(heads, nb, reset, qT, kT, vT, rate, valid, consts,
               outT, zt_o, zb_o, td_o, qa_o, ka_o, wt_o, rows, mp, q32):
    L=heads*MB
    same,ri,ci_=same_head(heads)
    tri=jnp.where(same&(ri<=ci_), 16.0/(ci_.astype(F32)+1.0), 0.0)
    diag=jnp.where(same,1.0,0.0)
    def pre(gr,_):
        qs=split_heads(qT,gr,heads); ks=split_heads(kT,gr,heads); vs=split_heads(vT,gr,heads)
        at=pl.ds(pl.multiple_of(gr*128,128),128)
        rt=rate[:,at]; vl=valid[:,at]
        for p in range(8):
            b=gr*8+p
            cut=slice(p*MB,(p+1)*MB)
            rows[b]=jnp.concatenate([jnp.concatenate([rt[h:h+1,cut] for h in range(heads)],1),
                                     jnp.concatenate([vl[:,cut]]*heads,1)],0)
            td_o[b]=vs[p]-ks[p]
            q32[b]=qs[p]
            qa_o[b]=padded(qs[p]).astype(BF)
            ka_o[b]=padded(ks[p]).astype(BF)
        return 0
    lax.fori_loop(0,nb//8,pre,0)
    def pre2(b,_):
        nxt=jnp.minimum(b+1,nb-1)
        ke=(ka_o[b].astype(F32)*(rows[b,0:1]*(1.0/MB))).astype(BF)
        keep=jnp.where(reset[nxt]>0,0.0,1.0)
        m=tn(ke,ka_o[nxt])*(diag*keep)
        pt=tn(ke,qa_o[b])*tri
        mp[b]=jnp.concatenate([m,pt],1).astype(BF)
        return 0
    lax.fori_loop(0,nb,pre2,0,unroll=8)
    w0,c0,g,s=unpack_consts(consts,heads)
    def body(b,carry):
        zt,wt,ct=carry
        nxt=jnp.minimum(b+1,nb-1)
        rs=reset[nxt]>0
        wt_b=wt.astype(BF)
        wt_o[b]=wt_b; zt_o[b]=zt
        r,n,v,u,m2,gt=step_grad(zt,td_o[b],g,s)
        gb=gt.astype(BF)
        kn=spread(ka_o[nxt][:HD],heads)
        wsel=jnp.where(rs,w0,wt).astype(BF)
        csel=jnp.where(rs,c0,ct)
        yk=nn(wsel,kn)+csel
        yq=nn(wt_b,spread(qa_o[b][:HD],heads))+ct
        rr=nn(gb,mp[b])
        e16=rows[b,0:1]*(1.0/MB)
        ke=(ka_o[b][:HD].astype(F32)*e16).astype(BF)
        rw=nt(gb,spread(ke,heads))
        ec=jnp.where(same,jnp.broadcast_to(e16,(L,L)),0.0).astype(BF)
        rc=nt(gb,ec)
        zb_o[b]=yq-rr[:,L:]
        z2=yk-rr[:,:L]
        return z2,jnp.where(rs,w0,wt-rw),jnp.where(rs,c0,ct-rc)
    zt=nn(w0.astype(BF),spread(ka_o[0][:HD],heads))+c0
    lax.fori_loop(0,nb,body,(zt,w0,c0),unroll=4)
    def post(gr,_):
        outs=[]
        for p in range(8):
            b=gr*8+p
            zb=zb_o[b]; cen=zb-avg(zb)
            n=cen*lax.rsqrt(avg(cen*cen)+EPS)
            outs.append((q32[b]+n*g+s)*rows[b,1:2])
        merge_heads(outT,gr,outs,heads)
        return 0
    lax.fori_loop(0,nb//8,post,0)

VM=pl.BlockSpec(memory_space=pltpu.VMEM)
SM=pl.BlockSpec(memory_space=pltpu.SMEM)
AN=pl.BlockSpec(memory_space=pl.ANY)

def pack_consts(w0, c0, g, s):
    heads=w0.shape[0]
    cols=[w0.transpose(2,0,1).reshape(HD,heads*HD)]+[lane_cols(v) for v in (c0,g,s)]
    return jnp.concatenate([jnp.pad(v,((0,0),(0,-v.shape[1]%128))) for v in cols],1)

def unpack_consts(ref, heads):
    wide=(heads*HD+127)//128*128; step=(heads*MB+127)//128*128
    return [ref[:,:heads*HD]]+[ref[:,wide+i*step:wide+i*step+heads*MB] for i in range(3)]

def ttt_fwd(reset, qT,kT,vT, rate, valid, consts):
    T=qT.shape[1]; heads=qT.shape[0]//HD; nb=T//MB; L=heads*MB; S=jax.ShapeDtypeStruct
    outs=[S((heads*HD,T),BF),S((nb,HD,L),F32),S((nb,HD,L),F32),S((nb,HD,L),F32),S((nb,HD+MB,L),BF),S((nb,HD+MB,L),BF),
          S((nb,HD,heads*HD),BF),S((nb,2,L),F32)]
    def whole(v): return pl.BlockSpec(v.shape,lambda i:(0,)*len(v.shape))
    args=[qT,kT,vT,rate,valid,consts]
    return pl.pallas_call(functools.partial(fwd_kernel,heads,nb),out_shape=outs,grid=(1,),
        in_specs=[SM]+[whole(v) for v in args],out_specs=[whole(v) for v in outs],
        scratch_shapes=[pltpu.VMEM((nb,L,2*L),BF),pltpu.VMEM((nb,HD,L),F32)],
        compiler_params=pltpu.CompilerParams(vmem_limit_bytes=34<<20), name="mix_forward",
        cost_estimate=pl.CostEstimate(flops=T*heads*64, bytes_accessed=T*heads, transcendentals=0))(
            reset,*args)

def bwd_kernel(heads, nb, base, last, reset, dOT, zt_i, zb_i, td_i, qa_i, ka_i, wt_i, rows, consts, *refs):
    if last:
        li=lci=None
    else:
        li,lci=refs[:2]; refs=refs[5:]
    (dqT, dkT, dvT, de_o, dg_o, ds_o, dw0_o, dc0_o, lo, lco,
               n_s, v_s, r_s, m2_s, gb_s, gh_s, nm_s, u_s, uc_s, dq_s, dk_s, du_s, dz_s, h_s, la_s, de_s)=refs
    L=heads*MB
    _,_,g,s=unpack_consts(consts,heads)
    same,ri,cj=same_head(heads)
    tri=jnp.where(same&(cj<=ri),1.0/(ri.astype(F32)+1.0),0.0)
    diag=jnp.where(same,1.0,0.0)
    diag_b=diag.astype(BF)
    dg_o[...]=jnp.zeros((HD,L),F32); ds_o[...]=jnp.zeros((HD,L),F32)
    dw0_o[...]=jnp.zeros_like(dw0_o); dc0_o[...]=jnp.zeros_like(dc0_o)
    def pre(gr,_):
        dos=split_heads(dOT,gr,heads)
        dga=jnp.zeros((HD,L),F32); dsa=jnp.zeros((HD,L),F32)
        for p in range(8):
            b=gr*8+p
            dO=dos[p].astype(F32)*rows[b,1:2]
            zb=zb_i[b]; cen=zb-avg(zb); rb=lax.rsqrt(avg(cen*cen)+EPS); nbar=cen*rb
            dga=dga+dO*nbar; dsa=dsa+dO
            dn=dO*g
            dzb=rb*(dn-avg(dn)-nbar*avg(dn*nbar))
            dzb_b=dzb.astype(BF)
            r,n,v,u,m2,gt=step_grad(zt_i[b],td_i[b],g,s)
            gb=gt.astype(BF)
            n_s[b]=n; v_s[b]=v; r_s[b]=r; m2_s[b]=m2; gb_s[b]=gt
            e=rows[b,0:1]
            ka=ka_i[b]; qa=qa_i[b]
            st=tn(qa,ka)*tri
            gh_s[b]=-nn(dzb_b,(st*e).astype(BF))
            dp=-tn(dzb_b,gb)
            de_s[b]=jnp.sum(dp*st,0,keepdims=True)
            dS=(dp*tri*e).astype(BF)
            dq_s[b]=dO+gather_blocks(tn(wt_i[b],dzb_b),heads)+nt(ka[:HD],dS)
            dk_s[b]=nn(qa[:HD],dS)
            prev=jnp.maximum(b-1,0)
            keep=jnp.where(reset[base+b]>0,0.0,1.0)
            nm_s[b]=(tn(ka,ka_i[prev])*(diag*keep)).astype(BF)
            u_s[b]=nt(dzb_b,spread(qa[:HD],heads))
            uc_s[b]=nn(dzb_b,diag_b)
        dg_o[...]+=dga; ds_o[...]+=dsa
        return 0
    lax.fori_loop(0,nb//8,pre,0)
    def body(k,carry):
        ht,la,lc=carry
        b=nb-1-k
        prev=jnp.maximum(b-1,0)
        rs=reset[base+b]>0
        n=n_s[b]; v=v_s[b]; r=r_s[b]; m2=m2_s[b]; gt=gb_s[b]
        h_s[b]=ht
        la_s[b]=la.astype(BF)
        dG=gh_s[b]-(rows[b,0:1]*(1.0/MB))*ht
        da=r*dG
        m3=avg(da); m4=avg(da*n); m6a=avg(dG*gt)
        du=da-m3-n*m4
        dn=(du*g-v*m4)*g-da*m2
        m5=avg(dn); m6=m6a+avg(dn*n)
        dz=(r*(dn-m5-n*m6)).astype(BF)
        du_s[b]=du
        dz_s[b]=dz
        la2=la+u_s[b]; lc2=lc+uc_s[b]
        y=nn(la2.astype(BF),spread(ka_i[prev][:HD],heads))+lc2
        h2=jnp.where(rs,0.0,y)+nn(dz,nm_s[b])
        la3=la2+nt(dz,spread(ka_i[b][:HD],heads)); lc3=lc2+nn(dz,diag_b)
        @pl.when(rs)
        def _():
            dw0_o[...]+=la3; dc0_o[...]+=lc3
        return h2,jnp.where(rs,0.0,la3),jnp.where(rs,0.0,lc3)
    la=jnp.zeros((HD,heads*HD),F32) if last else li[...]
    lc=jnp.zeros((HD,L),F32) if last else lci[...]
    ht=nn(la.astype(BF),spread(ka_i[nb-1][:HD],heads))+lc
    ht,la,lc=lax.fori_loop(0,nb,body,(ht,la,lc))
    lo[...]=la; lco[...]=lc
    def post(gr,_):
        dqs=[];dks=[];dvs=[];des=[]
        dga=jnp.zeros((HD,L),F32); dsa=jnp.zeros((HD,L),F32)
        for p in range(8):
            b=gr*8+p
            du=du_s[b]; dug=du*g; gt=gb_s[b]
            dga=dga+du*v_s[b]+dug*n_s[b]; dsa=dsa+dug
            dvs.append(-dug)
            dqs.append(dq_s[b])
            des.append(de_s[b]-avg(gt*h_s[b])*(HD/MB))
            dks.append(dug+dk_s[b]-(rows[b,0:1]*(1.0/MB))*gather_blocks(tn(la_s[b],gt.astype(BF)),heads)
                       +gather_blocks(tn(wt_i[b],dz_s[b]),heads))
        de_o[:,pl.ds(pl.multiple_of(gr*128,128),128)]=jnp.concatenate(
            [jnp.concatenate([d[:,h*MB:(h+1)*MB] for d in des],1) for h in range(heads)],0)
        merge_heads(dqT,gr,dqs,heads); merge_heads(dkT,gr,dks,heads); merge_heads(dvT,gr,dvs,heads)
        dg_o[...]+=dga; ds_o[...]+=dsa
        return 0
    lax.fori_loop(0,nb//8,post,0)

def ttt_bwd(part, parts, reset, dOT, zt,zb,td,qa,ka,wt,rows,consts, carry=None):
    T=dOT.shape[1]//parts; heads=dOT.shape[0]//HD; nb=T//MB; L=heads*MB; S=jax.ShapeDtypeStruct
    W=heads*HD; last=part==parts-1
    outs=[S((W,T*parts),BF)]*3+[S((heads,T),F32)]+[S((HD,L),F32)]*2+[S((HD,W),F32),S((HD,L),F32)]*2
    V=pltpu.VMEM
    scr=[V((nb,HD,L),F32),V((nb,HD,L),F32),V((nb,1,L),F32),V((nb,1,L),F32),V((nb,HD,L),F32),V((nb,HD,L),F32),
         V((nb,L,L),BF),V((nb,HD,W),F32),V((nb,HD,L),F32),V((nb,HD,L),F32),V((nb,HD,L),F32),V((nb,HD,L),F32),
         V((nb,HD,L),BF),V((nb,HD,L),F32),V((nb,HD,W),BF),V((nb,1,L),F32)]
    def whole(*dims): return pl.BlockSpec(dims,lambda i:(0,)*len(dims))
    def third(*dims): return pl.BlockSpec((nb,)+dims,lambda i:(part,)+(0,)*len(dims))
    nat=pl.BlockSpec((W,T),lambda i:(0,part))
    ins=[SM,nat]+[third(HD,L)]*3+[third(HD+MB,L)]*2+[third(HD,W),third(2,L),whole(*consts.shape)]
    args=[reset,dOT,zt,zb,td,qa,ka,wt,rows,consts]
    alias={}
    if not last:
        ins+=[whole(HD,W),whole(HD,L)]+[AN]*3
        alias={12:0,13:1,14:2}
        args+=list(carry)
    return pl.pallas_call(functools.partial(bwd_kernel,heads,nb,part*nb,last),out_shape=outs,grid=(1,),
        in_specs=ins,out_specs=[nat]*3+[whole(heads,T)]+[whole(HD,L)]*2+[whole(HD,W),whole(HD,L)]*2,
        scratch_shapes=scr,input_output_aliases=alias,
        compiler_params=pltpu.CompilerParams(vmem_limit_bytes=30<<20), name="mix_backward",
        cost_estimate=pl.CostEstimate(flops=T*heads*64, bytes_accessed=T*heads, transcendentals=0))(*args)

def lane_cols(x):
    return jnp.repeat(x.T,MB,axis=1)


ROWS = 64


def fetch(pieces, spots, buf, sems, f):
    copies = []
    for i, p in enumerate(pieces):
        at = pl.ds(pl.multiple_of(spots[i], 16), p.shape[0])
        copies.append(pltpu.make_async_copy(p, buf.at[at], sems.at[i]))
        copies[-1].start()
    acc = jnp.zeros((8, buf.shape[1]), F32)
    for i, c in enumerate(copies):
        c.wait()
        acc = fold(buf, spots[i], pieces[i].shape[0], f, acc)
    return jnp.sum(acc, 0, keepdims=True)


def fold(buf, first, rows, f, acc):
    def add(i, acc):
        v = f(buf[pl.ds(pl.multiple_of(first + i * ROWS, ROWS), ROWS), :].astype(F32))
        return acc + jnp.sum(v.reshape(ROWS // 8, 8, v.shape[1]), 0)

    return lax.fori_loop(0, rows // ROWS, add, acc)


def rms_kernel(n, lane, width, fresh, spots, blocks, *refs):
    pieces, (out, scale_out, gains, buf, sems, gain_sems) = refs[:n], refs[n:]
    if fresh:
        copies = []
        for i in range(blocks.shape[0]):
            at = pl.ds(pl.multiple_of(spots[i if i < 7 else 8], 16), blocks.shape[1])
            copies.append(pltpu.make_async_copy(blocks.at[i], gains.at[at], gain_sems.at[i]))
            copies[-1].start()
    scale = lax.rsqrt(fetch(pieces, spots, buf, sems, lambda v: v * v) * (1.0 / width) + EPS)
    if fresh:
        for c in copies:
            c.wait()
    scale_out[...] = scale
    source = gains if fresh else blocks

    def write(i, _):
        at = pl.ds(pl.multiple_of(i * ROWS, ROWS), ROWS)
        gain = source[at, lane:lane + 1].astype(F32)
        out[at, :] = (buf[at, :].astype(F32) * scale * gain).astype(BF)
        return 0

    lax.fori_loop(0, width // ROWS, write, 0)
    if not fresh:
        gains[...] = jnp.zeros_like(gains)


def collect_kernel(n, spots, *refs):
    pieces, (out, sems) = refs[:n], refs[n:]
    copies = []
    for i, p in enumerate(pieces):
        at = pl.ds(pl.multiple_of(spots[i], 16), p.shape[0])
        copies.append(pltpu.make_async_copy(p, out.at[at], sems.at[i]))
        copies[-1].start()
    for c in copies:
        c.wait()


def rms_rows(pieces, spots, gains, lane, tok, width):
    n = len(pieces)
    fresh = gains.ndim == 3
    count = gains.shape[0] if fresh else 1
    S = jax.ShapeDtypeStruct
    return pl.pallas_call(
        functools.partial(rms_kernel, n, lane, width, fresh),
        out_shape=[S((width, tok), BF), S((1, tok), F32), S((width, 128) if fresh else (16, 128), BF)],
        in_specs=[SM, AN if fresh else VM] + [AN] * n, out_specs=[VM, VM, VM],
        scratch_shapes=[pltpu.VMEM((width, tok), BF), pltpu.SemaphoreType.DMA((n,)), pltpu.SemaphoreType.DMA((count,))],
        compiler_params=pltpu.CompilerParams(vmem_limit_bytes=10 << 20), name="rms_rows",
        cost_estimate=pl.CostEstimate(flops=8 * width * tok, bytes_accessed=4 * width * tok, transcendentals=0),
    )(spots, gains, *pieces)


def collect(pieces, spots, tok, width):
    n = len(pieces)
    return pl.pallas_call(
        functools.partial(collect_kernel, n), out_shape=jax.ShapeDtypeStruct((width, tok), BF),
        in_specs=[SM] + [AN] * n, out_specs=VM, scratch_shapes=[pltpu.SemaphoreType.DMA((n,))],
        compiler_params=pltpu.CompilerParams(vmem_limit_bytes=10 << 20), name="collect",
        cost_estimate=pl.CostEstimate(flops=0, bytes_accessed=4 * width * tok, transcendentals=0),
    )(spots, *pieces)


def hold(x, *deps):
    return lax.optimization_barrier((x,) + deps)[0]


class Pieces:
    def __init__(self, x, devs):
        if devs != 8:
            self.direct = self.diag = (x,)
            self.all = [lax.all_gather(x, "head", axis=0, tiled=True)]
            return
        rows = x.shape[0]

        def swap(v, bit):
            return lax.ppermute(v, "head", [(i, i ^ bit) for i in range(8)])

        along_x = swap(x, 2)
        along_y = swap(x, 4)
        peer = swap(x, 1)
        low = swap(along_x[:rows // 2], 4)
        high = swap(along_y[rows // 2:], 2)
        self.direct = (along_x, along_y)
        self.diag = (low, high)
        self.all = [x, peer, along_x, swap(along_x, 1), along_y, swap(along_y, 1), low, high, swap(low, 1), swap(high, 1)]


class Scatter:
    def __init__(self, left, right, rows, own, devs):
        self.own, self.devs = own, devs
        self.terms = None
        if devs != 8:
            total = sum(tn(a, b) for a, b in zip(left, right)).astype(BF)
            self.pair = (total, total[:16])
            self.dot = jnp.sum(total.astype(F32) * rows.astype(F32), 0, keepdims=True)
            return
        me = lax.axis_index("head")
        self.chip = me // 2
        keep, give, self.dot = parts((me % 2).reshape(1), left, right, rows, own)
        self.pair = (keep, give)

    def swap(self, v, bit):
        return lax.ppermute(v, "head", [(i, i ^ bit) for i in range(8)])

    def add(self, a, b):
        return (a.astype(F32) + b.astype(F32)).astype(BF)

    def spread(self):
        if self.devs != 8:
            return
        half = self.own // 2
        self.acc = self.add(self.pair[0], self.swap(self.pair[1], 1))
        far, to_x, to_y, home = [lax.dynamic_index_in_dim(self.acc, self.chip ^ k, 0, keepdims=False) for k in (3, 1, 2, 0)]
        low, high = self.swap(far[:half], 2), self.swap(far[half:], 4)
        x_low, y_high = self.swap(to_x[:half], 2), self.swap(to_y[half:], 4)
        x_high, y_low = self.swap(self.add(to_x[half:], high), 2), self.swap(self.add(to_y[:half], low), 4)
        self.terms = (home, (x_low, x_high), (y_low, y_high))

    def result(self):
        if self.devs != 8:
            return lax.psum_scatter(self.pair[0], "head", scatter_dimension=0, tiled=True).astype(F32)
        if self.terms is None:
            self.spread()
        home, *pairs = self.terms
        total = home.astype(F32)
        for pair in pairs:
            total = total + jnp.concatenate([v.astype(F32) for v in pair], 0)
        return total


def spread_gains(cols, devs):
    cols = jnp.pad(cols, ((0, 0), (0, 128 - cols.shape[1])))[None]
    if devs != 8:
        return lax.all_gather(cols, "head", axis=1, tiled=True)
    for bit in (1, 2, 4):
        cols = jnp.concatenate([cols, lax.ppermute(cols, "head", [(i, i ^ bit) for i in range(8)])], 0)
    return cols


def piece_spots(own, devs):
    if devs != 8:
        return jnp.zeros((1,), jnp.int32)
    me = lax.axis_index("head")
    half = own // 2
    places = [(0, 0), (1, 0), (2, 0), (3, 0), (4, 0), (5, 0), (6, 0), (6, half), (7, 0), (7, half)]
    return jnp.stack([(me ^ bits) * own + off for bits, off in places]).astype(jnp.int32)


FREE = pl.CostEstimate(flops=0, bytes_accessed=0, transcendentals=0)
COLS = 512


def wide_params(mib):
    return pltpu.CompilerParams(vmem_limit_bytes=mib << 20)


def wgrad_kernel(a, b, out):
    out[...] = nt(a[...], b[...]).astype(BF)


def wgrad(a, b):
    rows, tok = a.shape
    n = b.shape[0]
    return pl.pallas_call(
        wgrad_kernel, grid=(n // COLS,), out_shape=jax.ShapeDtypeStruct((rows, n), BF),
        in_specs=[pl.BlockSpec((rows, tok), lambda i: (0, 0)), pl.BlockSpec((COLS, tok), lambda i: (i, 0))],
        out_specs=pl.BlockSpec((rows, COLS), lambda i: (0, i)),
        compiler_params=wide_params(10), cost_estimate=FREE, name="weight_gradient")(a, b)


def column_blocks(v):
    return pl.BlockSpec((v.shape[0], COLS), lambda i: (0, i))


def turn_kernel(landed, job, back, end, *refs):
    refs = list(refs)
    ins = [refs.pop(0) for _ in range(2 * landed + job * back + 2 * back)]
    if landed:
        x, air = ins.pop(0), ins.pop(0)
        half = refs.pop(0)
        half[...] = (x[...].astype(F32) + air[:x.shape[0], :].astype(F32)).astype(BF)
    if back:
        out = refs.pop(0)

        def put(v):
            out[:v.shape[0], :] = v
            if v.shape[0] < out.shape[0]:
                out[v.shape[0]:, :] = jnp.zeros((out.shape[0] - v.shape[0], out.shape[1]), BF)

        half, air = ins[-2:]

        def total():
            put((half[...].astype(F32) + air[...].astype(F32)).astype(BF))

        if job:
            pl.when(end[0] > 0)(lambda: put(ins[0][...]))
            pl.when(end[0] == 0)(total)
        else:
            total()


def turn(end, sent, came, job, back):
    ins = ([sent.x, came] if sent else []) + ([job.x] if job and back else []) + ([back.half, back.air] if back else [])
    outs = []
    if sent:
        outs.append(jax.ShapeDtypeStruct(sent.x.shape, BF))
    if back:
        rows = max(job.x.shape[0] if job else 0, back.half.shape[0])
        outs.append(jax.ShapeDtypeStruct((rows, back.half.shape[1]), BF))
    res = []
    if outs:
        res = list(pl.pallas_call(
            functools.partial(turn_kernel, bool(sent), bool(job), bool(back)), grid=(outs[0].shape[1] // COLS,),
            out_shape=outs, in_specs=[SM] + [column_blocks(v) for v in ins], out_specs=[column_blocks(v) for v in outs],
            compiler_params=wide_params(10), cost_estimate=FREE, name="turn")(end, *ins))
    half = res.pop(0) if sent else None
    load = res.pop(0) if back else (job.x if job else None)
    return half, load


def finish_kernel(sizes, end, *refs):
    n = len(sizes)
    airs, sents, out = refs[:n], refs[n:2 * n], refs[2 * n]
    for chosen, kind in ((airs, 1), (sents, 0)):
        @pl.when(end[0] == kind)
        def _():
            at = 0
            for v, rows in zip(chosen, sizes):
                out[at:at + rows, :] = v[:rows, :].astype(F32)
                at += rows


def finish(end, jobs):
    sizes = [job.x.shape[0] for job in jobs]
    vals = [job.landed for job in jobs] + [job.sent for job in jobs]
    out = jax.ShapeDtypeStruct((sum(sizes), vals[0].shape[1]), F32)
    return pl.pallas_call(
        functools.partial(finish_kernel, sizes), grid=(out.shape[1] // COLS,), out_shape=out,
        in_specs=[SM] + [column_blocks(v) for v in vals], out_specs=column_blocks(out),
        compiler_params=wide_params(12), cost_estimate=FREE, name="finish")(end, *vals)


def parts_kernel(n, core, *refs):
    left, right, (rows, keep, give, dot) = refs[:n], refs[n:2 * n], refs[2 * n:]
    which = pl.program_id(1)
    total = tn(left[0][...], right[0][...])
    for a, b in zip(left[1:], right[1:]):
        total = total + tn(a[...], b[...])
    low = total.astype(BF)

    @pl.when((pl.program_id(0) == 0) & (which == 0))
    def _():
        dot[...] = jnp.zeros_like(dot)

    dot[...] += jnp.sum(low.astype(F32) * rows[...].astype(F32), 0, keepdims=True)

    @pl.when(which == 0)
    def _():
        keep[0] = low

    @pl.when(which == 1)
    def _():
        give[0] = low


def parts(core, left, right, rows, own):
    tok = right[0].shape[1]
    n = len(left)
    chips = left[0].shape[1] // (2 * own)
    block = lambda c, w, core: c * 2 + (core[0] ^ w)
    S = jax.ShapeDtypeStruct
    spec = pltpu.PrefetchScalarGridSpec(
        num_scalar_prefetch=1, grid=(chips, 2),
        in_specs=[pl.BlockSpec((v.shape[0], own), lambda c, w, core: (0, block(c, w, core))) for v in left]
        + [pl.BlockSpec(v.shape, lambda c, w, core: (0, 0)) for v in right]
        + [pl.BlockSpec((own, tok), lambda c, w, core: (block(c, w, core), 0))],
        out_specs=[pl.BlockSpec((1, own, tok), lambda c, w, core: (c, 0, 0))] * 2
        + [pl.BlockSpec((1, tok), lambda c, w, core: (0, 0))])
    return pl.pallas_call(
        functools.partial(parts_kernel, n), grid_spec=spec,
        out_shape=[S((chips, own, tok), BF)] * 2 + [S((1, tok), F32)],
        compiler_params=wide_params(18), name="parts",
        cost_estimate=pl.CostEstimate(flops=10**10, bytes_accessed=10**7, transcendentals=0))(core, *left, *right, rows)


from jax.sharding import PartitionSpec as P


def col_sum(x):
    return jnp.sum(x, 0, keepdims=True)


def gelu_tanh(values):
    return jax.nn.gelu(values, approximate=True)


def layout(seq_lens, row_count):
    padded = (seq_lens + MB - 1) // MB * MB
    starts = jnp.cumsum(padded) - padded
    positions = jnp.arange(row_count, dtype=jnp.int32)
    inside = (positions[None, :] >= starts[:, None]) & (positions[None, :] < (starts + seq_lens)[:, None])
    valid_rows = jnp.any(inside, axis=0).astype(F32)
    block_first = jnp.arange(row_count // MB, dtype=jnp.int32) * MB
    begins = jnp.any((starts[:, None] == block_first[None, :]) & (seq_lens[:, None] > 0), axis=0)
    return valid_rows, (begins | (block_first == 0)).astype(jnp.int32)


def tie(*values):
    return lax.optimization_barrier(values)


class Sum:
    def __init__(self, x):
        self.x = x
        self.half = self.air = self.sent = self.landed = None


class Belt:
    def __init__(self):
        self.line = lax.axis_size("dp") == 4
        at = lax.axis_index("dp")
        self.end = ((at == 0) | (at == 3)).astype(jnp.int32).reshape(1)
        self.outer = self.inner = None
        self.groups = []
        self.idle = False

    def tick(self, x, *values):
        job = Sum(x) if x is not None else None
        if not self.line:
            return (job,) + tuple(tie(*values)) if values else (job,)
        airs = ([self.outer[2]] if self.outer else []) + ([self.inner.air] if self.inner else [])
        done = []
        if self.idle:
            done = [g for g in self.groups if g.out is None and all(s.landed is not None for s in g.jobs)]
            for g in done:
                g.out = finish(self.end, g.jobs)
        held = tie(*airs, *([x] if job else []), *values, *[g.out for g in done])
        for g, out in zip(reversed(done), reversed(held)):
            g.out = out
        if job:
            job.x = held[len(airs)]
        values = held[len(airs) + (1 if job else 0):len(held) - len(done)]
        back, self.inner = self.inner, None
        if back:
            back.air = held[len(airs) - 1]
        sent, gone = self.outer[:2] if self.outer else (None, None)
        if gone:
            gone.landed = held[0]
        half, load = turn(self.end, sent, held[0], job, back)
        if sent:
            sent.half = half
            sent.air = lax.ppermute(half, "dp", [(1, 2), (2, 1)])
            self.inner = sent
        self.outer = None
        if load is not None:
            self.outer = (job, back, lax.ppermute(load, "dp", [(0, 1), (1, 0), (2, 3), (3, 2)]))
            if back:
                back.sent = load
        loads = [v for v in (half, load) if v is not None]
        if values and loads:
            values = tie(*values, *loads)[:len(values)]
        return (job,) + tuple(values)

    def drain(self):
        self.idle = True
        while self.outer or self.inner:
            self.tick(None)

    def group(self, *jobs):
        self.groups.append(Group(jobs))
        return self.groups[-1]

    def result(self, group):
        if not self.line:
            return lax.psum(jnp.concatenate([s.x for s in group.jobs], 0), "dp").astype(F32)
        return finish(self.end, group.jobs) if group.out is None else group.out


class Group:
    def __init__(self, jobs):
        self.jobs = jobs
        self.out = None


def on_device(
    tokens, lengths, attn_gain, w_query, w_key, w_value, w_gate, w_rate, rate_bias,
    inner_weight, inner_bias, inner_gain, inner_shift, post_gain, post_shift, w_out,
    ffn_gain, w_hidden_gate, w_hidden_up, w_down, out_grad,
):
    tok = tokens.shape[1]
    own = tokens.shape[0]
    heads = inner_weight.shape[0]
    devs = lax.axis_size("head")
    width = own * devs
    belt = Belt()

    def gather(x):
        return lax.all_gather(x, "head", axis=0, tiled=True)

    def head_sum(v):
        if devs != 8:
            return lax.psum(v, "head")
        for bit in (1, 2, 4):
            v = v + lax.ppermute(v, "head", [(i, i ^ bit) for i in range(8)])
        return v

    valid, reset = layout(lengths, tok)
    vrow = valid[None, :]
    spots = piece_spots(own, devs)
    stacked = jnp.concatenate([w_query, w_key, w_value, w_gate, jnp.pad(w_rate.T, ((0, 16 - heads), (0, 0)))], 0)
    tok_pieces = Pieces(tokens, devs)
    gain_blocks = spread_gains(jnp.stack([attn_gain, post_gain, post_shift, ffn_gain], 1), devs)
    consts = [hold(v, *tok_pieces.direct).astype(F32) for v in (inner_weight, inner_bias, inner_gain, inner_shift)]
    consts = pack_consts(*consts)
    g_full = gather(hold(out_grad, gain_blocks, *tok_pieces.diag))
    nin, q1, gains = rms_rows(tok_pieces.all, spots, gain_blocks, 0, tok, width)
    gate = nn(w_gate, nin).astype(BF)
    gelu_own = gelu_tanh(gate.astype(F32))
    nin_q = hold(nin, gate)
    q_t = nn(w_query, nin_q)
    k_t = nn(w_key, nin_q)
    v_t = nn(w_value, nin_q)
    logits = tn(w_rate, nin) + rate_bias.astype(F32)[:, None]
    sig = jax.nn.sigmoid(logits)
    masked = sig * vrow
    mixer_own, zt, zb, td, qa, ka, wt, rows = ttt_fwd(
        reset, q_t, k_t, v_t, masked * (1.0 / HD), vrow, consts)

    mixer_own, g_full, gelu_own = tie(mixer_own, g_full, gelu_own)
    mixer_rows = mixer_own.astype(F32)
    mean3 = col_sum(mixer_rows) / own
    spread3 = col_sum((mixer_rows - mean3) * (mixer_rows - mean3))
    if devs == 8:
        count = own
        for bit in (1, 2, 4):
            both = jnp.concatenate([mean3, spread3], 0)
            other = lax.ppermute(both, "head", [(i, i ^ bit) for i in range(8)])
            gap = other[:1] - mean3
            mean3 = (mean3 + other[:1]) * 0.5
            spread3 = spread3 + other[1:] + gap * gap * (count * 0.5)
            count *= 2
    else:
        mean3 = lax.psum(mean3, "head") / devs
        spread3 = lax.psum(col_sum((mixer_rows - mean3) * (mixer_rows - mean3)), "head")
    r3 = lax.rsqrt(spread3 / width + EPS)
    n3 = (mixer_rows - mean3) * r3
    pg_own = post_gain.astype(F32)[:, None]
    ps_own = post_shift.astype(F32)[:, None]
    mixed_own = ((n3 * pg_own + ps_own) * gelu_own).astype(BF)
    mixed = collect(Pieces(mixed_own, devs).all, spots, tok, width)
    hidden = tokens.astype(F32) + nn(w_out, mixed)
    hidden_low = hidden.astype(BF)
    nmid, q2, _ = rms_rows(Pieces(hidden_low, devs).all, spots, gains, 3, tok, width)
    gate_val = nn(w_hidden_gate, nmid)
    up_val = nn(w_hidden_up, nmid)
    sg = jax.nn.sigmoid(gate_val)
    act = (gate_val * sg * up_val).astype(BF)

    def halves(x, other):
        cut = (x.shape[0] // 2 + 7) // 8 * 8
        return wgrad(x[:cut], other), wgrad(x[cut:], other)

    down = halves(act, g_full)
    here = lax.axis_index("head") + 1
    marks = lax.broadcasted_iota(jnp.int32, (1, tok), 1)
    rates = jnp.where(marks == 0, jnp.sum(masked), jnp.where(marks == here, jnp.max(masked), 0.0))
    d0, g_full, rates = belt.tick(down[0], g_full, rates)
    g_act = nn(w_down, g_full)
    g_up = (g_act * gate_val * sg).astype(BF)
    g_gate = (g_act * up_val * sg * (1.0 + gate_val * (1.0 - sg))).astype(BF)
    gn = Scatter([w_hidden_gate, w_hidden_up], [g_gate, g_up], nmid, own, devs)
    d1, *gn.pair, gn.dot, rates, g_up, g_gate = belt.tick(down[1], *gn.pair, gn.dot, rates, g_up, g_gate)
    gn.spread()
    hgate = halves(g_gate, nmid)
    sums = head_sum(jnp.concatenate([gn.dot, rates], 0))
    mid_dot, rates = sums[:1], sums[1:]
    gn = gn.result()
    h0, gn, mid_dot, rates, g_up, h1_x = belt.tick(hgate[0], gn, mid_dot, rates, g_up, hgate[1])
    hid_own = hidden_low.astype(F32)
    fg_own = ffn_gain.astype(F32)[:, None]
    g_ffn_gain = jnp.sum(gn * hid_own * q2, 1)
    g_hidden = out_grad.astype(F32) + q2 * fg_own * gn - hid_own * q2**2 * mid_dot / width
    g_branch = g_hidden.astype(BF)
    gm = Scatter([w_out], [g_branch], mixed, own, devs)
    hup = halves(g_up, nmid)
    h1, *gm.pair, g_branch, u0_x = belt.tick(h1_x, *gm.pair, g_branch, hup[0])
    gm.spread()
    out_w = wgrad(g_branch, mixed)
    gm = gm.result()
    u0, gm, out_w, u1_x, act = belt.tick(u0_x, gm, out_w, hup[1], act)
    ffn_part = tn(w_down, act).astype(BF)
    a_own, gelu_pull = jax.vjp(gelu_tanh, gate.astype(F32))
    g_post_gain = jnp.sum(gm * a_own * n3, 1)
    g_post_shift = jnp.sum(gm * a_own, 1)
    g_gate_pre = gelu_pull(gm * (n3 * pg_own + ps_own))[0].astype(BF)
    m = gm * a_own * pg_own
    sums = head_sum(jnp.concatenate([col_sum(m), col_sum(m * n3)], 0))
    s_plain, s_norm = sums[:1], sums[1:]
    g_mixer = r3 * (m - s_plain / width - n3 * s_norm / width)
    u1, g_mixer, g_gate_pre, out_w, ffn_part = belt.tick(u1_x, g_mixer, g_gate_pre, out_w, ffn_part)
    ffn = lax.psum_scatter(ffn_part, "head", scatter_dimension=0, tiled=True)
    gate_w = wgrad(g_gate_pre, nin)
    saved = (zt, zb, td, qa, ka, wt, rows, consts)
    b1 = ttt_bwd(1, 2, reset, g_mixer, *saved)
    so, lam, lam_c, gate_w = belt.tick(out_w, b1[8], b1[9], gate_w)
    b0 = ttt_bwd(0, 2, reset, g_mixer, *saved, carry=(lam, lam_c) + tuple(b1[:3]))
    dq, dk, dv = b0[:3]
    de_rows = jnp.concatenate([b0[3], b1[3]], 1)
    dgl, dsl, dw0, dc0 = [b0[i] + b1[i] for i in range(4, 8)]
    g_logits = de_rows * vrow * (1.0 / HD) * sig * (1.0 - sig)
    gl = g_logits.astype(BF)
    g_inner_w = dw0.reshape(HD, heads, HD).transpose(1, 2, 0)
    g_inner_b = dc0.reshape(HD, heads, MB)[:, :, 0].T
    g_inner_g = dgl.reshape(HD, heads, MB).sum(-1).T
    g_inner_s = dsl.reshape(HD, heads, MB).sum(-1).T
    wide_q, wide_k, wide_v = [wgrad(v, nin) for v in (dq, dk, dv)]
    wg, dq, dk, dv, gl, wide_q, wide_k, wide_v, ffn = belt.tick(
        gate_w, dq, dk, dv, gl, wide_q, wide_k, wide_v, ffn)
    result = (hidden + ffn.astype(F32)).astype(BF)
    tall = jnp.concatenate([dq, dk, dv, g_gate_pre, jnp.pad(gl, ((0, 16 - heads), (0, 0)))], 0)
    gi = Scatter([stacked], [tall], nin, own, devs)
    q, *gi.pair, gi.dot, wide_k = belt.tick(wide_q, *gi.pair, gi.dot, wide_k)
    gi.spread()
    in_dot = head_sum(gi.dot)
    gi = gi.result()
    g_wr = nt(gl, nin)
    k, gi, in_dot, g_wr = belt.tick(wide_k, gi, in_dot, g_wr)
    x_own = tokens.astype(F32)
    ag_own = attn_gain.astype(F32)[:, None]
    g_attn_gain = jnp.sum(gi * x_own * q1, 1)
    g_tokens = g_hidden + q1 * ag_own * gi - x_own * q1**2 * in_dot / width
    top = jnp.max(jnp.where(marks > 0, rates, 0.0))
    both = jnp.stack([rates[0, 0], top])
    cut = []
    for _ in range(3):
        cut.append(lax.reduce_precision(both, 8, 7))
        both = both - cut[-1]
    dps = lax.axis_size("dp")
    slot = (jnp.arange(dps) == lax.axis_index("dp")).astype(F32)
    slots = (slot[:, None, None] * jnp.stack(cut)[None]).reshape(-1)
    vectors = [g_attn_gain, g_post_gain, g_post_shift, g_ffn_gain, g_inner_b, g_inner_g, g_inner_s,
               jnp.sum(g_logits, 1), slots]
    vectors = [jnp.pad(u.reshape(-1), (0, own - u.size)) for u in vectors]
    small = jnp.concatenate([u.astype(BF).reshape(-1) for u in vectors + [g_inner_w, g_wr]])
    count = small.shape[0]
    small = jnp.pad(small, (0, -count % (16 * width))).reshape(-1, width)
    v, = belt.tick(jnp.concatenate([wide_v, small], 0))
    sums = [belt.group(*jobs) for jobs in ((d0, d1), (h0, h1), (u0, u1), (so,), (wg,), (q,), (k,), (v,))]
    belt.drain()
    s_down, s_hgate, s_hup, s_out, s_wg, s_wq, s_wk, s_wv = [belt.result(g) for g in sums]
    s_wv, small = s_wv[:own], s_wv[own:].reshape(-1)
    s_attn, s_pg, s_ps, s_fg, s_ib, s_ig, s_is, s_rb, slots = [small[i * own:(i + 1) * own] for i in range(9)]
    s_ib, s_ig, s_is = [v.reshape(heads, HD) for v in (s_ib, s_ig, s_is)]
    s_rb = s_rb[:heads]
    wide = 9 * own + heads * HD * HD
    s_iw = small[9 * own:wide].reshape(heads, HD, HD)
    s_wr = small[wide:count].reshape(heads, width)
    slots = jnp.sum(slots[:dps * 6].reshape(dps, 3, 2), 1)
    mean_rate = jnp.sum(slots[:, 0]) / (tok * dps * heads * devs)
    max_rate = jnp.max(slots[:, 1])

    return (
        result, g_tokens, s_attn, s_wq, s_wk, s_wv, s_wg,
        s_wr.T, s_rb, s_iw, s_ib, s_ig, s_is, s_pg, s_ps, s_out,
        s_fg, s_hgate, s_hup, s_down, mean_rate, max_rate,
    )


def solution(mesh):
    h = P("head")
    m = P("head", None)
    c = P("head", None, None)
    t = P("head", "dp")
    r = P(None, "head")
    ins = (t, P("dp"), h, m, m, m, m, r, h, c, m, m, m, h, h, m, h, m, m, m, t)
    outs = (t, t, h, m, m, m, m, r, h, c, m, m, m, h, h, m, h, m, m, m, P(), P())
    return jax.shard_map(on_device, mesh=mesh, in_specs=ins, out_specs=outs, check_vma=False)
```

```python
import jax, jax.numpy as jnp
from jax import lax
from jax.experimental import pallas as pl
from jax.experimental.pallas import tpu as pltpu
import functools
HD=64; MB=16; EPS=1e-6
F32=jnp.float32; BF=jnp.bfloat16

def nn(a,b): return lax.dot_general(a,b,(((1,),(0,)),((),())),preferred_element_type=F32)
def nt(a,b): return lax.dot_general(a,b,(((1,),(1,)),((),())),preferred_element_type=F32)
def tn(a,b): return lax.dot_general(a,b,(((0,),(0,)),((),())),preferred_element_type=F32)

def avg(x): return jnp.sum(x,0,keepdims=True)*(1.0/HD)

def lane_heads(heads, rows):
    return lax.broadcasted_iota(jnp.int32,(rows,heads*MB),1)//MB

def spread(x, heads):
    ids=lane_heads(heads,HD)
    return jnp.concatenate([jnp.where(ids==h,x,jnp.zeros_like(x)) for h in range(heads)],0)

def gather_blocks(x, heads):
    ids=lane_heads(heads,HD)
    out=jnp.zeros((HD,heads*MB),F32)
    for h in range(heads):
        out=out+jnp.where(ids==h,x[h*HD:(h+1)*HD],0.0)
    return out

def split_heads(ref, group, heads):
    cols=[ref[h*HD:(h+1)*HD, pl.ds(pl.multiple_of(group*128,128),128)] for h in range(heads)]
    return [jnp.concatenate([c[:,p*MB:(p+1)*MB] for c in cols],1) for p in range(8)]

def merge_heads(ref, group, parts, heads):
    for h in range(heads):
        blk=jnp.concatenate([p[:,h*MB:(h+1)*MB] for p in parts],1)
        ref[h*HD:(h+1)*HD, pl.ds(pl.multiple_of(group*128,128),128)]=blk.astype(ref.dtype)

def padded(x):
    rows=lax.broadcasted_iota(jnp.int32,(MB,x.shape[1]),0)
    return jnp.concatenate([x,jnp.where(rows==0,1.0,0.0).astype(F32)],0)

def same_head(heads):
    L=heads*MB
    r=lax.broadcasted_iota(jnp.int32,(L,L),0); c=lax.broadcasted_iota(jnp.int32,(L,L),1)
    return r//MB==c//MB, r%MB, c%MB

def step_grad(zt, td, g, s):
    mu=avg(zt); cen=zt-mu
    r=lax.rsqrt(avg(cen*cen)+EPS)
    n=cen*r
    v=n*g+s-td
    u=v*g
    m1=avg(u); m2=avg(u*n)
    return r,n,v,u,m2,r*(u-m1-n*m2)

def fwd_kernel(heads, nb, reset, qT, kT, vT, rate, valid, consts,
               outT, zt_o, zb_o, td_o, qa_o, ka_o, wt_o, rows, mp, q32):
    L=heads*MB
    same,ri,ci_=same_head(heads)
    tri=jnp.where(same&(ri<=ci_), 16.0/(ci_.astype(F32)+1.0), 0.0)
    diag=jnp.where(same,1.0,0.0)
    def pre(gr,_):
        qs=split_heads(qT,gr,heads); ks=split_heads(kT,gr,heads); vs=split_heads(vT,gr,heads)
        at=pl.ds(pl.multiple_of(gr*128,128),128)
        rt=rate[:,at]; vl=valid[:,at]
        for p in range(8):
            b=gr*8+p
            cut=slice(p*MB,(p+1)*MB)
            rows[b]=jnp.concatenate([jnp.concatenate([rt[h:h+1,cut] for h in range(heads)],1),
                                     jnp.concatenate([vl[:,cut]]*heads,1)],0)
            td_o[b]=vs[p]-ks[p]
            q32[b]=qs[p]
            qa_o[b]=padded(qs[p]).astype(BF)
            ka_o[b]=padded(ks[p]).astype(BF)
        return 0
    lax.fori_loop(0,nb//8,pre,0)
    def pre2(b,_):
        nxt=jnp.minimum(b+1,nb-1)
        ke=(ka_o[b].astype(F32)*(rows[b,0:1]*(1.0/MB))).astype(BF)
        keep=jnp.where(reset[nxt]>0,0.0,1.0)
        m=tn(ke,ka_o[nxt])*(diag*keep)
        pt=tn(ke,qa_o[b])*tri
        mp[b]=jnp.concatenate([m,pt],1).astype(BF)
        return 0
    lax.fori_loop(0,nb,pre2,0,unroll=8)
    w0,c0,g,s=unpack_consts(consts,heads)
    def body(b,carry):
        zt,wt,ct=carry
        nxt=jnp.minimum(b+1,nb-1)
        rs=reset[nxt]>0
        wt_b=wt.astype(BF)
        wt_o[b]=wt_b; zt_o[b]=zt
        r,n,v,u,m2,gt=step_grad(zt,td_o[b],g,s)
        gb=gt.astype(BF)
        kn=spread(ka_o[nxt][:HD],heads)
        wsel=jnp.where(rs,w0,wt).astype(BF)
        csel=jnp.where(rs,c0,ct)
        yk=nn(wsel,kn)+csel
        yq=nn(wt_b,spread(qa_o[b][:HD],heads))+ct
        rr=nn(gb,mp[b])
        e16=rows[b,0:1]*(1.0/MB)
        ke=(ka_o[b][:HD].astype(F32)*e16).astype(BF)
        rw=nt(gb,spread(ke,heads))
        ec=jnp.where(same,jnp.broadcast_to(e16,(L,L)),0.0).astype(BF)
        rc=nt(gb,ec)
        zb_o[b]=yq-rr[:,L:]
        z2=yk-rr[:,:L]
        return z2,jnp.where(rs,w0,wt-rw),jnp.where(rs,c0,ct-rc)
    zt=nn(w0.astype(BF),spread(ka_o[0][:HD],heads))+c0
    lax.fori_loop(0,nb,body,(zt,w0,c0),unroll=8)
    def post(gr,_):
        outs=[]
        for p in range(8):
            b=gr*8+p
            zb=zb_o[b]; cen=zb-avg(zb)
            n=cen*lax.rsqrt(avg(cen*cen)+EPS)
            outs.append((q32[b]+n*g+s)*rows[b,1:2])
        merge_heads(outT,gr,outs,heads)
        return 0
    lax.fori_loop(0,nb//8,post,0)

VM=pl.BlockSpec(memory_space=pltpu.VMEM)
SM=pl.BlockSpec(memory_space=pltpu.SMEM)
AN=pl.BlockSpec(memory_space=pl.ANY)

def pack_consts(w0, c0, g, s):
    heads=w0.shape[0]
    cols=[w0.transpose(2,0,1).reshape(HD,heads*HD)]+[lane_cols(v) for v in (c0,g,s)]
    return jnp.concatenate([jnp.pad(v,((0,0),(0,-v.shape[1]%128))) for v in cols],1)

def unpack_consts(ref, heads):
    wide=(heads*HD+127)//128*128; step=(heads*MB+127)//128*128
    return [ref[:,:heads*HD]]+[ref[:,wide+i*step:wide+i*step+heads*MB] for i in range(3)]

def ttt_fwd(reset, qT,kT,vT, rate, valid, consts):
    T=qT.shape[1]; heads=qT.shape[0]//HD; nb=T//MB; L=heads*MB; S=jax.ShapeDtypeStruct
    outs=[S((heads*HD,T),BF),S((nb,HD,L),F32),S((nb,HD,L),F32),S((nb,HD,L),F32),S((nb,HD+MB,L),BF),S((nb,HD+MB,L),BF),
          S((nb,HD,heads*HD),BF),S((nb,2,L),F32)]
    def whole(v): return pl.BlockSpec(v.shape,lambda i:(0,)*len(v.shape))
    args=[qT,kT,vT,rate,valid,consts]
    return pl.pallas_call(functools.partial(fwd_kernel,heads,nb),out_shape=outs,grid=(1,),
        in_specs=[SM]+[whole(v) for v in args],out_specs=[whole(v) for v in outs],
        scratch_shapes=[pltpu.VMEM((nb,L,2*L),BF),pltpu.VMEM((nb,HD,L),F32)],
        compiler_params=pltpu.CompilerParams(vmem_limit_bytes=34<<20), name="mix_forward",
        cost_estimate=pl.CostEstimate(flops=T*heads*64, bytes_accessed=T*heads, transcendentals=0))(
            reset,*args)

def bwd_kernel(heads, nb, base, last, reset, dOT, zt_i, zb_i, td_i, qa_i, ka_i, wt_i, rows, consts, *refs):
    if last:
        li=lci=None
    else:
        li,lci=refs[:2]; refs=refs[5:]
    (dqT, dkT, dvT, de_o, dg_o, ds_o, dw0_o, dc0_o, lo, lco,
               n_s, v_s, r_s, m2_s, gb_s, gh_s, nm_s, u_s, uc_s, dq_s, dk_s, du_s, dz_s, h_s, la_s, de_s)=refs
    L=heads*MB
    _,_,g,s=unpack_consts(consts,heads)
    same,ri,cj=same_head(heads)
    tri=jnp.where(same&(cj<=ri),1.0/(ri.astype(F32)+1.0),0.0)
    diag=jnp.where(same,1.0,0.0)
    diag_b=diag.astype(BF)
    dg_o[...]=jnp.zeros((HD,L),F32); ds_o[...]=jnp.zeros((HD,L),F32)
    dw0_o[...]=jnp.zeros_like(dw0_o); dc0_o[...]=jnp.zeros_like(dc0_o)
    def pre(gr,_):
        dos=split_heads(dOT,gr,heads)
        dga=jnp.zeros((HD,L),F32); dsa=jnp.zeros((HD,L),F32)
        for p in range(8):
            b=gr*8+p
            dO=dos[p].astype(F32)*rows[b,1:2]
            zb=zb_i[b]; cen=zb-avg(zb); rb=lax.rsqrt(avg(cen*cen)+EPS); nbar=cen*rb
            dga=dga+dO*nbar; dsa=dsa+dO
            dn=dO*g
            dzb=rb*(dn-avg(dn)-nbar*avg(dn*nbar))
            dzb_b=dzb.astype(BF)
            r,n,v,u,m2,gt=step_grad(zt_i[b],td_i[b],g,s)
            gb=gt.astype(BF)
            n_s[b]=n; v_s[b]=v; r_s[b]=r; m2_s[b]=m2; gb_s[b]=gt
            e=rows[b,0:1]
            ka=ka_i[b]; qa=qa_i[b]
            st=tn(qa,ka)*tri
            gh_s[b]=-nn(dzb_b,(st*e).astype(BF))
            dp=-tn(dzb_b,gb)
            de_s[b]=jnp.sum(dp*st,0,keepdims=True)
            dS=(dp*tri*e).astype(BF)
            dq_s[b]=dO+gather_blocks(tn(wt_i[b],dzb_b),heads)+nt(ka[:HD],dS)
            dk_s[b]=nn(qa[:HD],dS)
            prev=jnp.maximum(b-1,0)
            keep=jnp.where(reset[base+b]>0,0.0,1.0)
            nm_s[b]=(tn(ka,ka_i[prev])*(diag*keep)).astype(BF)
            u_s[b]=nt(dzb_b,spread(qa[:HD],heads))
            uc_s[b]=nn(dzb_b,diag_b)
        dg_o[...]+=dga; ds_o[...]+=dsa
        return 0
    lax.fori_loop(0,nb//8,pre,0)
    def body(k,carry):
        ht,la,lc=carry
        b=nb-1-k
        prev=jnp.maximum(b-1,0)
        rs=reset[base+b]>0
        n=n_s[b]; v=v_s[b]; r=r_s[b]; m2=m2_s[b]; gt=gb_s[b]
        h_s[b]=ht
        la_s[b]=la.astype(BF)
        dG=gh_s[b]-(rows[b,0:1]*(1.0/MB))*ht
        da=r*dG
        m3=avg(da); m4=avg(da*n); m6a=avg(dG*gt)
        du=da-m3-n*m4
        dn=(du*g-v*m4)*g-da*m2
        m5=avg(dn); m6=m6a+avg(dn*n)
        dz=(r*(dn-m5-n*m6)).astype(BF)
        du_s[b]=du
        dz_s[b]=dz
        la2=la+u_s[b]; lc2=lc+uc_s[b]
        y=nn(la2.astype(BF),spread(ka_i[prev][:HD],heads))+lc2
        h2=jnp.where(rs,0.0,y)+nn(dz,nm_s[b])
        la3=la2+nt(dz,spread(ka_i[b][:HD],heads)); lc3=lc2+nn(dz,diag_b)
        @pl.when(rs)
        def _():
            dw0_o[...]+=la3; dc0_o[...]+=lc3
        return h2,jnp.where(rs,0.0,la3),jnp.where(rs,0.0,lc3)
    la=jnp.zeros((HD,heads*HD),F32) if last else li[...]
    lc=jnp.zeros((HD,L),F32) if last else lci[...]
    ht=nn(la.astype(BF),spread(ka_i[nb-1][:HD],heads))+lc
    ht,la,lc=lax.fori_loop(0,nb,body,(ht,la,lc),unroll=4)
    lo[...]=la; lco[...]=lc
    def post(gr,_):
        dqs=[];dks=[];dvs=[];des=[]
        dga=jnp.zeros((HD,L),F32); dsa=jnp.zeros((HD,L),F32)
        for p in range(8):
            b=gr*8+p
            du=du_s[b]; dug=du*g; gt=gb_s[b]
            dga=dga+du*v_s[b]+dug*n_s[b]; dsa=dsa+dug
            dvs.append(-dug)
            dqs.append(dq_s[b])
            des.append(de_s[b]-avg(gt*h_s[b])*(HD/MB))
            dks.append(dug+dk_s[b]-(rows[b,0:1]*(1.0/MB))*gather_blocks(tn(la_s[b],gt.astype(BF)),heads)
                       +gather_blocks(tn(wt_i[b],dz_s[b]),heads))
        de_o[:,pl.ds(pl.multiple_of(gr*128,128),128)]=jnp.concatenate(
            [jnp.concatenate([d[:,h*MB:(h+1)*MB] for d in des],1) for h in range(heads)],0)
        merge_heads(dqT,gr,dqs,heads); merge_heads(dkT,gr,dks,heads); merge_heads(dvT,gr,dvs,heads)
        dg_o[...]+=dga; ds_o[...]+=dsa
        return 0
    lax.fori_loop(0,nb//8,post,0)

def ttt_bwd(part, parts, reset, dOT, zt,zb,td,qa,ka,wt,rows,consts, carry=None):
    T=dOT.shape[1]//parts; heads=dOT.shape[0]//HD; nb=T//MB; L=heads*MB; S=jax.ShapeDtypeStruct
    W=heads*HD; last=part==parts-1
    outs=[S((W,T*parts),BF)]*3+[S((heads,T),F32)]+[S((HD,L),F32)]*2+[S((HD,W),F32),S((HD,L),F32)]*2
    V=pltpu.VMEM
    scr=[V((nb,HD,L),F32),V((nb,HD,L),F32),V((nb,1,L),F32),V((nb,1,L),F32),V((nb,HD,L),F32),V((nb,HD,L),F32),
         V((nb,L,L),BF),V((nb,HD,W),F32),V((nb,HD,L),F32),V((nb,HD,L),F32),V((nb,HD,L),F32),V((nb,HD,L),F32),
         V((nb,HD,L),BF),V((nb,HD,L),F32),V((nb,HD,W),BF),V((nb,1,L),F32)]
    def whole(*dims): return pl.BlockSpec(dims,lambda i:(0,)*len(dims))
    def third(*dims): return pl.BlockSpec((nb,)+dims,lambda i:(part,)+(0,)*len(dims))
    nat=pl.BlockSpec((W,T),lambda i:(0,part))
    ins=[SM,nat]+[third(HD,L)]*3+[third(HD+MB,L)]*2+[third(HD,W),third(2,L),whole(*consts.shape)]
    args=[reset,dOT,zt,zb,td,qa,ka,wt,rows,consts]
    alias={}
    if not last:
        ins+=[whole(HD,W),whole(HD,L)]+[AN]*3
        alias={12:0,13:1,14:2}
        args+=list(carry)
    return pl.pallas_call(functools.partial(bwd_kernel,heads,nb,part*nb,last),out_shape=outs,grid=(1,),
        in_specs=ins,out_specs=[nat]*3+[whole(heads,T)]+[whole(HD,L)]*2+[whole(HD,W),whole(HD,L)]*2,
        scratch_shapes=scr,input_output_aliases=alias,
        compiler_params=pltpu.CompilerParams(vmem_limit_bytes=30<<20), name="mix_backward",
        cost_estimate=pl.CostEstimate(flops=T*heads*64, bytes_accessed=T*heads, transcendentals=0))(*args)

def lane_cols(x):
    return jnp.repeat(x.T,MB,axis=1)


ROWS = 64


def fetch(pieces, spots, buf, sems, f):
    copies = []
    for i, p in enumerate(pieces):
        at = pl.ds(pl.multiple_of(spots[i], 16), p.shape[0])
        copies.append(pltpu.make_async_copy(p, buf.at[at], sems.at[i]))
        copies[-1].start()
    acc = jnp.zeros((8, buf.shape[1]), F32)
    for i, c in enumerate(copies):
        c.wait()
        acc = fold(buf, spots[i], pieces[i].shape[0], f, acc)
    return jnp.sum(acc, 0, keepdims=True)


def fold(buf, first, rows, f, acc):
    def add(i, acc):
        v = f(buf[pl.ds(pl.multiple_of(first + i * ROWS, ROWS), ROWS), :].astype(F32))
        return acc + jnp.sum(v.reshape(ROWS // 8, 8, v.shape[1]), 0)

    return lax.fori_loop(0, rows // ROWS, add, acc)


def rms_kernel(n, lane, width, fresh, spots, blocks, *refs):
    pieces, (out, scale_out, gains, buf, sems, gain_sems) = refs[:n], refs[n:]
    if fresh:
        copies = []
        for i in range(blocks.shape[0]):
            at = pl.ds(pl.multiple_of(spots[i if i < 7 else 8], 16), blocks.shape[1])
            copies.append(pltpu.make_async_copy(blocks.at[i], gains.at[at], gain_sems.at[i]))
            copies[-1].start()
    scale = lax.rsqrt(fetch(pieces, spots, buf, sems, lambda v: v * v) * (1.0 / width) + EPS)
    if fresh:
        for c in copies:
            c.wait()
    scale_out[...] = scale
    source = gains if fresh else blocks

    def write(i, _):
        at = pl.ds(pl.multiple_of(i * ROWS, ROWS), ROWS)
        gain = source[at, lane:lane + 1].astype(F32)
        out[at, :] = (buf[at, :].astype(F32) * scale * gain).astype(BF)
        return 0

    lax.fori_loop(0, width // ROWS, write, 0)
    if not fresh:
        gains[...] = jnp.zeros_like(gains)


def collect_kernel(n, spots, *refs):
    pieces, (out, sems) = refs[:n], refs[n:]
    copies = []
    for i, p in enumerate(pieces):
        at = pl.ds(pl.multiple_of(spots[i], 16), p.shape[0])
        copies.append(pltpu.make_async_copy(p, out.at[at], sems.at[i]))
        copies[-1].start()
    for c in copies:
        c.wait()


def rms_rows(pieces, spots, gains, lane, tok, width):
    n = len(pieces)
    fresh = gains.ndim == 3
    count = gains.shape[0] if fresh else 1
    S = jax.ShapeDtypeStruct
    return pl.pallas_call(
        functools.partial(rms_kernel, n, lane, width, fresh),
        out_shape=[S((width, tok), BF), S((1, tok), F32), S((width, 128) if fresh else (16, 128), BF)],
        in_specs=[SM, AN if fresh else VM] + [AN] * n, out_specs=[VM, VM, VM],
        scratch_shapes=[pltpu.VMEM((width, tok), BF), pltpu.SemaphoreType.DMA((n,)), pltpu.SemaphoreType.DMA((count,))],
        compiler_params=pltpu.CompilerParams(vmem_limit_bytes=10 << 20), name="rms_rows",
        cost_estimate=pl.CostEstimate(flops=8 * width * tok, bytes_accessed=4 * width * tok, transcendentals=0),
    )(spots, gains, *pieces)


def collect(pieces, spots, tok, width):
    n = len(pieces)
    return pl.pallas_call(
        functools.partial(collect_kernel, n), out_shape=jax.ShapeDtypeStruct((width, tok), BF),
        in_specs=[SM] + [AN] * n, out_specs=VM, scratch_shapes=[pltpu.SemaphoreType.DMA((n,))],
        compiler_params=pltpu.CompilerParams(vmem_limit_bytes=10 << 20), name="collect",
        cost_estimate=pl.CostEstimate(flops=0, bytes_accessed=4 * width * tok, transcendentals=0),
    )(spots, *pieces)


def hold(x, *deps):
    return lax.optimization_barrier((x,) + deps)[0]


class Pieces:
    def __init__(self, x, devs):
        if devs != 8:
            self.direct = self.diag = (x,)
            self.all = [lax.all_gather(x, "head", axis=0, tiled=True)]
            return
        rows = x.shape[0]

        def swap(v, bit):
            return lax.ppermute(v, "head", [(i, i ^ bit) for i in range(8)])

        along_x = swap(x, 2)
        along_y = swap(x, 4)
        peer = swap(x, 1)
        low = swap(along_x[:rows // 2], 4)
        high = swap(along_y[rows // 2:], 2)
        self.direct = (along_x, along_y)
        self.diag = (low, high)
        self.all = [x, peer, along_x, swap(along_x, 1), along_y, swap(along_y, 1), low, high, swap(low, 1), swap(high, 1)]


class Scatter:
    def __init__(self, left, right, rows, own, devs):
        self.own, self.devs = own, devs
        self.terms = None
        if devs != 8:
            total = sum(tn(a, b) for a, b in zip(left, right)).astype(BF)
            self.pair = (total, total[:16])
            self.dot = jnp.sum(total.astype(F32) * rows.astype(F32), 0, keepdims=True)
            return
        me = lax.axis_index("head")
        self.chip = me // 2
        keep, give, self.dot = parts((me % 2).reshape(1), left, right, rows, own)
        self.pair = (keep, give)

    def swap(self, v, bit):
        return lax.ppermute(v, "head", [(i, i ^ bit) for i in range(8)])

    def add(self, a, b):
        return (a.astype(F32) + b.astype(F32)).astype(BF)

    def spread(self):
        if self.devs != 8:
            return
        half = self.own // 2
        self.acc = self.add(self.pair[0], self.swap(self.pair[1], 1))
        far, to_x, to_y, home = [lax.dynamic_index_in_dim(self.acc, self.chip ^ k, 0, keepdims=False) for k in (3, 1, 2, 0)]
        low, high = self.swap(far[:half], 2), self.swap(far[half:], 4)
        x_low, y_high = self.swap(to_x[:half], 2), self.swap(to_y[half:], 4)
        x_high, y_low = self.swap(self.add(to_x[half:], high), 2), self.swap(self.add(to_y[:half], low), 4)
        self.terms = (home, (x_low, x_high), (y_low, y_high))

    def result(self):
        if self.devs != 8:
            return lax.psum_scatter(self.pair[0], "head", scatter_dimension=0, tiled=True).astype(F32)
        if self.terms is None:
            self.spread()
        home, *pairs = self.terms
        total = home.astype(F32)
        for pair in pairs:
            total = total + jnp.concatenate([v.astype(F32) for v in pair], 0)
        return total


def spread_gains(cols, devs):
    cols = jnp.pad(cols, ((0, 0), (0, 128 - cols.shape[1])))[None]
    if devs != 8:
        return lax.all_gather(cols, "head", axis=1, tiled=True)
    for bit in (1, 2, 4):
        cols = jnp.concatenate([cols, lax.ppermute(cols, "head", [(i, i ^ bit) for i in range(8)])], 0)
    return cols


def piece_spots(own, devs):
    if devs != 8:
        return jnp.zeros((1,), jnp.int32)
    me = lax.axis_index("head")
    half = own // 2
    places = [(0, 0), (1, 0), (2, 0), (3, 0), (4, 0), (5, 0), (6, 0), (6, half), (7, 0), (7, half)]
    return jnp.stack([(me ^ bits) * own + off for bits, off in places]).astype(jnp.int32)


FREE = pl.CostEstimate(flops=0, bytes_accessed=0, transcendentals=0)
COLS = 512


def wide_params(mib):
    return pltpu.CompilerParams(vmem_limit_bytes=mib << 20)


def wgrad_kernel(a, b, out):
    out[...] = nt(a[...], b[...]).astype(BF)


def wgrad(a, b):
    rows, tok = a.shape
    n = b.shape[0]
    return pl.pallas_call(
        wgrad_kernel, grid=(n // COLS,), out_shape=jax.ShapeDtypeStruct((rows, n), BF),
        in_specs=[pl.BlockSpec((rows, tok), lambda i: (0, 0)), pl.BlockSpec((COLS, tok), lambda i: (i, 0))],
        out_specs=pl.BlockSpec((rows, COLS), lambda i: (0, i)),
        compiler_params=wide_params(10), cost_estimate=FREE, name="weight_gradient")(a, b)


def column_blocks(v):
    return pl.BlockSpec((v.shape[0], COLS), lambda i: (0, i))


def turn_kernel(landed, job, back, end, *refs):
    refs = list(refs)
    ins = [refs.pop(0) for _ in range(2 * landed + job * back + 2 * back)]
    if landed:
        x, air = ins.pop(0), ins.pop(0)
        half = refs.pop(0)
        half[...] = (x[...].astype(F32) + air[:x.shape[0], :].astype(F32)).astype(BF)
    if back:
        out = refs.pop(0)

        def put(v):
            out[:v.shape[0], :] = v
            if v.shape[0] < out.shape[0]:
                out[v.shape[0]:, :] = jnp.zeros((out.shape[0] - v.shape[0], out.shape[1]), BF)

        half, air = ins[-2:]

        def total():
            put((half[...].astype(F32) + air[...].astype(F32)).astype(BF))

        if job:
            pl.when(end[0] > 0)(lambda: put(ins[0][...]))
            pl.when(end[0] == 0)(total)
        else:
            total()


def turn(end, sent, came, job, back):
    ins = ([sent.x, came] if sent else []) + ([job.x] if job and back else []) + ([back.half, back.air] if back else [])
    outs = []
    if sent:
        outs.append(jax.ShapeDtypeStruct(sent.x.shape, BF))
    if back:
        rows = max(job.x.shape[0] if job else 0, back.half.shape[0])
        outs.append(jax.ShapeDtypeStruct((rows, back.half.shape[1]), BF))
    res = []
    if outs:
        res = list(pl.pallas_call(
            functools.partial(turn_kernel, bool(sent), bool(job), bool(back)), grid=(outs[0].shape[1] // COLS,),
            out_shape=outs, in_specs=[SM] + [column_blocks(v) for v in ins], out_specs=[column_blocks(v) for v in outs],
            compiler_params=wide_params(10), cost_estimate=FREE, name="turn")(end, *ins))
    half = res.pop(0) if sent else None
    load = res.pop(0) if back else (job.x if job else None)
    return half, load


def finish_kernel(sizes, end, *refs):
    n = len(sizes)
    airs, sents, out = refs[:n], refs[n:2 * n], refs[2 * n]
    for chosen, kind in ((airs, 1), (sents, 0)):
        @pl.when(end[0] == kind)
        def _():
            at = 0
            for v, rows in zip(chosen, sizes):
                out[at:at + rows, :] = v[:rows, :].astype(F32)
                at += rows


def finish(end, jobs):
    sizes = [job.x.shape[0] for job in jobs]
    vals = [job.landed for job in jobs] + [job.sent for job in jobs]
    out = jax.ShapeDtypeStruct((sum(sizes), vals[0].shape[1]), F32)
    return pl.pallas_call(
        functools.partial(finish_kernel, sizes), grid=(out.shape[1] // COLS,), out_shape=out,
        in_specs=[SM] + [column_blocks(v) for v in vals], out_specs=column_blocks(out),
        compiler_params=wide_params(12), cost_estimate=FREE, name="finish")(end, *vals)


def parts_kernel(n, core, *refs):
    left, right, (rows, keep, give, dot) = refs[:n], refs[n:2 * n], refs[2 * n:]
    which = pl.program_id(1)
    total = tn(left[0][...], right[0][...])
    for a, b in zip(left[1:], right[1:]):
        total = total + tn(a[...], b[...])
    low = total.astype(BF)

    @pl.when((pl.program_id(0) == 0) & (which == 0))
    def _():
        dot[...] = jnp.zeros_like(dot)

    dot[...] += jnp.sum(low.astype(F32) * rows[...].astype(F32), 0, keepdims=True)

    @pl.when(which == 0)
    def _():
        keep[0] = low

    @pl.when(which == 1)
    def _():
        give[0] = low


def parts(core, left, right, rows, own):
    tok = right[0].shape[1]
    n = len(left)
    chips = left[0].shape[1] // (2 * own)
    block = lambda c, w, core: c * 2 + (core[0] ^ w)
    S = jax.ShapeDtypeStruct
    spec = pltpu.PrefetchScalarGridSpec(
        num_scalar_prefetch=1, grid=(chips, 2),
        in_specs=[pl.BlockSpec((v.shape[0], own), lambda c, w, core: (0, block(c, w, core))) for v in left]
        + [pl.BlockSpec(v.shape, lambda c, w, core: (0, 0)) for v in right]
        + [pl.BlockSpec((own, tok), lambda c, w, core: (block(c, w, core), 0))],
        out_specs=[pl.BlockSpec((1, own, tok), lambda c, w, core: (c, 0, 0))] * 2
        + [pl.BlockSpec((1, tok), lambda c, w, core: (0, 0))])
    return pl.pallas_call(
        functools.partial(parts_kernel, n), grid_spec=spec,
        out_shape=[S((chips, own, tok), BF)] * 2 + [S((1, tok), F32)],
        compiler_params=wide_params(18), name="parts",
        cost_estimate=pl.CostEstimate(flops=10**10, bytes_accessed=10**7, transcendentals=0))(core, *left, *right, rows)


from jax.sharding import PartitionSpec as P


def col_sum(x):
    return jnp.sum(x, 0, keepdims=True)


def gelu_tanh(values):
    return jax.nn.gelu(values, approximate=True)


def layout(seq_lens, row_count):
    padded = (seq_lens + MB - 1) // MB * MB
    starts = jnp.cumsum(padded) - padded
    positions = jnp.arange(row_count, dtype=jnp.int32)
    inside = (positions[None, :] >= starts[:, None]) & (positions[None, :] < (starts + seq_lens)[:, None])
    valid_rows = jnp.any(inside, axis=0).astype(F32)
    block_first = jnp.arange(row_count // MB, dtype=jnp.int32) * MB
    begins = jnp.any((starts[:, None] == block_first[None, :]) & (seq_lens[:, None] > 0), axis=0)
    return valid_rows, (begins | (block_first == 0)).astype(jnp.int32)


def tie(*values):
    return lax.optimization_barrier(values)


class Sum:
    def __init__(self, x):
        self.x = x
        self.half = self.air = self.sent = self.landed = None


class Belt:
    def __init__(self):
        self.line = lax.axis_size("dp") == 4
        at = lax.axis_index("dp")
        self.end = ((at == 0) | (at == 3)).astype(jnp.int32).reshape(1)
        self.outer = self.inner = None
        self.groups = []
        self.idle = False

    def tick(self, x, *values):
        job = Sum(x) if x is not None else None
        if not self.line:
            return (job,) + tuple(tie(*values)) if values else (job,)
        airs = ([self.outer[2]] if self.outer else []) + ([self.inner.air] if self.inner else [])
        done = []
        if self.idle:
            done = [g for g in self.groups if g.out is None and all(s.landed is not None for s in g.jobs)]
            for g in done:
                g.out = finish(self.end, g.jobs)
        held = tie(*airs, *([x] if job else []), *values, *[g.out for g in done])
        for g, out in zip(reversed(done), reversed(held)):
            g.out = out
        if job:
            job.x = held[len(airs)]
        values = held[len(airs) + (1 if job else 0):len(held) - len(done)]
        back, self.inner = self.inner, None
        if back:
            back.air = held[len(airs) - 1]
        sent, gone = self.outer[:2] if self.outer else (None, None)
        if gone:
            gone.landed = held[0]
        half, load = turn(self.end, sent, held[0], job, back)
        if sent:
            sent.half = half
            sent.air = lax.ppermute(half, "dp", [(1, 2), (2, 1)])
            self.inner = sent
        self.outer = None
        if load is not None:
            self.outer = (job, back, lax.ppermute(load, "dp", [(0, 1), (1, 0), (2, 3), (3, 2)]))
            if back:
                back.sent = load
        loads = [v for v in (half, load) if v is not None]
        if values and loads:
            values = tie(*values, *loads)[:len(values)]
        return (job,) + tuple(values)

    def drain(self):
        self.idle = True
        while self.outer or self.inner:
            self.tick(None)

    def group(self, *jobs):
        self.groups.append(Group(jobs))
        return self.groups[-1]

    def result(self, group):
        if not self.line:
            return lax.psum(jnp.concatenate([s.x for s in group.jobs], 0), "dp").astype(F32)
        return finish(self.end, group.jobs) if group.out is None else group.out


class Group:
    def __init__(self, jobs):
        self.jobs = jobs
        self.out = None


def on_device(
    tokens, lengths, attn_gain, w_query, w_key, w_value, w_gate, w_rate, rate_bias,
    inner_weight, inner_bias, inner_gain, inner_shift, post_gain, post_shift, w_out,
    ffn_gain, w_hidden_gate, w_hidden_up, w_down, out_grad,
):
    tok = tokens.shape[1]
    own = tokens.shape[0]
    heads = inner_weight.shape[0]
    devs = lax.axis_size("head")
    width = own * devs
    belt = Belt()

    def gather(x):
        return lax.all_gather(x, "head", axis=0, tiled=True)

    def head_sum(v):
        if devs != 8:
            return lax.psum(v, "head")
        for bit in (1, 2, 4):
            v = v + lax.ppermute(v, "head", [(i, i ^ bit) for i in range(8)])
        return v

    valid, reset = layout(lengths, tok)
    vrow = valid[None, :]
    spots = piece_spots(own, devs)
    stacked = jnp.concatenate([w_query, w_key, w_value, w_gate, jnp.pad(w_rate.T, ((0, 16 - heads), (0, 0)))], 0)
    tok_pieces = Pieces(tokens, devs)
    gain_blocks = spread_gains(jnp.stack([attn_gain, post_gain, post_shift, ffn_gain], 1), devs)
    consts = [hold(v, *tok_pieces.direct).astype(F32) for v in (inner_weight, inner_bias, inner_gain, inner_shift)]
    consts = pack_consts(*consts)
    g_full = gather(hold(out_grad, gain_blocks, *tok_pieces.diag))
    nin, q1, gains = rms_rows(tok_pieces.all, spots, gain_blocks, 0, tok, width)
    gate = nn(w_gate, nin).astype(BF)
    gelu_own = gelu_tanh(gate.astype(F32))
    nin_q = hold(nin, gate)
    q_t = nn(w_query, nin_q)
    k_t = nn(w_key, nin_q)
    v_t = nn(w_value, nin_q)
    logits = tn(w_rate, nin) + rate_bias.astype(F32)[:, None]
    sig = jax.nn.sigmoid(logits)
    masked = sig * vrow
    mixer_own, zt, zb, td, qa, ka, wt, rows = ttt_fwd(
        reset, q_t, k_t, v_t, masked * (1.0 / HD), vrow, consts)

    mixer_own, g_full, gelu_own = tie(mixer_own, g_full, gelu_own)
    mixer_rows = mixer_own.astype(F32)
    mean3 = col_sum(mixer_rows) / own
    spread3 = col_sum((mixer_rows - mean3) * (mixer_rows - mean3))
    if devs == 8:
        count = own
        for bit in (1, 2, 4):
            both = jnp.concatenate([mean3, spread3], 0)
            other = lax.ppermute(both, "head", [(i, i ^ bit) for i in range(8)])
            gap = other[:1] - mean3
            mean3 = (mean3 + other[:1]) * 0.5
            spread3 = spread3 + other[1:] + gap * gap * (count * 0.5)
            count *= 2
    else:
        mean3 = lax.psum(mean3, "head") / devs
        spread3 = lax.psum(col_sum((mixer_rows - mean3) * (mixer_rows - mean3)), "head")
    r3 = lax.rsqrt(spread3 / width + EPS)
    n3 = (mixer_rows - mean3) * r3
    pg_own = post_gain.astype(F32)[:, None]
    ps_own = post_shift.astype(F32)[:, None]
    mixed_own = ((n3 * pg_own + ps_own) * gelu_own).astype(BF)
    mixed = collect(Pieces(mixed_own, devs).all, spots, tok, width)
    hidden = tokens.astype(F32) + nn(w_out, mixed)
    hidden_low = hidden.astype(BF)
    nmid, q2, _ = rms_rows(Pieces(hidden_low, devs).all, spots, gains, 3, tok, width)
    gate_val = nn(w_hidden_gate, nmid)
    up_val = nn(w_hidden_up, nmid)
    sg = jax.nn.sigmoid(gate_val)
    act = (gate_val * sg * up_val).astype(BF)

    def halves(x, other):
        cut = (x.shape[0] // 2 + 7) // 8 * 8
        return wgrad(x[:cut], other), wgrad(x[cut:], other)

    down = halves(act, g_full)
    here = lax.axis_index("head") + 1
    marks = lax.broadcasted_iota(jnp.int32, (1, tok), 1)
    rates = jnp.where(marks == 0, jnp.sum(masked), jnp.where(marks == here, jnp.max(masked), 0.0))
    d0, g_full, rates = belt.tick(down[0], g_full, rates)
    g_act = nn(w_down, g_full)
    g_up = (g_act * gate_val * sg).astype(BF)
    g_gate = (g_act * up_val * sg * (1.0 + gate_val * (1.0 - sg))).astype(BF)
    gn = Scatter([w_hidden_gate, w_hidden_up], [g_gate, g_up], nmid, own, devs)
    d1, *gn.pair, gn.dot, rates, g_up, g_gate = belt.tick(down[1], *gn.pair, gn.dot, rates, g_up, g_gate)
    gn.spread()
    hgate = halves(g_gate, nmid)
    sums = head_sum(jnp.concatenate([gn.dot, rates], 0))
    mid_dot, rates = sums[:1], sums[1:]
    gn = gn.result()
    h0, gn, mid_dot, rates, g_up, h1_x = belt.tick(hgate[0], gn, mid_dot, rates, g_up, hgate[1])
    hid_own = hidden_low.astype(F32)
    fg_own = ffn_gain.astype(F32)[:, None]
    g_ffn_gain = jnp.sum(gn * hid_own * q2, 1)
    g_hidden = out_grad.astype(F32) + q2 * fg_own * gn - hid_own * q2**2 * mid_dot / width
    g_branch = g_hidden.astype(BF)
    gm = Scatter([w_out], [g_branch], mixed, own, devs)
    hup = halves(g_up, nmid)
    h1, *gm.pair, g_branch, u0_x = belt.tick(h1_x, *gm.pair, g_branch, hup[0])
    gm.spread()
    out_w = wgrad(g_branch, mixed)
    gm = gm.result()
    u0, gm, out_w, u1_x, act = belt.tick(u0_x, gm, out_w, hup[1], act)
    ffn_part = tn(w_down, act).astype(BF)
    a_own, gelu_pull = jax.vjp(gelu_tanh, gate.astype(F32))
    g_post_gain = jnp.sum(gm * a_own * n3, 1)
    g_post_shift = jnp.sum(gm * a_own, 1)
    g_gate_pre = gelu_pull(gm * (n3 * pg_own + ps_own))[0].astype(BF)
    m = gm * a_own * pg_own
    sums = head_sum(jnp.concatenate([col_sum(m), col_sum(m * n3)], 0))
    s_plain, s_norm = sums[:1], sums[1:]
    g_mixer = r3 * (m - s_plain / width - n3 * s_norm / width)
    u1, g_mixer, g_gate_pre, out_w, ffn_part = belt.tick(u1_x, g_mixer, g_gate_pre, out_w, ffn_part)
    ffn = lax.psum_scatter(ffn_part, "head", scatter_dimension=0, tiled=True)
    gate_w = wgrad(g_gate_pre, nin)
    saved = (zt, zb, td, qa, ka, wt, rows, consts)
    b1 = ttt_bwd(1, 2, reset, g_mixer, *saved)
    so, lam, lam_c, gate_w = belt.tick(out_w, b1[8], b1[9], gate_w)
    b0 = ttt_bwd(0, 2, reset, g_mixer, *saved, carry=(lam, lam_c) + tuple(b1[:3]))
    dq, dk, dv = b0[:3]
    de_rows = jnp.concatenate([b0[3], b1[3]], 1)
    dgl, dsl, dw0, dc0 = [b0[i] + b1[i] for i in range(4, 8)]
    g_logits = de_rows * vrow * (1.0 / HD) * sig * (1.0 - sig)
    gl = g_logits.astype(BF)
    g_inner_w = dw0.reshape(HD, heads, HD).transpose(1, 2, 0)
    g_inner_b = dc0.reshape(HD, heads, MB)[:, :, 0].T
    g_inner_g = dgl.reshape(HD, heads, MB).sum(-1).T
    g_inner_s = dsl.reshape(HD, heads, MB).sum(-1).T
    wide_q, wide_k, wide_v = [wgrad(v, nin) for v in (dq, dk, dv)]
    wg, dq, dk, dv, gl, wide_q, wide_k, wide_v, ffn = belt.tick(
        gate_w, dq, dk, dv, gl, wide_q, wide_k, wide_v, ffn)
    result = (hidden + ffn.astype(F32)).astype(BF)
    tall = jnp.concatenate([dq, dk, dv, g_gate_pre, jnp.pad(gl, ((0, 16 - heads), (0, 0)))], 0)
    gi = Scatter([stacked], [tall], nin, own, devs)
    q, *gi.pair, gi.dot, wide_k = belt.tick(wide_q, *gi.pair, gi.dot, wide_k)
    gi.spread()
    in_dot = head_sum(gi.dot)
    gi = gi.result()
    g_wr = nt(gl, nin)
    k, gi, in_dot, g_wr = belt.tick(wide_k, gi, in_dot, g_wr)
    x_own = tokens.astype(F32)
    ag_own = attn_gain.astype(F32)[:, None]
    g_attn_gain = jnp.sum(gi * x_own * q1, 1)
    g_tokens = g_hidden + q1 * ag_own * gi - x_own * q1**2 * in_dot / width
    top = jnp.max(jnp.where(marks > 0, rates, 0.0))
    both = jnp.stack([rates[0, 0], top])
    cut = []
    for _ in range(3):
        cut.append(lax.reduce_precision(both, 8, 7))
        both = both - cut[-1]
    dps = lax.axis_size("dp")
    slot = (jnp.arange(dps) == lax.axis_index("dp")).astype(F32)
    slots = (slot[:, None, None] * jnp.stack(cut)[None]).reshape(-1)
    vectors = [g_attn_gain, g_post_gain, g_post_shift, g_ffn_gain, g_inner_b, g_inner_g, g_inner_s,
               jnp.sum(g_logits, 1), slots]
    vectors = [jnp.pad(u.reshape(-1), (0, own - u.size)) for u in vectors]
    small = jnp.concatenate([u.astype(BF).reshape(-1) for u in vectors + [g_inner_w, g_wr]])
    count = small.shape[0]
    small = jnp.pad(small, (0, -count % (16 * width))).reshape(-1, width)
    v, = belt.tick(jnp.concatenate([wide_v, small], 0))
    sums = [belt.group(*jobs) for jobs in ((d0, d1), (h0, h1), (u0, u1), (so,), (wg,), (q,), (k,), (v,))]
    belt.drain()
    s_down, s_hgate, s_hup, s_out, s_wg, s_wq, s_wk, s_wv = [belt.result(g) for g in sums]
    s_wv, small = s_wv[:own], s_wv[own:].reshape(-1)
    s_attn, s_pg, s_ps, s_fg, s_ib, s_ig, s_is, s_rb, slots = [small[i * own:(i + 1) * own] for i in range(9)]
    s_ib, s_ig, s_is = [v.reshape(heads, HD) for v in (s_ib, s_ig, s_is)]
    s_rb = s_rb[:heads]
    wide = 9 * own + heads * HD * HD
    s_iw = small[9 * own:wide].reshape(heads, HD, HD)
    s_wr = small[wide:count].reshape(heads, width)
    slots = jnp.sum(slots[:dps * 6].reshape(dps, 3, 2), 1)
    mean_rate = jnp.sum(slots[:, 0]) / (tok * dps * heads * devs)
    max_rate = jnp.max(slots[:, 1])

    return (
        result, g_tokens, s_attn, s_wq, s_wk, s_wv, s_wg,
        s_wr.T, s_rb, s_iw, s_ib, s_ig, s_is, s_pg, s_ps, s_out,
        s_fg, s_hgate, s_hup, s_down, mean_rate, max_rate,
    )


def solution(mesh):
    h = P("head")
    m = P("head", None)
    c = P("head", None, None)
    t = P("head", "dp")
    r = P(None, "head")
    ins = (t, P("dp"), h, m, m, m, m, r, h, c, m, m, m, h, h, m, h, m, m, m, t)
    outs = (t, t, h, m, m, m, m, r, h, c, m, m, m, h, h, m, h, m, m, m, P(), P())
    return jax.shard_map(on_device, mesh=mesh, in_specs=ins, out_specs=outs, check_vma=False)
```
